32 devices in a mesh: section: 2 (over x), dp: 8 (over z, y), rep: 2 (over core).
Axes of the slice: x: 2, y: 2, z: 4, core: 2. Of those that a mesh axis runs over, the one named last changes fastest.
Arguments:
- boundary: bfloat16 [2, 48, 196, 768], P('section', ('dp', 'rep')), may hold values from -6 to 6
- keep_index: int32 [48, 196], P(('dp', 'rep')), may hold values from 0 to 195, each once within a row
- keep_count: int32 [48], P(('dp', 'rep')), may hold values from 49 to 196, as said below
- gain_one: bfloat16 [2, 768], P('section'), may hold values from 0.099609375 to 1.8984375
- shift_one: bfloat16 [2, 768], P('section'), may hold values from -1.5 to 1.5
- w_qkv: bfloat16 [2, 768, 2304], P('section'), may hold values from -0.3125 to 0.3125
- bias_query: bfloat16 [2, 768], P('section'), may hold values from -2.5 to 2.5
- bias_value: bfloat16 [2, 768], P('section'), may hold values from -2.5 to 2.5
- w_out: bfloat16 [2, 768, 768], P('section'), may hold values from -0.625 to 0.625
- bias_out: bfloat16 [2, 768], P('section'), may hold values from -1.5 to 1.5
- gain_two: bfloat16 [2, 768], P('section'), may hold values from 0.099609375 to 1.8984375
- shift_two: bfloat16 [2, 768], P('section'), may hold values from -1.5 to 1.5
- w_up: bfloat16 [2, 768, 3072], P('section'), may hold values from -0.21875 to 0.21875
- bias_up: bfloat16 [2, 3072], P('section'), may hold values from -2.5 to 2.5
- w_down: bfloat16 [2, 3072, 768], P('section'), may hold values from -0.109375 to 0.109375
- bias_down: bfloat16 [2, 768], P('section'), may hold values from -1.5 to 1.5
Outputs:
- section_outputs: bfloat16 [2, 48, 196, 768], P('section', ('dp', 'rep'))
- input_grads: bfloat16 [2, 48, 196, 768], P('section', ('dp', 'rep'))
- grad_gain_one: float32 [2, 768], P('section')
- grad_shift_one: float32 [2, 768], P('section')
- grad_w_qkv: float32 [2, 768, 2304], P('section')
- grad_bias_query: float32 [2, 768], P('section')
- grad_bias_value: float32 [2, 768], P('section')
- grad_w_out: float32 [2, 768, 768], P('section')
- grad_bias_out: float32 [2, 768], P('section')
- grad_gain_two: float32 [2, 768], P('section')
- grad_shift_two: float32 [2, 768], P('section')
- grad_w_up: float32 [2, 768, 3072], P('section')
- grad_bias_up: float32 [2, 3072], P('section')
- grad_w_down: float32 [2, 3072, 768], P('section')
- grad_bias_down: float32 [2, 768], P('section')
The draws below stay inside these ranges and needn't reach their ends.
Inputs may be any that keep to these rules, and one draw needn't show every extreme that they name: `keep_count`: among the images of each index of dp and rep one keeps all 196 patches. `keep_index`: each row is a permutation of the patches.
All inputs are finite; a program needn't handle non-finite values.
Results may differ from the reference program's by a relative error of at most 0.025.
The reference program's roundings to bfloat16 on the way count: a program that leaves them out, or rounds other values in their place, can miss the bound.
Values may be sent and summed in bfloat16 or wider, within the bound.
No kernel may reach another device: no remote copies, remote signals or barrier semaphores. Data moves between devices by JAX's collectives and lax.ppermute only.
A program may use at most 256 MiB of HBM per device.

```python
import math
import jax
import jax.numpy as jnp
from jax import lax

HEAD_DIM = 64
D = 768
FF = 3072
PATCHES = 196
IMG_DEV = 3
IMAGES = 48
N_SECTION = 2


def draw_keep_count(key, part):
    blocks = IMAGES // IMG_DEV
    key_floor, key_spread, key_full, key_block = jax.random.split(key, 4)
    floor_level = jax.random.randint(key_floor, (blocks, 1), 0, 3 * PATCHES // 4 + 1)
    floor_count = PATCHES // 4 + floor_level
    spread = jax.random.randint(key_spread, (blocks, IMG_DEV), 0, 1 << 20)
    counts = floor_count + spread % (PATCHES + 1 - floor_count)
    slot_index = lax.broadcasted_iota(jnp.int32, (blocks, IMG_DEV), 1)
    block_index = lax.broadcasted_iota(jnp.int32, (blocks, IMG_DEV), 0)
    full_slot = jax.random.randint(key_full, (blocks, 1), 0, IMG_DEV)
    counts = jnp.where(slot_index == full_slot, PATCHES, counts)
    short_block = jax.random.randint(key_block, (), 0, blocks)
    short_slot = (full_slot + 1) % IMG_DEV
    counts = jnp.where((block_index == short_block) & (slot_index == short_slot), PATCHES // 4, counts)
    return counts.reshape(IMAGES).astype(jnp.int32)


def block_scale(stream_key, extent, pieces, low, largest):
    level, own = 1.0, jax.random.fold_in(stream_key, 6)
    for axis_at, blocks in pieces:
        heights = jnp.exp(jax.random.uniform(jax.random.fold_in(own, axis_at), (blocks,), jnp.float32, low / len(pieces), largest / len(pieces)))
        level = level * jnp.repeat(heights, extent[axis_at] // blocks).reshape([-1 if axis == axis_at else 1 for axis in range(len(extent))])
    return level


def gaussian(stream_key, extent, width, limit, cuts=(), dtype=jnp.bfloat16):
    values = width * jax.random.normal(stream_key, extent, jnp.float32)
    if cuts:
        values = values * block_scale(stream_key, extent, cuts, -0.22, 0.18)
    return jnp.clip(values, -limit, limit).astype(dtype)


def setup_inputs(seed: int = 0) -> dict:
    key_of = jax.random.split(jax.random.key(seed), 17)
    boundary = gaussian(key_of[0], (N_SECTION, IMAGES, PATCHES, D), 1.0, 6.0, ((0, 2), (1, 16)))
    keep_index = jax.vmap(lambda own: jax.random.permutation(own, PATCHES))(jax.random.split(key_of[1], IMAGES)).reshape((IMAGES, PATCHES)).astype(jnp.int32)
    keep_count = draw_keep_count(jax.random.fold_in(key_of[16], 71), 0)
    gain_one = jnp.clip(1.0 + 0.18 * jax.random.normal(key_of[3], (N_SECTION, D), jnp.float32), 0.099609375, 1.8984375).astype(jnp.bfloat16)
    shift_one = gaussian(key_of[4], (N_SECTION, D), 0.3, 1.5, ((0, 2),))
    w_qkv = gaussian(key_of[5], (N_SECTION, D, 3 * D), (D // 2) ** -0.5, 0.3125, ((0, 2),))
    bias_query = gaussian(key_of[6], (N_SECTION, D), 0.5, 2.5, ((0, 2),))
    bias_value = gaussian(key_of[7], (N_SECTION, D), 0.5, 2.5, ((0, 2),))
    w_out = gaussian(key_of[8], (N_SECTION, D, D), (D // 8) ** -0.5, 0.625, ((0, 2),))
    bias_out = gaussian(key_of[9], (N_SECTION, D), 0.3, 1.5, ((0, 2),))
    gain_two = jnp.clip(1.0 + 0.18 * jax.random.normal(key_of[10], (N_SECTION, D), jnp.float32), 0.099609375, 1.8984375).astype(jnp.bfloat16)
    shift_two = gaussian(key_of[11], (N_SECTION, D), 0.3, 1.5, ((0, 2),))
    w_up = gaussian(key_of[12], (N_SECTION, D, FF), D ** -0.5, 0.21875, ((0, 2),))
    bias_up = gaussian(key_of[13], (N_SECTION, FF), 0.5, 2.5, ((0, 2),))
    w_down = gaussian(key_of[14], (N_SECTION, FF, D), FF ** -0.5, 0.109375, ((0, 2),))
    bias_down = gaussian(key_of[15], (N_SECTION, D), 0.3, 1.5, ((0, 2),))
    return {"boundary": boundary, "keep_index": keep_index, "keep_count": keep_count, "gain_one": gain_one, "shift_one": shift_one, "w_qkv": w_qkv, "bias_query": bias_query, "bias_value": bias_value, "w_out": w_out, "bias_out": bias_out, "gain_two": gain_two, "shift_two": shift_two, "w_up": w_up, "bias_up": bias_up, "w_down": w_down, "bias_down": bias_down}


@jax.custom_vjp
def low(v):
    return lax.optimization_barrier(v.astype(jnp.bfloat16)).astype(jnp.float32)

@jax.custom_vjp
def low_back(v):
    return v

def low_keep(v):
    return (low(v), None)

def low_pass(kept, grad):
    return (grad,)

def back_keep(v):
    return (v, None)

def back_low(kept, grad):
    return (low(grad),)
low.defvjp(low_keep, low_pass)
low_back.defvjp(back_keep, back_low)
norm_eps = 1e-06
masked_score = -1e+30

def product(left, right):
    return jnp.matmul(left, right, precision=lax.Precision.HIGHEST)

def layer_norm(values, gain, shift):
    row_mean = lax.optimization_barrier(jnp.mean(values, axis=-1, keepdims=True))
    centred = values - row_mean
    variance = lax.optimization_barrier(jnp.mean(centred * centred, axis=-1, keepdims=True))
    return centred * lax.rsqrt(variance + norm_eps) * gain + shift

def encoder(inputs, valid_rows, params):
    gain_one, shift_one, w_qkv, bias_query, bias_value, w_out, bias_out, gain_two, shift_two, w_up, bias_up, w_down, bias_down = params
    batch_size, row_count, model_width = inputs.shape
    head_count = model_width // HEAD_DIM
    heads_shape = (batch_size, row_count, head_count, HEAD_DIM)
    normed = low(layer_norm(inputs, gain_one, shift_one))
    packed = product(normed, w_qkv)
    queries = low_back(low(packed[..., :model_width] + bias_query)).reshape(heads_shape)
    key_rows = low_back(low(packed[..., model_width:2 * model_width])).reshape(heads_shape)
    values = low_back(low(packed[..., 2 * model_width:] + bias_value)).reshape(heads_shape)
    score_scale = 1.0 / math.sqrt(HEAD_DIM)
    scores = low_back(jnp.einsum('bqhd,bkhd->bhqk', queries, key_rows, precision=lax.Precision.HIGHEST) * score_scale)
    scores = jnp.where(valid_rows[:, None, None, :] > 0, scores, masked_score)
    attention = low(jax.nn.softmax(scores, axis=-1))
    attended = jnp.einsum('bhqk,bkhd->bqhd', attention, values, precision=lax.Precision.HIGHEST)
    attended = low_back(low(attended.reshape(batch_size, row_count, model_width)))
    residual = inputs + low_back(product(attended, w_out) + bias_out)
    normed_two = low(layer_norm(residual, gain_two, shift_two))
    pre_gelu = low_back(product(normed_two, w_up) + bias_up)
    hidden = low(jax.nn.gelu(pre_gelu, approximate=False))
    return (residual + low_back(product(hidden, w_down) + bias_down)) * valid_rows[..., None]

def reference(boundary, keep_index, keep_count, gain_one, shift_one, w_qkv, bias_query, bias_value, w_out, bias_out, gain_two, shift_two, w_up, bias_up, w_down, bias_down):
    weights = tuple((weight.astype(jnp.float32) for weight in (gain_one, shift_one, w_qkv, bias_query, bias_value, w_out, bias_out, gain_two, shift_two, w_up, bias_up, w_down, bias_down)))
    group_count = IMAGES // IMG_DEV

    def grouped(array):
        return array.reshape((group_count, IMG_DEV) + array.shape[1:])
    first_params = tuple((weight[0] for weight in weights))
    second_params = tuple((weight[1] for weight in weights))

    def step(carry, items):
        patch_rows, cotangent, keep_rows, count_rows = items
        slot_iota = lax.broadcasted_iota(jnp.int32, keep_rows.shape, 1)
        valid_rows = (slot_iota < count_rows[:, None]).astype(jnp.float32)

        def first_layer(patches, params):
            kept_rows = jnp.take_along_axis(patches, keep_rows[:, :, None], axis=1) * valid_rows[..., None]
            return low(encoder(kept_rows, valid_rows, params))

        def second_layer(inputs, params):
            return encoder(inputs, valid_rows, params)
        first, first_back = jax.vjp(first_layer, patch_rows.astype(jnp.float32), first_params)
        second, second_back = jax.vjp(second_layer, first, second_params)
        grad_first, second_grads = second_back(cotangent.astype(jnp.float32))
        grad_first = grad_first.astype(jnp.bfloat16)
        grad_patch, first_grads = first_back(grad_first.astype(jnp.float32))
        first_sums, second_sums = carry
        first_sums = tuple((total + grad for total, grad in zip(first_sums, first_grads)))
        second_sums = tuple((total + grad for total, grad in zip(second_sums, second_grads)))
        outputs = (first.astype(jnp.bfloat16), second.astype(jnp.bfloat16), grad_patch.astype(jnp.bfloat16), grad_first)
        return ((first_sums, second_sums), outputs)
    zeros_init = tuple((jnp.zeros(weight.shape[1:], jnp.float32) for weight in weights))
    (first_sums, second_sums), outputs = lax.scan(step, (zeros_init, zeros_init), (grouped(boundary[0]), grouped(boundary[1]), grouped(keep_index), grouped(keep_count)))
    whole_shape = boundary.shape[1:]
    first_rows, second_rows, patch_grads, first_grads = outputs
    section_outputs = jnp.stack([first_rows.reshape(whole_shape), second_rows.reshape(whole_shape)])
    input_grads = jnp.stack([patch_grads.reshape(whole_shape), first_grads.reshape(whole_shape)])
    grads = tuple((jnp.stack([first_sum, second_sum]) / IMAGES for first_sum, second_sum in zip(first_sums, second_sums)))
    return (section_outputs, input_grads, grads[0], grads[1], grads[2], grads[3], grads[4], grads[5], grads[6], grads[7], grads[8], grads[9], grads[10], grads[11], grads[12])
```

```python
from functools import partial
import math

import jax
import jax.numpy as jnp
from jax import lax
from jax.experimental import pallas as pl
from jax.experimental.pallas import tpu as pltpu
from jax.sharding import PartitionSpec as P

HEAD_DIM = 64
PAIR = 2 * HEAD_DIM
ROW_TILE = 16
COLUMNS = 256

norm_eps = 1e-06
masked_score = -1e30
f32 = jnp.float32
bf16 = jnp.bfloat16

NN = (((1,), (0,)), ((), ()))
NT = (((1,), (1,)), ((), ()))
TN = (((0,), (0,)), ((), ()))

GAIN_ONE, SHIFT_ONE, BIAS_QUERY, BIAS_VALUE, BIAS_OUT, GAIN_TWO, SHIFT_TWO, BIAS_DOWN, BIAS_UP = range(9)


def product(left, right, dims):
    return lax.dot_general(left, right, dims, preferred_element_type=f32)


def spans(size, step):
    return [slice(at, min(at + step, size)) for at in range(0, size, step)]


def column_sum(values):
    return jnp.sum(values, axis=0, keepdims=True)


def centre(values):
    centred = values - jnp.mean(values, axis=-1, keepdims=True)
    scale = lax.rsqrt(jnp.mean(centred * centred, axis=-1, keepdims=True) + norm_eps)
    return centred * scale, scale


class Fetch:
    def __init__(self, first, pairs, sem):
        self.first = first
        self.copies = {
            name: pltpu.make_async_copy(source, target, sem.at[at])
            for at, (name, source, target) in enumerate(pairs)
        }

    def start(self):
        @pl.when(self.first)
        def _():
            for copy in self.copies.values():
                copy.start()

    def wait(self, name):
        copy = self.copies.pop(name, None)
        if copy is not None:

            @pl.when(self.first)
            def _():
                copy.wait()


def row_mask(shape, count):
    return lax.broadcasted_iota(jnp.int32, shape, 0) < count


def gather_matrix(index_ref, count):
    slots = index_ref.shape[-1]
    padded = -(-slots // ROW_TILE) * ROW_TILE
    shape = (padded, slots)
    patch = lax.broadcasted_iota(jnp.int32, shape, 0)
    slot = lax.broadcasted_iota(jnp.int32, shape, 1)
    chosen = jnp.broadcast_to(index_ref[...], shape) == patch
    return jnp.where(chosen & (slot < count), 1.0, 0.0).astype(bf16)


def forward_part(r, fetch, vec, weights, count):
    rows, width = r["u"].shape[-2:]
    hidden = weights["up"].shape[1]
    for span in spans(rows, ROW_TILE):
        normal, _ = centre(r["u"][span, :].astype(f32))
        r["a"][span, :] = (normal * vec(GAIN_ONE) + vec(SHIFT_ONE)).astype(bf16)
    fetch.wait("qkv")
    for span in spans(3 * width, COLUMNS):
        packed = product(r["a"][...], weights["qkv"][:, span], NN)
        if span.start < width:
            packed = packed + vec(BIAS_QUERY, span)
        elif span.start >= 2 * width:
            packed = packed + vec(BIAS_VALUE, slice(span.start - 2 * width, span.stop - 2 * width))
        r["qkv"][:, span] = packed.astype(bf16)
    low = (lax.broadcasted_iota(jnp.int32, (1, PAIR), 1) < HEAD_DIM).astype(bf16)
    lane = lax.broadcasted_iota(jnp.int32, (rows, PAIR), 1) < HEAD_DIM
    for at in range(0, width, PAIR):
        query = r["qkv"][:, at : at + PAIR]
        key = r["qkv"][:, width + at : width + at + PAIR]
        value = r["qkv"][:, 2 * width + at : 2 * width + at + PAIR]
        both = jnp.concatenate([query * low, query * (1 - low)], axis=0)
        scores = product(both, key, NT) * (1.0 / math.sqrt(HEAD_DIM))
        live = lax.broadcasted_iota(jnp.int32, scores.shape, 1) < count
        scores = jnp.where(live, scores, masked_score)
        powers = jnp.exp(scores - jnp.max(scores, axis=-1, keepdims=True))
        chance = powers * (1.0 / jnp.sum(powers, axis=-1, keepdims=True))
        mixed = product(chance.astype(bf16), value, NN)
        r["o"][:, at : at + PAIR] = jnp.where(lane, mixed[:rows], mixed[rows:]).astype(bf16)
    fetch.wait("out")
    for span in spans(width, COLUMNS):
        r["r"][:, span] = r["u"][:, span].astype(f32) + (
            product(r["o"][...], weights["out"][:, span], NN) + vec(BIAS_OUT, span)
        )
    for span in spans(rows, ROW_TILE):
        normal, _ = centre(r["r"][span, :])
        r["c"][span, :] = (normal * vec(GAIN_TWO) + vec(SHIFT_TWO)).astype(bf16)
    fetch.wait("up")
    for span in spans(hidden, COLUMNS):
        z = product(r["c"][...], weights["up"][:, span], NN) + vec(BIAS_UP, span)
        share = 0.5 * (1.0 + lax.erf(z * math.sqrt(0.5)))
        r["m"][:, span] = (z * share).astype(bf16)
        if r.get("slope") is not None:
            r["slope"][:, span] = share + z * (jnp.exp(-0.5 * z * z) * (1.0 / math.sqrt(2 * math.pi)))
    fetch.wait("down")
    outer = r["y"].shape[-2]
    for span in spans(width, COLUMNS):
        y = r["r"][:, span] + (product(r["m"][...], weights["down"][:, span], NN) + vec(BIAS_DOWN, span))
        y = jnp.where(row_mask(y.shape, count), y, 0.0)
        r["y"][:, span] = y.astype(bf16)[:outer]


def norm_back(normal, scale, gain, grad):
    x = grad * gain
    return scale * (
        x - jnp.mean(x, axis=-1, keepdims=True) - normal * jnp.mean(x * normal, axis=-1, keepdims=True)
    )


def backward_part(r, fetch, vec, weights, count, add):
    rows, width = r["u"].shape[-2:]
    hidden = weights["up"].shape[1]
    for span in spans(rows, ROW_TILE):
        live = lax.broadcasted_iota(jnp.int32, (ROW_TILE, width), 0) + span.start < count
        r["gd"][span, :] = jnp.where(live, r["e"][span, :], jnp.zeros((), bf16))
    add(BIAS_DOWN, lambda: column_sum(r["gd"][...].astype(f32)))
    fetch.wait("down")
    for span in spans(hidden, COLUMNS):
        gz = product(r["gd"][...], weights["down"][span, :], NT) * r["slope"][:, span]
        r["gz"][:, span] = gz.astype(bf16)
        add(BIAS_UP, lambda: column_sum(r["gz"][:, span].astype(f32)), span)
    fetch.wait("up")
    for span in spans(width, COLUMNS):
        r["gr"][:, span] = product(r["gz"][...], weights["up"][span, :], NT)
    gain_sum, shift_sum = 0.0, 0.0
    for span in spans(rows, ROW_TILE):
        normal, scale = centre(r["r"][span, :])
        gc = r["gr"][span, :]
        gain_sum, shift_sum = gain_sum + gc * normal, shift_sum + gc
        gr = r["gd"][span, :].astype(f32) + norm_back(normal, scale, vec(GAIN_TWO), gc)
        r["gr"][span, :] = gr
        r["gb"][span, :] = gr.astype(bf16)
    add(GAIN_TWO, lambda: column_sum(gain_sum))
    add(SHIFT_TWO, lambda: column_sum(shift_sum))
    add(BIAS_OUT, lambda: column_sum(r["gb"][...].astype(f32)))
    fetch.wait("out")
    for span in spans(width, COLUMNS):
        r["go"][:, span] = product(r["gb"][...], weights["out"][span, :], NT).astype(bf16)
    low = (lax.broadcasted_iota(jnp.int32, (1, PAIR), 1) < HEAD_DIM).astype(bf16)
    lane = lax.broadcasted_iota(jnp.int32, (rows, PAIR), 1) < HEAD_DIM
    score_scale = 1.0 / math.sqrt(HEAD_DIM)
    live = row_mask((rows, rows), count)
    for at in range(0, width, PAIR):
        query = r["qkv"][:, at : at + PAIR]
        key = r["qkv"][:, width + at : width + at + PAIR]
        value = r["qkv"][:, 2 * width + at : 2 * width + at + PAIR]
        go = r["go"][:, at : at + PAIR]
        scores = product(jnp.concatenate([key * low, key * (1 - low)], axis=0), query, NT) * score_scale
        grads = product(jnp.concatenate([value * low, value * (1 - low)], axis=0), go, NT)
        chances, inner = [], []
        for head in range(2):
            score = jnp.where(live, scores[head * rows : (head + 1) * rows], masked_score)
            powers = jnp.exp(score - jnp.max(score, axis=0, keepdims=True))
            chance = powers * (1.0 / jnp.sum(powers, axis=0, keepdims=True))
            gp = grads[head * rows : (head + 1) * rows]
            gs = chance * (gp - jnp.sum(gp * chance, axis=0, keepdims=True))
            chances.append(chance.astype(bf16))
            inner.append(jnp.where(live, gs, 0.0).astype(bf16))
        gw = product(jnp.concatenate(chances, axis=0), go, NN)
        gk = product(jnp.concatenate(inner, axis=0), query, NN) * score_scale
        gq = [product(gs, key, TN) * score_scale for gs in inner]
        r["gqkv"][:, at : at + PAIR] = jnp.where(lane, gq[0], gq[1]).astype(bf16)
        r["gqkv"][:, width + at : width + at + PAIR] = jnp.where(lane, gk[:rows], gk[rows:]).astype(bf16)
        r["gqkv"][:, 2 * width + at : 2 * width + at + PAIR] = jnp.where(lane, gw[:rows], gw[rows:]).astype(
            bf16
        )
    add(BIAS_QUERY, lambda: column_sum(r["gqkv"][:, :width].astype(f32)))
    add(BIAS_VALUE, lambda: column_sum(r["gqkv"][:, 2 * width :].astype(f32)))
    fetch.wait("qkv")
    for span in spans(width, COLUMNS):
        r["ga"][:, span] = product(r["gqkv"][...], weights["qkv"][span, :], NT)
    gain_sum, shift_sum = 0.0, 0.0
    for span in spans(rows, ROW_TILE):
        normal, scale = centre(r["u"][span, :].astype(f32))
        ga = r["ga"][span, :]
        gain_sum, shift_sum = gain_sum + ga * normal, shift_sum + ga
        gu = r["gr"][span, :] + norm_back(normal, scale, vec(GAIN_ONE), ga)
        r["gu"][span, :] = gu.astype(bf16)
    add(GAIN_ONE, lambda: column_sum(gain_sum))
    add(SHIFT_ONE, lambda: column_sum(shift_sum))


def vector_reader(ref):
    def vec(row, span=None):
        width = ref.shape[1]
        if span is None:
            return ref[row : row + 1, :]
        at = row + span.start // width
        start = span.start % width
        return ref[at : at + 1, start : start + span.stop - span.start]

    return vec


def vector_adder(ref):
    def add(row, values, span=None):
        width = ref.shape[1]
        values = values()
        at, start = row, 0
        if span is not None:
            at, start = row + span.start // width, span.start % width
        ref[at : at + 1, start : start + values.shape[1]] += values

    return add


def pad_rows(target, source):
    inner, rows = source.shape[0], target.shape[0]
    target[:inner, :] = source[...]
    if rows > inner:
        target[inner:, :] = jnp.zeros((rows - inner, target.shape[1]), target.dtype)


WEIGHTS = ("qkv", "out", "up", "down")
ANY = pl.BlockSpec(memory_space=pl.ANY)


def image_block(shape):
    return pl.BlockSpec((pl.Squeezed(),) + tuple(shape), lambda i, *_: (i, 0, 0))


def fixed_block(shape):
    return pl.BlockSpec(tuple(shape), lambda i, *_: (0,) * len(shape))


def weight_scratch(weights):
    return [pltpu.VMEM(weight.shape, weight.dtype) for weight in weights] + [
        pltpu.SemaphoreType.DMA((len(weights),))
    ]


def call(kernel, images, scalars, ins, in_specs, outs, out_specs, scratch, flops, name):
    return pl.pallas_call(
        kernel,
        out_shape=outs,
        grid_spec=pltpu.PrefetchScalarGridSpec(
            num_scalar_prefetch=1,
            grid=(images,),
            in_specs=in_specs,
            out_specs=out_specs,
            scratch_shapes=scratch,
        ),
        compiler_params=pltpu.CompilerParams(
            dimension_semantics=("arbitrary",), vmem_limit_bytes=60 << 20
        ),
        cost_estimate=pl.CostEstimate(flops=flops, bytes_accessed=flops // 300, transcendentals=0),
        name=name,
    )(scalars, *ins)


def first_forward(scalars, index, source, vectors, weights):
    images, slots, width = source.shape
    rows = -(-slots // ROW_TILE) * ROW_TILE
    hidden = weights[2].shape[1]

    def kernel(scalar_ref, index_ref, source_ref, vec_ref, *rest):
        hbm, (u_ref, y_ref), rest = rest[:4], rest[4:6], rest[6:]
        local, sem, rest = rest[:4], rest[4], rest[5:]
        padded, a_ref, qkv_ref, o_ref, r_ref, c_ref, m_ref = rest
        image = pl.program_id(0)
        fetch = Fetch(image == 0, list(zip(WEIGHTS, hbm, local)), sem)
        fetch.start()
        count = scalar_ref[1 + image]
        pad_rows(padded, source_ref)
        chosen = gather_matrix(index_ref, count)
        gathered = product(chosen, padded[...], TN)
        u_ref[:slots, :] = gathered.astype(bf16)
        u_ref[slots:, :] = jnp.zeros((rows - slots, width), bf16)
        refs = dict(u=u_ref, a=a_ref, qkv=qkv_ref, o=o_ref, r=r_ref, c=c_ref, m=m_ref, y=y_ref)
        forward_part(refs, fetch, vector_reader(vec_ref), dict(zip(WEIGHTS, local)), count)

    return call(
        kernel,
        images,
        scalars,
        (index, source, vectors) + weights,
        [image_block((1, slots)), image_block((slots, width)), fixed_block(vectors.shape)] + [ANY] * 4,
        [
            jax.ShapeDtypeStruct((images, rows, width), bf16),
            jax.ShapeDtypeStruct((images, slots, width), bf16),
        ],
        [image_block((rows, width)), image_block((slots, width))],
        weight_scratch(weights)
        + [
            pltpu.VMEM((rows, width), bf16),
            pltpu.VMEM((rows, width), bf16),
            pltpu.VMEM((rows, 3 * width), bf16),
            pltpu.VMEM((rows, width), bf16),
            pltpu.VMEM((rows, width), f32),
            pltpu.VMEM((rows, width), bf16),
            pltpu.VMEM((rows, hidden), bf16),
        ],
        images * 2 * rows * 12 * width * width,
        "first_forward",
    )


def whole_layer(scalars, kept, received, cotangent, vectors, weights):
    images, rows, width = kept.shape
    slots = cotangent.shape[1]
    hidden = weights[2].shape[1]
    saved = [
        ((rows, width), bf16),
        ((rows, width), bf16),
        ((rows, 3 * width), bf16),
        ((rows, width), bf16),
        ((rows, width), f32),
        ((rows, width), bf16),
        ((rows, hidden), bf16),
        ((rows, hidden), f32),
        ((slots, width), bf16),
        ((slots, width), bf16),
    ]

    def kernel(scalar_ref, kept_ref, received_ref, e_ref, vec_ref, *rest):
        hbm, outs, rest = rest[:4], rest[4:14], rest[14:]
        local, sem, rest = rest[:4], rest[4], rest[5:]
        e_pad, gd_ref, gz_ref, gb_ref, gr_ref, go_ref, gqkv_ref, ga_ref, gu_pad = rest
        u_ref, a_ref, qkv_ref, o_ref, r_ref, c_ref, m_ref, slope_ref, y_ref, gu_ref = outs
        image = pl.program_id(0)
        fetch = Fetch(image == 0, list(zip(WEIGHTS, hbm, local)), sem)
        fetch.start()
        count = scalar_ref[1 + image]

        @pl.when(scalar_ref[0] == 0)
        def _():
            u_ref[...] = kept_ref[...]

        @pl.when(scalar_ref[0] != 0)
        def _():
            pad_rows(u_ref, received_ref)

        pad_rows(e_pad, e_ref)
        refs = dict(
            u=u_ref, a=a_ref, qkv=qkv_ref, o=o_ref, r=r_ref, c=c_ref, m=m_ref, slope=slope_ref, y=y_ref,
            e=e_pad, gd=gd_ref, gz=gz_ref, gb=gb_ref, gr=gr_ref, go=go_ref, gqkv=gqkv_ref, ga=ga_ref,
            gu=gu_pad,
        )
        vec = vector_reader(vec_ref)
        near = dict(zip(WEIGHTS, local))
        forward_part(refs, fetch, vec, near, count)
        backward_part(refs, fetch, vec, near, count, lambda row, values, span=None: None)
        gu_ref[...] = gu_pad[:slots, :]

    return call(
        kernel,
        images,
        scalars,
        (kept, received, cotangent, vectors) + weights,
        [
            image_block((rows, width)),
            image_block((slots, width)),
            image_block((slots, width)),
            fixed_block(vectors.shape),
        ]
        + [ANY] * 4,
        [jax.ShapeDtypeStruct((images,) + shape, dtype) for shape, dtype in saved],
        [image_block(shape) for shape, _ in saved],
        weight_scratch(weights)
        + [
            pltpu.VMEM((rows, width), bf16),
            pltpu.VMEM((rows, width), bf16),
            pltpu.VMEM((rows, hidden), bf16),
            pltpu.VMEM((rows, width), bf16),
            pltpu.VMEM((rows, width), f32),
            pltpu.VMEM((rows, width), bf16),
            pltpu.VMEM((rows, 3 * width), bf16),
            pltpu.VMEM((rows, width), f32),
            pltpu.VMEM((rows, width), bf16),
        ],
        images * 4 * rows * 12 * width * width,
        "whole_layer",
    )


def layer_backward(scalars, index, u, qkv, r, slope, cotangent, received, vectors, weights):
    images, rows, width = u.shape
    slots = cotangent.shape[1]
    hidden = weights[2].shape[1]
    made = [
        ((rows, width), bf16),
        ((rows, hidden), bf16),
        ((rows, width), bf16),
        ((rows, 3 * width), bf16),
        ((slots, width), bf16),
    ]
    lines = vectors.shape[0]

    def kernel(scalar_ref, index_ref, u_ref, qkv_ref, r_ref, slope_ref, e_ref, received_ref, vec_ref, *rest):
        hbm, outs, rest = rest[:4], rest[4:10], rest[10:]
        local, sem, rest = rest[:4], rest[4], rest[5:]
        gd_ref, gz_ref, gb_ref, gqkv_ref, grad_ref, sums_ref = outs
        e_pad, gr_ref, go_ref, ga_ref, gu_ref = rest
        image = pl.program_id(0)
        order = ("down", "up", "out", "qkv")
        found = dict(zip(WEIGHTS, zip(hbm, local)))
        fetch = Fetch(image == 0, [(name,) + found[name] for name in order], sem)
        fetch.start()
        count = scalar_ref[1 + image]
        early = scalar_ref[0] == 0

        @pl.when(image == 0)
        def _():
            sums_ref[...] = jnp.zeros(sums_ref.shape, f32)

        @pl.when(early)
        def _():
            pad_rows(e_pad, received_ref)

        @pl.when(jnp.logical_not(early))
        def _():
            pad_rows(e_pad, e_ref)

        refs = dict(
            u=u_ref, qkv=qkv_ref, r=r_ref, slope=slope_ref, e=e_pad, gd=gd_ref, gz=gz_ref, gb=gb_ref,
            gr=gr_ref, go=go_ref, gqkv=gqkv_ref, ga=ga_ref, gu=gu_ref,
        )
        near = dict(zip(WEIGHTS, local))
        backward_part(refs, fetch, vector_reader(vec_ref), near, count, vector_adder(sums_ref))

        @pl.when(early)
        def _():
            chosen = gather_matrix(index_ref, count)
            grad_ref[...] = product(chosen, gu_ref[:slots, :], NN)[:slots, :].astype(bf16)

        @pl.when(jnp.logical_not(early))
        def _():
            grad_ref[...] = gu_ref[:slots, :]

    return call(
        kernel,
        images,
        scalars,
        (index, u, qkv, r, slope, cotangent, received, vectors) + weights,
        [
            image_block((1, slots)),
            image_block((rows, width)),
            image_block((rows, 3 * width)),
            image_block((rows, width)),
            image_block((rows, hidden)),
            image_block((slots, width)),
            image_block((slots, width)),
            fixed_block(vectors.shape),
        ]
        + [ANY] * 4,
        [jax.ShapeDtypeStruct((images,) + shape, dtype) for shape, dtype in made]
        + [jax.ShapeDtypeStruct((lines, width), f32)],
        [image_block(shape) for shape, _ in made] + [fixed_block((lines, width))],
        weight_scratch(weights)
        + [
            pltpu.VMEM((rows, width), bf16),
            pltpu.VMEM((rows, width), f32),
            pltpu.VMEM((rows, width), bf16),
            pltpu.VMEM((rows, width), f32),
            pltpu.VMEM((rows, width), bf16),
        ],
        images * 2 * rows * 12 * width * width,
        "layer_backward",
    )


def weight_gradient(side, sources, name):
    depth = sources[0][0].shape[0]
    width = min(min(left.shape[1], right.shape[1]) for left, right in sources)
    starts = [0]
    for left, right in sources:
        starts.append(starts[-1] + max(left.shape[1], right.shape[1]) // width)
    blocks = starts[-1]
    half = blocks // 2

    def chosen(i, scalar_ref):
        bit = scalar_ref[0]
        return jnp.where(i < half, (1 - bit) * half + i, bit * half + i - half)

    def kernel(scalar_ref, *refs):
        send_ref, keep_ref = refs[-2:]
        step = pl.program_id(0)
        block = chosen(step, scalar_ref)
        for at in range(len(sources)):
            left_ref, right_ref = refs[2 * at : 2 * at + 2]

            @pl.when((block >= starts[at]) & (block < starts[at + 1]) & (step < half))
            def _():
                for span in spans(width, COLUMNS):
                    send_ref[:, span] = product(left_ref[...], right_ref[:, span], TN).astype(bf16)

            @pl.when((block >= starts[at]) & (block < starts[at + 1]) & (step >= half))
            def _():
                for span in spans(width, COLUMNS):
                    keep_ref[:, span] = product(left_ref[...], right_ref[:, span], TN)

    def column_block(array, first, last):
        if array.shape[1] == width:
            return pl.BlockSpec((depth, width), lambda i, s: (0, 0))
        return pl.BlockSpec(
            (depth, width), lambda i, s: (0, jnp.clip(chosen(i, s), first, last - 1) - first)
        )

    out = (half, width, width)
    square = (pl.Squeezed(), width, width)
    return call(
        kernel,
        blocks,
        side,
        [array for source in sources for array in source],
        [
            column_block(array, starts[at], starts[at + 1])
            for at, source in enumerate(sources)
            for array in source
        ],
        [jax.ShapeDtypeStruct(out, bf16), jax.ShapeDtypeStruct(out, f32)],
        [
            pl.BlockSpec(square, lambda i, s: (jnp.minimum(i, half - 1), 0, 0)),
            pl.BlockSpec(square, lambda i, s: (jnp.maximum(i - half, 0), 0, 0)),
        ],
        [],
        2 * depth * width * width * blocks,
        name,
    )


def swapped(value, axis, stride):
    length = lax.axis_size(axis)
    return lax.ppermute(value, axis, [(i, i ^ stride) for i in range(length)])


def bit_of(axis, stride):
    return (lax.axis_index(axis) // stride) % 2


def halved(pair, bit):
    height = pair.shape[0] // 2
    send = lax.dynamic_slice_in_dim(pair, (1 - bit) * height, height, axis=0).astype(bf16)
    keep = lax.dynamic_slice_in_dim(pair, bit * height, height, axis=0)
    return send, keep


def joined(mine, other, bit):
    first = bit == 0
    return jnp.concatenate([jnp.where(first, mine, other), jnp.where(first, other, mine)], axis=0)


def strides_of(size):
    return [1 << at for at in range(size.bit_length() - 1)]


def reduce_blocks(send, keep, total):
    width = send.shape[-1]
    send, keep = send.reshape(-1, width), keep.reshape(-1, width)
    value = keep + swapped(send, "rep", 1).astype(f32)
    strides = strides_of(lax.axis_size("dp"))
    for stride in strides:
        send, keep = halved(value, bit_of("dp", stride))
        value = keep + swapped(send, "dp", stride).astype(f32)
    value = (value / total).astype(bf16)
    for stride in reversed(strides):
        value = joined(value, swapped(value, "dp", stride), bit_of("dp", stride))
    return value, swapped(value, "rep", 1)


def reduce_vectors(value):
    value = value + swapped(value, "rep", 1)
    for stride in strides_of(lax.axis_size("dp")):
        value = value + swapped(value, "dp", stride)
    return value


def shards(
    boundary,
    keep_index,
    keep_count,
    gain_one,
    shift_one,
    w_qkv,
    bias_query,
    bias_value,
    w_out,
    bias_out,
    gain_two,
    shift_two,
    w_up,
    bias_up,
    w_down,
    bias_down,
):
    images, slots = keep_index.shape
    width = boundary.shape[-1]
    weights = (w_qkv[0], w_out[0], w_up[0], w_down[0])
    hidden = weights[2].shape[1]
    small = (gain_one, shift_one, bias_query, bias_value, bias_out, gain_two, shift_two, bias_down)
    used = len(small) + hidden // width
    vectors = jnp.concatenate(
        [jnp.concatenate(small, axis=0), bias_up.reshape(-1, width), jnp.zeros((-used % 8, width), bf16)], axis=0
    ).astype(f32)
    section = lax.axis_index("section").astype(jnp.int32)
    scalars = jnp.concatenate([section[None], keep_count])
    index = keep_index[:, None, :]
    rows_in = boundary[0]

    kept, output = first_forward(scalars, index, rows_in, vectors, weights)
    received = lax.ppermute(output, "section", [(0, 1)])
    u, a, qkv, o, r, c, m, slope, output, grad_first = whole_layer(
        scalars, kept, received, rows_in, vectors, weights
    )
    returned = lax.ppermute(grad_first, "section", [(1, 0)])
    gd, gz, gb, gqkv, grad_rows, sums = layer_backward(
        scalars, index, u, qkv, r, slope, rows_in, returned, vectors, weights
    )

    def flat(array):
        return array.reshape(-1, array.shape[-1])

    total = images * lax.axis_size(("dp", "rep"))
    rep = lax.axis_index("rep")
    side = rep.astype(jnp.int32)[None]
    grads = (
        weight_gradient(side, [(flat(m), flat(gd))], "grad_down"),
        weight_gradient(side, [(flat(c), flat(gz))], "grad_up"),
        weight_gradient(side, [(flat(a), flat(gqkv)), (flat(o), flat(gb))], "grad_attention"),
    )
    down, up, attention = [
        joined(mine, other, rep).astype(f32).reshape(-1, width, width)
        for mine, other in (reduce_blocks(send, keep, total) for send, keep in grads)
    ]
    sums = reduce_vectors(sums) / total

    def across(blocks):
        return jnp.transpose(blocks, (1, 0, 2)).reshape(width, -1)

    return (
        output[None],
        grad_rows[None],
        sums[GAIN_ONE][None],
        sums[SHIFT_ONE][None],
        across(attention[:3])[None],
        sums[BIAS_QUERY][None],
        sums[BIAS_VALUE][None],
        attention[3][None],
        sums[BIAS_OUT][None],
        sums[GAIN_TWO][None],
        sums[SHIFT_TWO][None],
        across(up)[None],
        sums[BIAS_UP : BIAS_UP + hidden // width].reshape(1, -1),
        down.reshape(1, -1, width),
        sums[BIAS_DOWN][None],
    )


def solution(mesh):
    per_image = ("dp", "rep")
    matrix, line = P("section", None, None), P("section", None)
    rows = P("section", per_image, None, None)
    kinds = (line, line, matrix, line, line, matrix, line, line, line, matrix, line, matrix, line)
    return jax.shard_map(
        shards,
        mesh=mesh,
        in_specs=(rows, P(per_image, None), P(per_image)) + kinds,
        out_specs=(rows, rows) + kinds,
        check_vma=False,
    )
```

```python
import functools
from functools import partial
import math

import jax
import jax.numpy as jnp
from jax import lax
from jax.experimental import pallas as pl
from jax.experimental.pallas import tpu as pltpu
from jax.sharding import PartitionSpec as P

HEAD_DIM = 64
PAIR = 2 * HEAD_DIM
ROW_TILE = 16
COLUMNS = 256

norm_eps = 1e-06
masked_score = -1e30
f32 = jnp.float32
bf16 = jnp.bfloat16

NN = (((1,), (0,)), ((), ()))
NT = (((1,), (1,)), ((), ()))
TN = (((0,), (0,)), ((), ()))

VECTORS = range(9)
GAIN_ONE, SHIFT_ONE, BIAS_QUERY, BIAS_VALUE, BIAS_OUT, GAIN_TWO, SHIFT_TWO, BIAS_DOWN, BIAS_UP = VECTORS
SECTION, DP, REP = "section", "dp", "rep"
U, A, QKV, O, R, C, M, SLOPE, GD, GZ, GB, GR, GO, GQKV, GA, GU, E, Y, GRAD = range(19)
WEIGHTS = range(19, 23)
W_QKV, W_OUT, W_UP, W_DOWN = WEIGHTS
DOWN, UP, QUERY_VALUE, KEY_OUT, SUMS, OUT = range(100, 106)
ORDER = "FAGFdAFUdAuQdqKudqkuqdkusdkquskqukqdksdqusqkuk"
COST = 10**11
ANY = pl.BlockSpec(memory_space=pl.ANY)


def product(left, right, dims):
    return lax.dot_general(left, right, dims, preferred_element_type=f32)


def spans(size, step):
    return [slice(at, min(at + step, size)) for at in range(0, size, step)]


def column_sum(values):
    return jnp.sum(values, axis=0, keepdims=True)


def centre(values):
    centred = values - jnp.mean(values, axis=-1, keepdims=True)
    scale = lax.rsqrt(jnp.mean(centred * centred, axis=-1, keepdims=True) + norm_eps)
    return centred * scale, scale


class Copies:
    def __init__(self, sem, pairs):
        self.made = {
            name: pltpu.make_async_copy(source, target, sem.at[at])
            for at, (name, (source, target)) in enumerate(pairs.items())
        }

    def start(self, *names):
        for name in names or tuple(self.made):
            if name in self.made:
                self.made[name].start()

    def wait(self, *names):
        for name in names or tuple(self.made):
            if name in self.made:
                self.made.pop(name).wait()


def first_section():
    return lax.axis_index(SECTION) == 0


def row_mask(shape, count):
    return lax.broadcasted_iota(jnp.int32, shape, 0) < count


def gather_matrix(slots_of, count):
    slots = slots_of.shape[1]
    shape = (-(-slots // ROW_TILE) * ROW_TILE, slots)
    patch = lax.broadcasted_iota(jnp.int32, shape, 0)
    slot = lax.broadcasted_iota(jnp.int32, shape, 1)
    chosen = jnp.broadcast_to(slots_of, shape) == patch
    return jnp.where(chosen & (slot < count), 1.0, 0.0).astype(bf16)


def forward_part(r, wait, done, vec, weights, count):
    rows, width = r[U].shape[-2:]
    hidden = weights[W_UP].shape[1]
    for span in spans(rows, ROW_TILE):
        normal, _ = centre(r[U][span, :].astype(f32))
        r[A][span, :] = (normal * vec(GAIN_ONE) + vec(SHIFT_ONE)).astype(bf16)
    done(U, A)
    wait(W_QKV)
    for span in spans(3 * width, COLUMNS):
        packed = product(r[A][...], weights[W_QKV][:, span], NN)
        if span.start < width:
            packed = packed + vec(BIAS_QUERY, span)
        elif span.start >= 2 * width:
            packed = packed + vec(BIAS_VALUE, slice(span.start - 2 * width, span.stop - 2 * width))
        r[QKV][:, span] = packed.astype(bf16)
    done(QKV)
    low = (lax.broadcasted_iota(jnp.int32, (1, PAIR), 1) < HEAD_DIM).astype(bf16)
    lane = lax.broadcasted_iota(jnp.int32, (rows, PAIR), 1) < HEAD_DIM
    for at in range(0, width, PAIR):
        query = r[QKV][:, at : at + PAIR]
        key = r[QKV][:, width + at : width + at + PAIR]
        value = r[QKV][:, 2 * width + at : 2 * width + at + PAIR]
        both = jnp.concatenate([query * low, query * (1 - low)], axis=0)
        scores = product(both, key, NT) * (1.0 / math.sqrt(HEAD_DIM))
        live = lax.broadcasted_iota(jnp.int32, scores.shape, 1) < count
        scores = jnp.where(live, scores, masked_score)
        powers = jnp.exp(scores - jnp.max(scores, axis=-1, keepdims=True))
        chance = powers * (1.0 / jnp.sum(powers, axis=-1, keepdims=True))
        mixed = product(chance.astype(bf16), value, NN)
        r[O][:, at : at + PAIR] = jnp.where(lane, mixed[:rows], mixed[rows:]).astype(bf16)
    done(O)
    wait(W_OUT)
    for span in spans(width, COLUMNS):
        r[R][:, span] = r[U][:, span].astype(f32) + (
            product(r[O][...], weights[W_OUT][:, span], NN) + vec(BIAS_OUT, span)
        )
    for span in spans(rows, ROW_TILE):
        normal, _ = centre(r[R][span, :])
        r[C][span, :] = (normal * vec(GAIN_TWO) + vec(SHIFT_TWO)).astype(bf16)
    done(R, C)
    wait(W_UP)
    for span in spans(hidden, COLUMNS):
        z = product(r[C][...], weights[W_UP][:, span], NN) + vec(BIAS_UP, span)
        share = 0.5 * (1.0 + lax.erf(z * math.sqrt(0.5)))
        r[M][:, span] = (z * share).astype(bf16)
        r[SLOPE][:, span] = share + z * (jnp.exp(-0.5 * z * z) * (1.0 / math.sqrt(2 * math.pi)))
    done(M, SLOPE)


def output_part(r, vec, weights, count):
    rows, width = r[R].shape
    outer = r[Y].shape[0]
    for span in spans(width, COLUMNS):
        y = r[R][:, span] + (product(r[M][...], weights[W_DOWN][:, span], NN) + vec(BIAS_DOWN, span))
        r[Y][:, span] = jnp.where(row_mask(y.shape, count), y, 0.0).astype(bf16)[:outer]


def norm_back(normal, scale, gain, grad):
    x = grad * gain
    return scale * (
        x - jnp.mean(x, axis=-1, keepdims=True) - normal * jnp.mean(x * normal, axis=-1, keepdims=True)
    )


def feed_forward_back(r, wait, done, vec, weights, count, add):
    rows, width = r[R].shape
    hidden = weights[W_UP].shape[1]
    for span in spans(rows, ROW_TILE):
        live = lax.broadcasted_iota(jnp.int32, (ROW_TILE, width), 0) + span.start < count
        r[GD][span, :] = jnp.where(live, r[E][span, :], jnp.zeros((), bf16))
    add(BIAS_DOWN, lambda: column_sum(r[GD][...].astype(f32)))
    wait(W_DOWN, SLOPE)
    for span in spans(hidden, COLUMNS):
        gz = product(r[GD][...], weights[W_DOWN][span, :], NT) * r[SLOPE][:, span]
        r[GZ][:, span] = gz.astype(bf16)
        add(BIAS_UP, lambda: column_sum(r[GZ][:, span].astype(f32)), span)
    done(GZ)
    wait(W_UP, R)
    for span in spans(width, COLUMNS):
        r[GR][:, span] = product(r[GZ][...], weights[W_UP][span, :], NT)
    gain_sum, shift_sum = 0.0, 0.0
    for span in spans(rows, ROW_TILE):
        normal, scale = centre(r[R][span, :])
        gc = r[GR][span, :]
        gain_sum, shift_sum = gain_sum + gc * normal, shift_sum + gc
        gr = r[GD][span, :].astype(f32) + norm_back(normal, scale, vec(GAIN_TWO), gc)
        r[GR][span, :] = gr
        r[GB][span, :] = gr.astype(bf16)
    done(GB, GR)
    add(GAIN_TWO, lambda: column_sum(gain_sum))
    add(SHIFT_TWO, lambda: column_sum(shift_sum))
    add(BIAS_OUT, lambda: column_sum(r[GB][...].astype(f32)))


def attention_back(r, wait, done, vec, weights, count, add):
    rows, width = r[U].shape
    wait(GB, W_OUT)
    for span in spans(width, COLUMNS):
        r[GO][:, span] = product(r[GB][...], weights[W_OUT][span, :], NT).astype(bf16)
    wait(QKV)
    low = (lax.broadcasted_iota(jnp.int32, (1, PAIR), 1) < HEAD_DIM).astype(bf16)
    lane = lax.broadcasted_iota(jnp.int32, (rows, PAIR), 1) < HEAD_DIM
    score_scale = 1.0 / math.sqrt(HEAD_DIM)
    live = row_mask((rows, rows), count)
    for at in range(0, width, PAIR):
        query = r[QKV][:, at : at + PAIR]
        key = r[QKV][:, width + at : width + at + PAIR]
        value = r[QKV][:, 2 * width + at : 2 * width + at + PAIR]
        go = r[GO][:, at : at + PAIR]
        scores = product(jnp.concatenate([key * low, key * (1 - low)], axis=0), query, NT) * score_scale
        grads = product(jnp.concatenate([value * low, value * (1 - low)], axis=0), go, NT)
        chances, inner = [], []
        for head in range(2):
            score = jnp.where(live, scores[head * rows : (head + 1) * rows], masked_score)
            powers = jnp.exp(score - jnp.max(score, axis=0, keepdims=True))
            chance = powers * (1.0 / jnp.sum(powers, axis=0, keepdims=True))
            gp = grads[head * rows : (head + 1) * rows]
            gs = chance * (gp - jnp.sum(gp * chance, axis=0, keepdims=True))
            chances.append(chance.astype(bf16))
            inner.append(jnp.where(live, gs, 0.0).astype(bf16))
        gw = product(jnp.concatenate(chances, axis=0), go, NN)
        gk = product(jnp.concatenate(inner, axis=0), query, NN) * score_scale
        gq = [product(gs, key, TN) * score_scale for gs in inner]
        r[GQKV][:, at : at + PAIR] = jnp.where(lane, gq[0], gq[1]).astype(bf16)
        r[GQKV][:, width + at : width + at + PAIR] = jnp.where(lane, gk[:rows], gk[rows:]).astype(bf16)
        r[GQKV][:, 2 * width + at : 2 * width + at + PAIR] = jnp.where(lane, gw[:rows], gw[rows:]).astype(
            bf16
        )
    done(GQKV)
    add(BIAS_QUERY, lambda: column_sum(r[GQKV][:, :width].astype(f32)))
    add(BIAS_VALUE, lambda: column_sum(r[GQKV][:, 2 * width :].astype(f32)))
    wait(W_QKV, U, GR)
    for span in spans(width, COLUMNS):
        r[GA][:, span] = product(r[GQKV][...], weights[W_QKV][span, :], NT)
    gain_sum, shift_sum = 0.0, 0.0
    for span in spans(rows, ROW_TILE):
        normal, scale = centre(r[U][span, :].astype(f32))
        ga = r[GA][span, :]
        gain_sum, shift_sum = gain_sum + ga * normal, shift_sum + ga
        gu = r[GR][span, :] + norm_back(normal, scale, vec(GAIN_ONE), ga)
        r[GU][span, :] = gu.astype(bf16)
    add(GAIN_ONE, lambda: column_sum(gain_sum))
    add(SHIFT_ONE, lambda: column_sum(shift_sum))


def vector_reader(refs):
    named = dict(zip(VECTORS, refs))

    def vec(name, span=None):
        ref = named[name]
        return (ref[...] if span is None else ref[:, span]).astype(f32)

    return vec


def vector_adder(ref):
    def add(name, values, span=None):
        values = values()
        start = 0 if span is None else span.start
        row, start = VECTORS.index(name) + start // ref.shape[1], start % ref.shape[1]
        ref[row : row + 1, start : start + values.shape[1]] += values

    return add


def pad_rows(target, source):
    inner, rows = source.shape[0], target.shape[0]
    target[:inner, :] = source[...]
    if rows > inner:
        target[inner:, :] = jnp.zeros((rows - inner, target.shape[1]), target.dtype)


def padded_rows(slots):
    return -(-slots // ROW_TILE) * ROW_TILE


def image_block(shape, image):
    return pl.BlockSpec((pl.Squeezed(),) + tuple(shape), lambda *_: (image, 0, 0))


def fixed_block(shape):
    return pl.BlockSpec(tuple(shape), lambda *_: (0,) * len(shape))


def weight_scratch(weights):
    return [pltpu.VMEM(weight.shape, weight.dtype) for weight in weights] + [
        pltpu.SemaphoreType.DMA((len(weights),))
    ]


def fetch_weights(sem, hbm, local, order=WEIGHTS):
    found = dict(zip(WEIGHTS, zip(hbm, local)))
    return Copies(sem, {name: found[name] for name in order}), dict(zip(WEIGHTS, local))


def call(kernel, steps, scalars, ins, in_specs, outs, out_specs, scratch, name, aliases=None):
    return pl.pallas_call(
        kernel,
        out_shape=outs,
        grid_spec=pltpu.PrefetchScalarGridSpec(
            num_scalar_prefetch=1,
            grid=(steps,),
            in_specs=in_specs,
            out_specs=out_specs,
            scratch_shapes=scratch,
        ),
        compiler_params=pltpu.CompilerParams(
            dimension_semantics=("arbitrary",), vmem_limit_bytes=60 << 20
        ),
        input_output_aliases=aliases or {},
        cost_estimate=pl.CostEstimate(flops=COST, bytes_accessed=COST, transcendentals=0),
        name=name,
    )(scalars, *ins)


def split(refs, *sizes):
    out, at = [], 0
    for size in sizes:
        out.append(refs[at] if size is None else refs[at : at + size])
        at += 1 if size is None else size
    assert at == len(refs)
    return out


def nothing(*_):
    return None


SAVED = (U, A, QKV, O, R, C, M, SLOPE)
MADE = (GZ, GB, GQKV, GRAD)


def image_shapes(slots, rows, width, hidden):
    narrow, wide = (rows, width), (rows, hidden)
    return {
        U: (narrow, bf16),
        A: (narrow, bf16),
        QKV: ((rows, 3 * width), bf16),
        O: (narrow, bf16),
        R: (narrow, f32),
        C: (narrow, bf16),
        M: (wide, bf16),
        SLOPE: (wide, f32),
        GD: (narrow, bf16),
        GZ: (wide, bf16),
        GB: (narrow, bf16),
        GR: (narrow, f32),
        GO: (narrow, bf16),
        GQKV: ((rows, 3 * width), bf16),
        GA: (narrow, f32),
        GU: (narrow, bf16),
        E: (narrow, bf16),
        Y: ((slots, width), bf16),
        GRAD: ((slots, width), bf16),
    }


def first_forward(image, carry, count, index, source, vectors, weights):
    images, slots, width = source.shape
    rows, hidden = padded_rows(slots), weights[2].shape[1]
    shapes = image_shapes(slots, rows, width, hidden)
    work = SAVED + (Y,)
    old = () if carry is None else tuple(carry)
    at = 1 + 2 + len(vectors) + 4

    def kernel(count_ref, index_ref, source_ref, *rest):
        vecs, hbm, _, places, y_ref, local, sem, scratch, padded, out_sem = split(
            rest, len(vectors), 4, len(old), len(work), None, 4, None, len(work), None, None
        )

        @pl.when(first_section())
        def _():
            fetch, near = fetch_weights(sem, hbm, local)
            fetch.start()
            kept = count_ref[image]
            refs = dict(zip(work, scratch))
            store = Copies(out_sem, {name: (refs[name], place.at[image]) for name, place in zip(work, places)})
            pad_rows(padded, source_ref)
            chosen = gather_matrix(index_ref[image : image + 1, :], kept)
            refs[U][:slots, :] = product(chosen, padded[...], TN).astype(bf16)
            refs[U][slots:, :] = jnp.zeros((rows - slots, width), bf16)
            vec = vector_reader(vecs)
            forward_part(refs, fetch.wait, store.start, vec, near, kept)
            fetch.wait(W_DOWN)
            output_part(refs, vec, near, kept)
            store.start(Y)
            y_ref[...] = refs[Y][...]
            store.wait()

    *carry, output = call(
        kernel,
        1,
        count,
        (index, source) + vectors + weights + old,
        [fixed_block(index.shape), image_block((slots, width), image)]
        + [fixed_block(vector.shape) for vector in vectors]
        + [ANY] * (4 + len(old)),
        [jax.ShapeDtypeStruct((images,) + shapes[name][0], shapes[name][1]) for name in work]
        + [jax.ShapeDtypeStruct((1, slots, width), bf16)],
        [ANY] * len(work) + [image_block((slots, width), 0)],
        weight_scratch(weights)
        + [pltpu.VMEM(*shapes[name]) for name in work]
        + [pltpu.VMEM((rows, width), bf16), pltpu.SemaphoreType.DMA((len(work),))],
        f"first_forward_{image}",
        {at + k: k for k in range(len(old))},
    )
    return carry, output


def middle(image, saved, made, sums, count, received, cotangent, vectors, weights):
    images, slots, width = cotangent.shape
    rows, hidden = padded_rows(slots), weights[2].shape[1]
    shapes = image_shapes(slots, rows, width, hidden)
    carry = SAVED + MADE
    lines = -(-(len(vectors) - 1 + hidden // width) // 8) * 8
    work = (E, GD, GR, GO, GA, GU) + carry
    old = tuple(saved) + (() if made is None else tuple(made) + (sums,))
    at = 1 + 2 + len(vectors) + 4

    def kernel(count_ref, received_ref, e_ref, *rest):
        vecs, hbm, previous, places, sums_ref, grad_ref, local, sem, scratch, out_sem = split(
            rest, len(vectors), 4, len(old), len(carry), None, None, 4, None, len(work), None
        )
        sums_ref[...] = jnp.zeros(sums_ref.shape, f32) if made is None else previous[-1][...]

        @pl.when(jnp.logical_not(first_section()))
        def _():
            fetch, near = fetch_weights(sem, hbm, local)
            fetch.start()
            live = count_ref[image]
            refs = dict(zip(work, scratch))
            store = Copies(
                out_sem, {name: (refs[name], place.at[image]) for name, place in zip(carry, places)}
            )
            pad_rows(refs[U], received_ref)
            pad_rows(refs[E], e_ref)
            vec, add = vector_reader(vecs), vector_adder(sums_ref)
            forward_part(refs, fetch.wait, store.start, vec, near, live)
            fetch.wait(W_DOWN)
            feed_forward_back(refs, nothing, store.start, vec, near, live, add)
            attention_back(refs, nothing, store.start, vec, near, live, add)
            refs[GRAD][...] = refs[GU][:slots, :]
            store.start(GRAD)
            grad_ref[...] = refs[GU][:slots, :]
            store.wait()

    results = call(
        kernel,
        1,
        count,
        (received, cotangent) + vectors + weights + old,
        [image_block((slots, width), 0), image_block((slots, width), image)]
        + [fixed_block(vector.shape) for vector in vectors]
        + [ANY] * (4 + len(old) - (made is not None))
        + ([] if made is None else [fixed_block(sums.shape)]),
        [jax.ShapeDtypeStruct((images,) + shapes[name][0], shapes[name][1]) for name in carry]
        + [jax.ShapeDtypeStruct((lines, width), f32), jax.ShapeDtypeStruct((1, slots, width), bf16)],
        [ANY] * len(carry) + [fixed_block((lines, width)), image_block((slots, width), 0)],
        weight_scratch(weights)
        + [pltpu.VMEM(*shapes[name]) for name in work]
        + [pltpu.SemaphoreType.DMA((len(carry),))],
        f"middle_{image}",
        {at + k: k for k in range(len(old))},
    )
    return results[: len(SAVED)], results[len(SAVED) : -2], results[-2], results[-1]


def late_feed_forward(image, saved, made, output, sums, count, received, vectors, weights):
    images, rows, hidden = saved[SAVED.index(M)].shape
    slots, width = received.shape[1:]
    shapes = image_shapes(slots, rows, width, hidden)
    loads = (SLOPE, R, M)
    stores = (GZ, GB, Y)
    work = (SLOPE, R, M, E, GD, GZ, GB, Y)
    near_names = (W_DOWN, W_UP)
    old = [made[MADE.index(GZ)], made[MADE.index(GB)], output, sums]
    at = 1 + 1 + len(vectors) + len(loads) + len(near_names)

    def kernel(count_ref, received_ref, *rest):
        vecs, sources, hbm, previous, places, sums_ref, gr_ref, local, scratch, sem = split(
            rest, len(vectors), len(loads), 2, len(old), len(stores), None, None, 2, len(work), None
        )
        live = count_ref[image]
        refs = dict(zip(work, scratch)) | {GR: gr_ref}
        near = dict(zip(near_names, local))
        far = dict(zip(near_names, hbm))
        source = {name: ref.at[image] for name, ref in zip(loads, sources)}
        place = {name: ref.at[image] for name, ref in zip(stores, places)}
        vec = vector_reader(vecs)
        sums_ref[...] = previous[-1][...]
        early = first_section()

        @pl.when(early)
        def _():
            fetch = Copies(
                sem,
                {
                    W_DOWN: (far[W_DOWN], near[W_DOWN]),
                    SLOPE: (source[SLOPE], refs[SLOPE]),
                    W_UP: (far[W_UP], near[W_UP]),
                    R: (source[R], refs[R]),
                },
            )
            fetch.start()
            store = Copies(sem.at[pl.ds(4, 2)], {name: (refs[name], place[name]) for name in (GZ, GB)})
            pad_rows(refs[E], received_ref)
            feed_forward_back(refs, fetch.wait, store.start, vec, near, live, vector_adder(sums_ref))
            store.wait()

        @pl.when(jnp.logical_not(early))
        def _():
            fetch = Copies(
                sem,
                {
                    M: (source[M], refs[M]),
                    W_DOWN: (far[W_DOWN], near[W_DOWN]),
                    R: (source[R], refs[R]),
                },
            )
            fetch.start()
            fetch.wait()
            output_part(refs, vec, near, live)
            store = Copies(sem.at[pl.ds(4, 1)], {Y: (refs[Y], place[Y])})
            store.start()
            store.wait()

    gz, gb, output, sums, gr = call(
        kernel,
        1,
        count,
        (received,)
        + vectors
        + tuple(saved[SAVED.index(name)] for name in loads)
        + tuple(weights[WEIGHTS.index(name)] for name in near_names)
        + tuple(old),
        [image_block((slots, width), 0)]
        + [fixed_block(vector.shape) for vector in vectors]
        + [ANY] * (len(loads) + len(near_names) + len(old) - 1)
        + [fixed_block(sums.shape)],
        [
            jax.ShapeDtypeStruct((images,) + shapes[GZ][0], bf16),
            jax.ShapeDtypeStruct((images,) + shapes[GB][0], bf16),
            jax.ShapeDtypeStruct((images,) + shapes[Y][0], bf16),
            jax.ShapeDtypeStruct(sums.shape, f32),
            jax.ShapeDtypeStruct((1,) + shapes[GR][0], f32),
        ],
        [ANY] * 3 + [fixed_block(sums.shape), image_block(shapes[GR][0], 0)],
        [pltpu.VMEM(weights[WEIGHTS.index(name)].shape, bf16) for name in near_names]
        + [pltpu.VMEM(*shapes[name]) for name in work]
        + [pltpu.SemaphoreType.DMA((7,))],
        f"late_feed_forward_{image}",
        {at + k: k for k in range(len(old))},
    )
    return [gz, gb] + list(made[2:]), output, sums, gr


def late_attention(image, saved, made, sums, gr, count, index, vectors, weights):
    images, slots, width = made[MADE.index(GRAD)].shape
    rows, hidden = saved[SAVED.index(M)].shape[1:]
    shapes = image_shapes(slots, rows, width, hidden)
    work = (GB, QKV, U, GO, GQKV, GA, GU, GRAD)
    near_names = (W_OUT, W_QKV)
    old = [made[MADE.index(GQKV)], made[MADE.index(GRAD)], sums]
    sources = (made[MADE.index(GB)], saved[SAVED.index(QKV)], saved[SAVED.index(U)])
    at = 1 + 2 + len(vectors) + len(sources) + len(near_names)

    def kernel(count_ref, index_ref, gr_ref, *rest):
        vecs, loads, hbm, previous, gqkv_ref, grad_ref, sums_ref, local, scratch, sem = split(
            rest, len(vectors), len(sources), 2, len(old), None, None, None, 2, len(work), None
        )
        live = count_ref[image]
        sums_ref[...] = previous[-1][...]
        refs = dict(zip(work, scratch)) | {GR: gr_ref}
        near = dict(zip(near_names, local))

        @pl.when(first_section())
        def _():
            fetch = Copies(
                sem,
                {
                    GB: (loads[0].at[image], refs[GB]),
                    W_OUT: (hbm[0], near[W_OUT]),
                    QKV: (loads[1].at[image], refs[QKV]),
                    W_QKV: (hbm[1], near[W_QKV]),
                    U: (loads[2].at[image], refs[U]),
                },
            )
            fetch.start()
            store = Copies(
                sem.at[pl.ds(5, 2)],
                {GQKV: (refs[GQKV], gqkv_ref.at[image]), GRAD: (refs[GRAD], grad_ref.at[image])},
            )
            attention_back(refs, fetch.wait, store.start, vector_reader(vecs), near, live, vector_adder(sums_ref))
            chosen = gather_matrix(index_ref[image : image + 1, :], live)
            refs[GRAD][...] = product(chosen, refs[GU][:slots, :], NN)[:slots, :].astype(bf16)
            store.start(GRAD)
            store.wait()

    gqkv, grad, sums = call(
        kernel,
        1,
        count,
        (index, gr)
        + vectors
        + sources
        + tuple(weights[WEIGHTS.index(name)] for name in near_names)
        + tuple(old),
        [fixed_block(index.shape), image_block((rows, width), 0)]
        + [fixed_block(vector.shape) for vector in vectors]
        + [ANY] * (len(sources) + len(near_names) + len(old) - 1)
        + [fixed_block(sums.shape)],
        [
            jax.ShapeDtypeStruct((images,) + shapes[GQKV][0], bf16),
            jax.ShapeDtypeStruct((images,) + shapes[GRAD][0], bf16),
            jax.ShapeDtypeStruct(sums.shape, f32),
        ],
        [ANY] * 2 + [fixed_block(sums.shape)],
        [pltpu.VMEM(weights[WEIGHTS.index(name)].shape, bf16) for name in near_names]
        + [pltpu.VMEM(*shapes[name]) for name in work]
        + [pltpu.SemaphoreType.DMA((7,))],
        f"late_attention_{image}",
        {at + k: k for k in range(len(old))},
    )
    return list(made[:2]) + [gqkv, grad], sums


def pick(table, at):
    value = table[0]
    for k in range(1, len(table)):
        value = jnp.where(at == k, table[k], value)
    return value


def weight_gradient(side, arrays, blocks, name):
    depth = arrays[0].shape[0]
    width = min(array.shape[1] for array in arrays)
    half = len(blocks) // 2

    def chosen(i, scalar_ref):
        bit = scalar_ref[0]
        return jnp.where(i < half, (1 - bit) * half + i, bit * half + i - half)

    def kernel(scalar_ref, *refs):
        send_ref, keep_ref = refs[-2:]
        step = pl.program_id(0)
        block = chosen(step, scalar_ref)
        for left, right in dict.fromkeys((left, right) for left, right, _ in blocks):
            here = functools.reduce(
                jnp.logical_or, [block == k for k, entry in enumerate(blocks) if entry[:2] == (left, right)]
            )

            @pl.when(here & (step < half))
            def _():
                send_ref[...] = product(refs[left][...], refs[right][...], TN).astype(bf16)

            @pl.when(here & (step >= half))
            def _():
                keep_ref[...] = product(refs[left][...], refs[right][...], TN)

    def columns(at):
        table = [column if right == at else 0 for _, right, column in blocks]
        return pl.BlockSpec((depth, width), lambda i, s: (0, pick(table, chosen(i, s))))

    return call(
        kernel,
        2 * half,
        side,
        arrays,
        [columns(at) for at in range(len(arrays))],
        [jax.ShapeDtypeStruct((half * width, width), bf16), jax.ShapeDtypeStruct((half * width, width), f32)],
        [
            pl.BlockSpec((width, width), lambda i, s: (jnp.minimum(i, half - 1), 0)),
            pl.BlockSpec((width, width), lambda i, s: (jnp.maximum(i - half, 0), 0)),
        ],
        [],
        name,
    )


def down_gradient(side, count, m, cotangent, received):
    images, slots, width = cotangent.shape
    rows, hidden = m.shape[1:]
    blocks = hidden // width
    half = blocks // 2
    scalars = jnp.concatenate([side, count])

    def chosen(i, scalar_ref):
        bit = scalar_ref[0]
        return jnp.where(i < half, (1 - bit) * half + i, bit * half + i - half)

    def kernel(scalar_ref, m_ref, e_ref, *rest):
        arrived, (send_ref, keep_ref, gd_ref) = rest[:images], rest[images:]
        step = pl.program_id(0)
        early = first_section()

        @pl.when(step == 0)
        def _():
            for image in range(images):
                live = row_mask((slots, width), scalar_ref[1 + image])
                top = slice(image * rows, image * rows + slots)
                gd_ref[top, :] = jnp.where(live, jnp.where(early, arrived[image][...], e_ref[image]), jnp.zeros((), bf16))
                gd_ref[top.stop : (image + 1) * rows, :] = jnp.zeros((rows - slots, width), bf16)

        left = m_ref[...].reshape(images * rows, width)

        @pl.when(step < half)
        def _():
            send_ref[...] = product(left, gd_ref[...], TN).astype(bf16)

        @pl.when(step >= half)
        def _():
            keep_ref[...] = product(left, gd_ref[...], TN)

    return call(
        kernel,
        blocks,
        scalars,
        (m, cotangent) + tuple(received),
        [
            pl.BlockSpec((images, rows, width), lambda i, s: (0, 0, chosen(i, s))),
            fixed_block(cotangent.shape),
        ]
        + [image_block((slots, width), 0)] * images,
        [jax.ShapeDtypeStruct((half * width, width), bf16), jax.ShapeDtypeStruct((half * width, width), f32)],
        [
            pl.BlockSpec((width, width), lambda i, s: (jnp.minimum(i, half - 1), 0)),
            pl.BlockSpec((width, width), lambda i, s: (jnp.maximum(i - half, 0), 0)),
        ],
        [pltpu.VMEM((images * rows, width), bf16)],
        "grad_down",
    )


def assembled(side, mine, other, places, shapes, name, before=None):
    width = mine.shape[1]
    half = mine.shape[0] // width
    before = before or {}

    def chosen(i, scalar_ref):
        bit = scalar_ref[0]
        return jnp.where(i < half, bit * half + i, (1 - bit) * half + i - half)

    def kernel(scalar_ref, mine_ref, other_ref, *refs):
        outs = refs[len(before) :]
        step = pl.program_id(0)
        block = chosen(step, scalar_ref)
        for at, out_ref in enumerate(outs):
            here = functools.reduce(
                jnp.logical_or, [block == k for k, entry in enumerate(places) if entry[0] == at]
            )

            @pl.when(here & (step < half))
            def _():
                out_ref[...] = mine_ref[...].astype(f32)

            @pl.when(here & (step >= half))
            def _():
                out_ref[...] = other_ref[...].astype(f32)

    def place(at):
        last = [entry for entry in places if entry[0] == at][0]
        entries = [entry if entry[0] == at else last for entry in places]

        def index(i, s):
            block = chosen(i, s)
            return (pick([entry[1] for entry in entries], block), pick([entry[2] for entry in entries], block))

        return index

    return call(
        kernel,
        2 * half,
        side,
        (mine, other) + tuple(before.values()),
        [
            pl.BlockSpec((width, width), lambda i, s: (jnp.minimum(i, half - 1), 0)),
            pl.BlockSpec((width, width), lambda i, s: (jnp.maximum(i - half, 0), 0)),
        ]
        + [ANY] * len(before),
        [jax.ShapeDtypeStruct(shape, f32) for shape in shapes],
        [pl.BlockSpec((width, width), place(at)) for at in range(len(shapes))],
        [],
        name,
        {3 + k: at for k, at in enumerate(before)},
    )


def swapped(value, axis, stride):
    length = lax.axis_size(axis)
    return lax.ppermute(value, axis, [(i, i ^ stride) for i in range(length)])


def bit_of(axis, stride):
    return (lax.axis_index(axis) // stride) % 2


def plain_call(kernel, ins, outs, scratch, name):
    return pl.pallas_call(
        kernel,
        out_shape=outs,
        in_specs=[ANY] * len(ins),
        out_specs=[pl.BlockSpec(memory_space=pltpu.VMEM)] * len(outs),
        scratch_shapes=scratch,
        compiler_params=pltpu.CompilerParams(vmem_limit_bytes=60 << 20),
        cost_estimate=pl.CostEstimate(flops=COST, bytes_accessed=COST, transcendentals=0),
        name=name,
    )(*ins)


def halved(keep, coming, stride):
    height, width = keep.shape[0] // 2, keep.shape[1]
    if height % ROW_TILE:
        bit = bit_of(DP, stride)
        pair = keep + coming.astype(f32)
        send = lax.dynamic_slice_in_dim(pair, (1 - bit) * height, height, axis=0).astype(bf16)
        return send, lax.dynamic_slice_in_dim(pair, bit * height, height, axis=0)

    def kernel(keep_ref, coming_ref, send_ref, stay_ref, kept, came, sem):
        bit = bit_of(DP, stride)
        copies = []
        for at, half in enumerate((1 - bit, bit)):
            rows = pl.ds(pl.multiple_of(half * height, ROW_TILE), height)
            copies.append(pltpu.make_async_copy(keep_ref.at[rows, :], kept.at[at], sem.at[2 * at]))
            copies.append(pltpu.make_async_copy(coming_ref.at[rows, :], came.at[at], sem.at[2 * at + 1]))
        for copy in copies:
            copy.start()
        for copy in copies[:2]:
            copy.wait()
        send_ref[...] = (kept[0] + came[0].astype(f32)).astype(bf16)
        for copy in copies[2:]:
            copy.wait()
        stay_ref[...] = kept[1] + came[1].astype(f32)

    shape = (height, width)
    return plain_call(
        kernel,
        (keep, coming),
        [jax.ShapeDtypeStruct(shape, bf16), jax.ShapeDtypeStruct(shape, f32)],
        [
            pltpu.VMEM((2,) + shape, f32),
            pltpu.VMEM((2,) + shape, bf16),
            pltpu.SemaphoreType.DMA((4,)),
        ],
        f"halved_{stride}",
    )


def summed(keep, coming, total):
    if keep.shape[0] % ROW_TILE:
        return ((keep + coming.astype(f32)) / total).astype(bf16)

    def kernel(keep_ref, coming_ref, out_ref, kept, came, sem):
        copies = [
            pltpu.make_async_copy(keep_ref, kept, sem.at[0]),
            pltpu.make_async_copy(coming_ref, came, sem.at[1]),
        ]
        for copy in copies:
            copy.start()
        for copy in copies:
            copy.wait()
        out_ref[...] = ((kept[...] + came[...].astype(f32)) / total).astype(bf16)

    return plain_call(
        kernel,
        (keep, coming),
        [jax.ShapeDtypeStruct(keep.shape, bf16)],
        [pltpu.VMEM(keep.shape, f32), pltpu.VMEM(keep.shape, bf16), pltpu.SemaphoreType.DMA((2,))],
        "summed",
    )[0]


def joined(mine, other, stride):
    height, width = mine.shape
    if height % ROW_TILE:
        first = bit_of(DP, stride) == 0
        return jnp.concatenate([jnp.where(first, mine, other), jnp.where(first, other, mine)], axis=0)

    def kernel(mine_ref, other_ref, out_ref, sem):
        bit = bit_of(DP, stride)
        copies = []
        for at, (half, source) in enumerate(((bit, mine_ref), (1 - bit, other_ref))):
            rows = pl.ds(pl.multiple_of(half * height, ROW_TILE), height)
            copies.append(pltpu.make_async_copy(source, out_ref.at[rows, :], sem.at[at]))
        for copy in copies:
            copy.start()
        for copy in copies:
            copy.wait()

    return plain_call(
        kernel,
        (mine, other),
        [jax.ShapeDtypeStruct((2 * height, width), bf16)],
        [pltpu.SemaphoreType.DMA((2,))],
        f"joined_{stride}",
    )[0]


def strides_of(size):
    return [1 << at for at in range(size.bit_length() - 1)]


class Line:
    def __init__(self):
        self.last = None

    def gate(self, value):
        if self.last is None:
            return value
        return lax.optimization_barrier((value, self.last))[0]

    def passed(self, value):
        self.last = value


class Exchange:
    def __init__(self, line, send, keep, strides, total):
        self.line, self.keep, self.strides, self.total = line, keep, strides, total
        self.at, self.value, self.result = 0, None, None
        self.coming = swapped(send, REP, 1)

    def advance(self):
        coming = self.line.gate(self.coming)
        count = len(self.strides)
        if self.at < count:
            stride = self.strides[self.at]
            send, self.keep = halved(self.keep, coming, stride)
            self.coming = swapped(send, DP, stride)
            self.line.passed(send)
        elif self.at == count:
            self.value = summed(self.keep, coming, self.total)
            self.coming = swapped(self.value, DP, self.strides[-1])
            self.line.passed(self.value)
        elif self.at <= 2 * count:
            stride = self.strides[2 * count - self.at]
            self.value = joined(self.value, coming, stride)
            if self.at < 2 * count:
                self.coming = swapped(self.value, DP, self.strides[2 * count - 1 - self.at])
            else:
                self.coming = swapped(self.value, REP, 1)
            self.line.passed(self.value)
        else:
            self.result = (self.value, coming)
            self.line.passed(coming)
        self.at += 1


class Total:
    def __init__(self, line, value, strides, total):
        self.line, self.value, self.total = line, value, total
        self.partners = [(REP, 1)] + [(DP, stride) for stride in strides]
        self.at, self.result = 0, None
        self.coming = swapped(value, *self.partners[0])

    def advance(self):
        self.value = self.value + self.line.gate(self.coming)
        self.at += 1
        if self.at < len(self.partners):
            self.coming = swapped(self.value, *self.partners[self.at])
        else:
            self.result = self.value / self.total
        self.line.passed(self.value)


def shards(
    boundary,
    keep_index,
    keep_count,
    gain_one,
    shift_one,
    w_qkv,
    bias_query,
    bias_value,
    w_out,
    bias_out,
    gain_two,
    shift_two,
    w_up,
    bias_up,
    w_down,
    bias_down,
):
    images = keep_index.shape[0]
    width = boundary.shape[-1]
    weights = (w_qkv[0], w_out[0], w_up[0], w_down[0])
    hidden = weights[2].shape[1]
    vectors = (gain_one, shift_one, bias_query, bias_value, bias_out, gain_two, shift_two, bias_down, bias_up)
    rows_in = boundary[0]

    line = Line()
    carry, received = None, []
    for image in range(images):
        carry, first_output = first_forward(image, carry, keep_count, keep_index, rows_in, vectors, weights)
        received.append(lax.ppermute(first_output, SECTION, [(0, 1)]))
    saved, output = carry[:-1], carry[-1]
    made, sums, returned = None, None, []
    for image in range(images):
        saved, made, sums, grad_first = middle(
            image, saved, made, sums, keep_count, received[image], rows_in, vectors, weights
        )
        returned.append(lax.ppermute(grad_first, SECTION, [(1, 0)]))
    line.passed(grad_first)

    def flat(name):
        array = saved[SAVED.index(name)] if name in SAVED else made[MADE.index(name)]
        return array.reshape(-1, array.shape[-1])

    total = images * lax.axis_size((DP, REP))
    side = lax.axis_index(REP).astype(jnp.int32)[None]
    near_first = strides_of(lax.axis_size(DP))
    far_first = near_first[1::-1] + near_first[2:]
    square, many = (width, width), hidden // width
    forwards, attentions = list(range(images)), list(range(images))
    residual = [None] * images
    exchanges, outs = {}, {}

    def begin(name, pair, strides):
        line.passed(pair[0])
        exchanges[name] = Exchange(line, *pair, strides, total)

    def feed_forward():
        nonlocal made, output, sums
        image = forwards.pop(0)
        made, output, sums, residual[image] = late_feed_forward(
            image, saved, made, output, sums, line.gate(keep_count), returned[image], vectors, weights
        )
        line.passed(residual[image])

    def attention():
        nonlocal made, sums
        image = attentions.pop(0)
        made, sums = late_attention(
            image, saved, made, sums, residual[image], line.gate(keep_count), keep_index, vectors, weights
        )
        line.passed(sums)

    def grad_down():
        pair = down_gradient(line.gate(side), keep_count, saved[SAVED.index(M)], rows_in, returned)
        begin(DOWN, pair, near_first)

    def grad_up():
        blocks = [(0, 1, column) for column in range(many)]
        begin(UP, weight_gradient(line.gate(side), (flat(C), flat(GZ)), blocks, "grad_up"), near_first)

    def grad_query_value():
        exchanges[SUMS] = Total(line, sums, near_first, total)
        pair = weight_gradient(line.gate(side), (flat(A), flat(GQKV)), [(0, 1, 0), (0, 1, 2)], "grad_query_value")
        begin(QUERY_VALUE, pair, far_first)

    def grad_key_out():
        arrays = (flat(A), flat(GQKV), flat(O), flat(GB))
        pair = weight_gradient(line.gate(side), arrays, [(0, 1, 1), (2, 3, 0)], "grad_key_out")
        begin(KEY_OUT, pair, near_first)

    def end(name):
        places, shapes = {
            DOWN: ([(0, k, 0) for k in range(many)], [(hidden, width)]),
            UP: ([(0, 0, k) for k in range(many)], [(width, hidden)]),
            QUERY_VALUE: ([(0, 0, 0), (0, 0, 2)], [(width, 3 * width)]),
            KEY_OUT: ([(0, 0, 1), (1, 0, 0)], [(width, 3 * width), square]),
        }[name]
        part = name in (QUERY_VALUE, KEY_OUT)
        before = {0: outs[QKV]} if part and QKV in outs else {}
        mine, other = exchanges[name].result
        whole = assembled(line.gate(side), mine, other, places, shapes, f"whole_{name}", before)
        line.passed(whole[0])
        outs[QKV if part else name] = whole[0]
        outs.update({OUT: piece for piece in whole[1:]})

    steps = dict(zip("FAGUQK", (feed_forward, attention, grad_down, grad_up, grad_query_value, grad_key_out)))
    transfers = dict(zip("duqks", (DOWN, UP, QUERY_VALUE, KEY_OUT, SUMS)))
    stages = 2 * len(near_first) + 2
    plain = "FA" * images + "GUQK" + "duqk" * stages + "s" * (stages // 2)
    for step in ORDER if (images, stages) == (3, 8) else plain:
        if step in steps:
            steps[step]()
            continue
        name = transfers[step]
        exchanges[name].advance()
        if exchanges[name].result is not None and name != SUMS:
            end(name)
    assert all(exchange.result is not None for exchange in exchanges.values())
    sums = exchanges[SUMS].result
    small = [sums[at : at + 1] for at in VECTORS[:-1]]
    return (
        output[None],
        made[MADE.index(GRAD)][None],
        small[GAIN_ONE],
        small[SHIFT_ONE],
        outs[QKV][None],
        small[BIAS_QUERY],
        small[BIAS_VALUE],
        outs[OUT][None],
        small[BIAS_OUT],
        small[GAIN_TWO],
        small[SHIFT_TWO],
        outs[UP][None],
        sums[BIAS_UP : BIAS_UP + many].reshape(1, -1),
        outs[DOWN][None],
        small[BIAS_DOWN],
    )


def solution(mesh):
    per_image = (DP, REP)
    matrix, line = P(SECTION, None, None), P(SECTION, None)
    rows = P(SECTION, per_image, None, None)
    kinds = (line, line, matrix, line, line, matrix, line, line, line, matrix, line, matrix, line)
    return jax.shard_map(
        shards,
        mesh=mesh,
        in_specs=(rows, P(per_image, None), P(per_image)) + kinds,
        out_specs=(rows, rows) + kinds,
        check_vma=False,
    )
```

```python
import functools
from functools import partial
import math

import jax
import jax.numpy as jnp
from jax import lax
from jax.experimental import pallas as pl
from jax.experimental.pallas import tpu as pltpu
from jax.sharding import PartitionSpec as P

HEAD_DIM = 64
PAIR = 2 * HEAD_DIM
ROW_TILE = 16
COLUMNS = 256

norm_eps = 1e-06
masked_score = -1e30
f32 = jnp.float32
bf16 = jnp.bfloat16

NN = (((1,), (0,)), ((), ()))
NT = (((1,), (1,)), ((), ()))
TN = (((0,), (0,)), ((), ()))

VECTORS = range(9)
GAIN_ONE, SHIFT_ONE, BIAS_QUERY, BIAS_VALUE, BIAS_OUT, GAIN_TWO, SHIFT_TWO, BIAS_DOWN, BIAS_UP = VECTORS
SECTION, DP, REP = "section", "dp", "rep"
U, A, QKV, O, R, C, M, SLOPE, GD, GZ, GB, GR, GO, GQKV, GA, GU, E, Y, GRAD = range(19)
WEIGHTS = range(19, 23)
W_QKV, W_OUT, W_UP, W_DOWN = WEIGHTS
DOWN, UP, QUERY_VALUE, KEY_OUT, SUMS, OUT = range(100, 106)
ORDER = "FAGFUduAQduqdKukdqukqdskuqdkqskuqkdsdquqkusk"
COST = 10**11
ANY = pl.BlockSpec(memory_space=pl.ANY)


def product(left, right, dims):
    return lax.dot_general(left, right, dims, preferred_element_type=f32)


def spans(size, step):
    return [slice(at, min(at + step, size)) for at in range(0, size, step)]


def column_sum(values):
    return jnp.sum(values, axis=0, keepdims=True)


def centre(values):
    centred = values - jnp.mean(values, axis=-1, keepdims=True)
    scale = lax.rsqrt(jnp.mean(centred * centred, axis=-1, keepdims=True) + norm_eps)
    return centred * scale, scale


class Copies:
    def __init__(self, sem, pairs):
        self.made = {
            name: pltpu.make_async_copy(source, target, sem.at[at])
            for at, (name, (source, target)) in enumerate(pairs.items())
        }

    def start(self, *names):
        for name in names or tuple(self.made):
            if name in self.made:
                self.made[name].start()

    def wait(self, *names):
        for name in names or tuple(self.made):
            if name in self.made:
                self.made.pop(name).wait()


def first_section():
    return lax.axis_index(SECTION) == 0


def row_mask(shape, count):
    return lax.broadcasted_iota(jnp.int32, shape, 0) < count


def gather_matrix(slots_of, count):
    slots = slots_of.shape[1]
    shape = (-(-slots // ROW_TILE) * ROW_TILE, slots)
    patch = lax.broadcasted_iota(jnp.int32, shape, 0)
    slot = lax.broadcasted_iota(jnp.int32, shape, 1)
    chosen = jnp.broadcast_to(slots_of, shape) == patch
    return jnp.where(chosen & (slot < count), 1.0, 0.0).astype(bf16)


def forward_part(r, wait, done, vec, weights, count):
    rows, width = r[U].shape[-2:]
    hidden = weights[W_UP].shape[1]
    for span in spans(rows, ROW_TILE):
        normal, _ = centre(r[U][span, :].astype(f32))
        r[A][span, :] = (normal * vec(GAIN_ONE) + vec(SHIFT_ONE)).astype(bf16)
    done(U, A)
    wait(W_QKV)
    for span in spans(3 * width, COLUMNS):
        packed = product(r[A][...], weights[W_QKV][:, span], NN)
        if span.start < width:
            packed = packed + vec(BIAS_QUERY, span)
        elif span.start >= 2 * width:
            packed = packed + vec(BIAS_VALUE, slice(span.start - 2 * width, span.stop - 2 * width))
        r[QKV][:, span] = packed.astype(bf16)
    done(QKV)
    low = (lax.broadcasted_iota(jnp.int32, (1, PAIR), 1) < HEAD_DIM).astype(bf16)
    lane = lax.broadcasted_iota(jnp.int32, (rows, PAIR), 1) < HEAD_DIM
    for at in range(0, width, PAIR):
        query = r[QKV][:, at : at + PAIR]
        key = r[QKV][:, width + at : width + at + PAIR]
        value = r[QKV][:, 2 * width + at : 2 * width + at + PAIR]
        both = jnp.concatenate([query * low, query * (1 - low)], axis=0)
        scores = product(both, key, NT) * (1.0 / math.sqrt(HEAD_DIM))
        live = lax.broadcasted_iota(jnp.int32, scores.shape, 1) < count
        scores = jnp.where(live, scores, masked_score)
        powers = jnp.exp(scores - jnp.max(scores, axis=-1, keepdims=True))
        chance = powers * (1.0 / jnp.sum(powers, axis=-1, keepdims=True))
        mixed = product(chance.astype(bf16), value, NN)
        r[O][:, at : at + PAIR] = jnp.where(lane, mixed[:rows], mixed[rows:]).astype(bf16)
    done(O)
    wait(W_OUT)
    for span in spans(width, COLUMNS):
        r[R][:, span] = r[U][:, span].astype(f32) + (
            product(r[O][...], weights[W_OUT][:, span], NN) + vec(BIAS_OUT, span)
        )
    for span in spans(rows, ROW_TILE):
        normal, _ = centre(r[R][span, :])
        r[C][span, :] = (normal * vec(GAIN_TWO) + vec(SHIFT_TWO)).astype(bf16)
    done(R, C)
    wait(W_UP)
    for span in spans(hidden, COLUMNS):
        z = product(r[C][...], weights[W_UP][:, span], NN) + vec(BIAS_UP, span)
        share = 0.5 * (1.0 + lax.erf(z * math.sqrt(0.5)))
        r[M][:, span] = (z * share).astype(bf16)
        r[SLOPE][:, span] = share + z * (jnp.exp(-0.5 * z * z) * (1.0 / math.sqrt(2 * math.pi)))
    done(M, SLOPE)


def output_part(r, vec, weights, count):
    rows, width = r[R].shape
    outer = r[Y].shape[0]
    for span in spans(width, COLUMNS):
        y = r[R][:, span] + (product(r[M][...], weights[W_DOWN][:, span], NN) + vec(BIAS_DOWN, span))
        r[Y][:, span] = jnp.where(row_mask(y.shape, count), y, 0.0).astype(bf16)[:outer]


def norm_back(normal, scale, gain, grad):
    x = grad * gain
    return scale * (
        x - jnp.mean(x, axis=-1, keepdims=True) - normal * jnp.mean(x * normal, axis=-1, keepdims=True)
    )


def feed_forward_back(r, wait, done, vec, weights, count, add):
    rows, width = r[R].shape
    hidden = weights[W_UP].shape[1]
    for span in spans(rows, ROW_TILE):
        live = lax.broadcasted_iota(jnp.int32, (ROW_TILE, width), 0) + span.start < count
        r[GD][span, :] = jnp.where(live, r[E][span, :], jnp.zeros((), bf16))
    add(BIAS_DOWN, lambda: column_sum(r[GD][...].astype(f32)))
    wait(W_DOWN, SLOPE)
    for span in spans(hidden, COLUMNS):
        gz = product(r[GD][...], weights[W_DOWN][span, :], NT) * r[SLOPE][:, span]
        r[GZ][:, span] = gz.astype(bf16)
        add(BIAS_UP, lambda: column_sum(r[GZ][:, span].astype(f32)), span)
    done(GZ)
    wait(W_UP, R)
    for span in spans(width, COLUMNS):
        r[GR][:, span] = product(r[GZ][...], weights[W_UP][span, :], NT)
    gain_sum, shift_sum = 0.0, 0.0
    for span in spans(rows, ROW_TILE):
        normal, scale = centre(r[R][span, :])
        gc = r[GR][span, :]
        gain_sum, shift_sum = gain_sum + gc * normal, shift_sum + gc
        gr = r[GD][span, :].astype(f32) + norm_back(normal, scale, vec(GAIN_TWO), gc)
        r[GR][span, :] = gr
        r[GB][span, :] = gr.astype(bf16)
    done(GB, GR)
    add(GAIN_TWO, lambda: column_sum(gain_sum))
    add(SHIFT_TWO, lambda: column_sum(shift_sum))
    add(BIAS_OUT, lambda: column_sum(r[GB][...].astype(f32)))


def attention_back(r, wait, done, vec, weights, count, add):
    rows, width = r[U].shape
    wait(GB, W_OUT)
    for span in spans(width, COLUMNS):
        r[GO][:, span] = product(r[GB][...], weights[W_OUT][span, :], NT).astype(bf16)
    wait(QKV)
    low = (lax.broadcasted_iota(jnp.int32, (1, PAIR), 1) < HEAD_DIM).astype(bf16)
    lane = lax.broadcasted_iota(jnp.int32, (rows, PAIR), 1) < HEAD_DIM
    score_scale = 1.0 / math.sqrt(HEAD_DIM)
    live = row_mask((rows, rows), count)
    for at in range(0, width, PAIR):
        query = r[QKV][:, at : at + PAIR]
        key = r[QKV][:, width + at : width + at + PAIR]
        value = r[QKV][:, 2 * width + at : 2 * width + at + PAIR]
        go = r[GO][:, at : at + PAIR]
        scores = product(jnp.concatenate([key * low, key * (1 - low)], axis=0), query, NT) * score_scale
        grads = product(jnp.concatenate([value * low, value * (1 - low)], axis=0), go, NT)
        chances, inner = [], []
        for head in range(2):
            score = jnp.where(live, scores[head * rows : (head + 1) * rows], masked_score)
            powers = jnp.exp(score - jnp.max(score, axis=0, keepdims=True))
            chance = powers * (1.0 / jnp.sum(powers, axis=0, keepdims=True))
            gp = grads[head * rows : (head + 1) * rows]
            gs = chance * (gp - jnp.sum(gp * chance, axis=0, keepdims=True))
            chances.append(chance.astype(bf16))
            inner.append(jnp.where(live, gs, 0.0).astype(bf16))
        gw = product(jnp.concatenate(chances, axis=0), go, NN)
        gk = product(jnp.concatenate(inner, axis=0), query, NN) * score_scale
        gq = [product(gs, key, TN) * score_scale for gs in inner]
        r[GQKV][:, at : at + PAIR] = jnp.where(lane, gq[0], gq[1]).astype(bf16)
        r[GQKV][:, width + at : width + at + PAIR] = jnp.where(lane, gk[:rows], gk[rows:]).astype(bf16)
        r[GQKV][:, 2 * width + at : 2 * width + at + PAIR] = jnp.where(lane, gw[:rows], gw[rows:]).astype(
            bf16
        )
    done(GQKV)
    add(BIAS_QUERY, lambda: column_sum(r[GQKV][:, :width].astype(f32)))
    add(BIAS_VALUE, lambda: column_sum(r[GQKV][:, 2 * width :].astype(f32)))
    wait(W_QKV, U, GR)
    for span in spans(width, COLUMNS):
        r[GA][:, span] = product(r[GQKV][...], weights[W_QKV][span, :], NT)
    gain_sum, shift_sum = 0.0, 0.0
    for span in spans(rows, ROW_TILE):
        normal, scale = centre(r[U][span, :].astype(f32))
        ga = r[GA][span, :]
        gain_sum, shift_sum = gain_sum + ga * normal, shift_sum + ga
        gu = r[GR][span, :] + norm_back(normal, scale, vec(GAIN_ONE), ga)
        r[GU][span, :] = gu.astype(bf16)
    add(GAIN_ONE, lambda: column_sum(gain_sum))
    add(SHIFT_ONE, lambda: column_sum(shift_sum))


def vector_reader(refs):
    named = dict(zip(VECTORS, refs))

    def vec(name, span=None):
        ref = named[name]
        return (ref[...] if span is None else ref[:, span]).astype(f32)

    return vec


def vector_adder(ref):
    def add(name, values, span=None):
        values = values()
        start = 0 if span is None else span.start
        row, start = VECTORS.index(name) + start // ref.shape[1], start % ref.shape[1]
        ref[row : row + 1, start : start + values.shape[1]] += values

    return add


def pad_rows(target, source):
    inner, rows = source.shape[0], target.shape[0]
    target[:inner, :] = source[...]
    if rows > inner:
        target[inner:, :] = jnp.zeros((rows - inner, target.shape[1]), target.dtype)


def padded_rows(slots):
    return -(-slots // ROW_TILE) * ROW_TILE


def image_block(shape, image):
    return pl.BlockSpec((pl.Squeezed(),) + tuple(shape), lambda *_: (image, 0, 0))


def fixed_block(shape):
    return pl.BlockSpec(tuple(shape), lambda *_: (0,) * len(shape))


def weight_scratch(weights):
    return [pltpu.VMEM(weight.shape, weight.dtype) for weight in weights] + [
        pltpu.SemaphoreType.DMA((len(weights),))
    ]


def fetch_weights(sem, hbm, local, order=WEIGHTS):
    found = dict(zip(WEIGHTS, zip(hbm, local)))
    return Copies(sem, {name: found[name] for name in order}), dict(zip(WEIGHTS, local))


def call(kernel, steps, scalars, ins, in_specs, outs, out_specs, scratch, name, aliases=None, room=60):
    return pl.pallas_call(
        kernel,
        out_shape=outs,
        grid_spec=pltpu.PrefetchScalarGridSpec(
            num_scalar_prefetch=1,
            grid=(steps,),
            in_specs=in_specs,
            out_specs=out_specs,
            scratch_shapes=scratch,
        ),
        compiler_params=pltpu.CompilerParams(
            dimension_semantics=("arbitrary",), vmem_limit_bytes=room << 20
        ),
        input_output_aliases=aliases or {},
        cost_estimate=pl.CostEstimate(flops=COST, bytes_accessed=COST, transcendentals=0),
        name=name,
    )(scalars, *ins)


def split(refs, *sizes):
    out, at = [], 0
    for size in sizes:
        out.append(refs[at] if size is None else refs[at : at + size])
        at += 1 if size is None else size
    assert at == len(refs)
    return out


def nothing(*_):
    return None


SAVED = (U, A, QKV, O, R, C, M, SLOPE)
MADE = (GZ, GB, GQKV, GRAD)


def image_shapes(slots, rows, width, hidden):
    narrow, wide = (rows, width), (rows, hidden)
    return {
        U: (narrow, bf16),
        A: (narrow, bf16),
        QKV: ((rows, 3 * width), bf16),
        O: (narrow, bf16),
        R: (narrow, f32),
        C: (narrow, bf16),
        M: (wide, bf16),
        SLOPE: (wide, f32),
        GD: (narrow, bf16),
        GZ: (wide, bf16),
        GB: (narrow, bf16),
        GR: (narrow, f32),
        GO: (narrow, bf16),
        GQKV: ((rows, 3 * width), bf16),
        GA: (narrow, f32),
        GU: (narrow, bf16),
        E: (narrow, bf16),
        Y: ((slots, width), bf16),
        GRAD: ((slots, width), bf16),
    }


def first_forward(image, carry, count, index, source, vectors, weights):
    images, slots, width = source.shape
    rows, hidden = padded_rows(slots), weights[2].shape[1]
    shapes = image_shapes(slots, rows, width, hidden)
    work = SAVED + (Y,)
    old = () if carry is None else tuple(carry)
    at = 1 + 2 + len(vectors) + 4

    def kernel(count_ref, index_ref, source_ref, *rest):
        vecs, hbm, _, places, y_ref, local, sem, scratch, padded, out_sem = split(
            rest, len(vectors), 4, len(old), len(work), None, 4, None, len(work), None, None
        )

        @pl.when(first_section())
        def _():
            fetch, near = fetch_weights(sem, hbm, local)
            fetch.start()
            kept = count_ref[image]
            refs = dict(zip(work, scratch))
            store = Copies(out_sem, {name: (refs[name], place.at[image]) for name, place in zip(work, places)})
            pad_rows(padded, source_ref)
            chosen = gather_matrix(index_ref[image : image + 1, :], kept)
            refs[U][:slots, :] = product(chosen, padded[...], TN).astype(bf16)
            refs[U][slots:, :] = jnp.zeros((rows - slots, width), bf16)
            vec = vector_reader(vecs)
            forward_part(refs, fetch.wait, store.start, vec, near, kept)
            fetch.wait(W_DOWN)
            output_part(refs, vec, near, kept)
            store.start(Y)
            y_ref[...] = refs[Y][...]
            store.wait()

    *carry, output = call(
        kernel,
        1,
        count,
        (index, source) + vectors + weights + old,
        [fixed_block(index.shape), image_block((slots, width), image)]
        + [fixed_block(vector.shape) for vector in vectors]
        + [ANY] * (4 + len(old)),
        [jax.ShapeDtypeStruct((images,) + shapes[name][0], shapes[name][1]) for name in work]
        + [jax.ShapeDtypeStruct((1, slots, width), bf16)],
        [ANY] * len(work) + [image_block((slots, width), 0)],
        weight_scratch(weights)
        + [pltpu.VMEM(*shapes[name]) for name in work]
        + [pltpu.VMEM((rows, width), bf16), pltpu.SemaphoreType.DMA((len(work),))],
        f"first_forward_{image}",
        {at + k: k for k in range(len(old))},
    )
    return carry, output


def tick(first, image, late, saved, made, output, sums, scalars, index, received, source, vectors, weights):
    images, slots, width = source.shape
    rows, hidden = padded_rows(slots), weights[2].shape[1]
    shapes = image_shapes(slots, rows, width, hidden)
    carry = SAVED + MADE + (Y,)
    lines = -(-(len(vectors) - 1 + hidden // width) // 8) * 8
    work = (E, GD, GR, GO, GA, GU) + carry
    old = tuple(saved) + (() if made is None else tuple(made)) + (output,) + (() if made is None else (sums,))
    slots_of = [k for k, name in enumerate(carry) if made is not None or name not in MADE]
    slots_of += [] if made is None else [len(carry)]
    at = 1 + 3 + len(vectors) + 4
    other = first if first is not None else late if late is not None else image

    def kernel(scalar_ref, index_ref, received_ref, source_ref, *rest):
        vecs, hbm, previous, places, sums_ref, send_ref, local, sem, scratch, out_sem = split(
            rest, len(vectors), 4, len(old), len(carry), None, None, 4, None, len(work), None
        )
        sums_ref[...] = jnp.zeros(sums_ref.shape, f32) if made is None else previous[-1][...]
        early = first_section()
        later = jnp.logical_not(early)
        here = jnp.where(early, other, image)
        live = scalar_ref[here]
        refs = dict(zip(work, scratch))
        place = {name: ref.at[here] for name, ref in zip(carry, places)}
        store = Copies(out_sem, {name: (refs[name], place[name]) for name in carry})
        vec, add = vector_reader(vecs), vector_adder(sums_ref)

        def gathered():
            pad_rows(refs[E], source_ref)
            chosen = gather_matrix(index_ref[first : first + 1, :], live)
            refs[U][:slots, :] = product(chosen, refs[E][...], TN).astype(bf16)
            refs[U][slots:, :] = jnp.zeros((rows - slots, width), bf16)

        def forward(fetch, near):
            forward_part(refs, fetch.wait, store.start, vec, near, live)
            fetch.wait(W_DOWN)

        def backward(near):
            feed_forward_back(refs, nothing, store.start, vec, near, live, add)
            attention_back(refs, nothing, store.start, vec, near, live, add)

        def sent():
            refs[GRAD][...] = refs[GU][:slots, :]
            store.start(GRAD)
            send_ref[...] = refs[GU][:slots, :]

        if first is not None:
            fetch, near = fetch_weights(sem, hbm, local)
            fetch.start()

            @pl.when(early)
            def _():
                gathered()

            @pl.when(later)
            def _():
                pad_rows(refs[U], received_ref)

            forward(fetch, near)

            @pl.when(early)
            def _():
                output_part(refs, vec, near, live)
                store.start(Y)
                send_ref[...] = refs[Y][...]
                Copies(out_sem, {name: (refs[name], place[name]) for name in carry}).wait(*SAVED, Y)

            @pl.when(later)
            def _():
                pad_rows(refs[E], source_ref)
                backward(near)
                sent()
                Copies(out_sem, {name: (refs[name], place[name]) for name in carry}).wait(*SAVED, *MADE)

            return

        @pl.when(later)
        def _():
            fetch, near = fetch_weights(sem, hbm, local)
            fetch.start()
            pad_rows(refs[U], received_ref)
            pad_rows(refs[E], source_ref)
            forward(fetch, near)
            if late is None:
                backward(near)
                sent()
                store.wait(*SAVED, *MADE)

        if late is None:
            return

        @pl.when(early)
        def _():
            fetch, _ = fetch_weights(sem, hbm, local, (W_DOWN, W_UP, W_OUT, W_QKV))
            load = Copies(out_sem, {name: (place[name], refs[name]) for name in (SLOPE, R, QKV, U)})
            fetch.start()
            load.start()
            pad_rows(refs[E], received_ref)
            fetch.wait()
            load.wait()

        backward(dict(zip(WEIGHTS, local)))

        @pl.when(early)
        def _():
            chosen = gather_matrix(index_ref[late : late + 1, :], live)
            refs[GRAD][...] = product(chosen, refs[GU][:slots, :], NN)[:slots, :].astype(bf16)
            store.start(GRAD)

        @pl.when(later)
        def _():
            sent()
            Copies(out_sem, {name: (refs[name], place[name]) for name in SAVED}).wait()

        store.wait(*MADE)

    results = call(
        kernel,
        1,
        scalars,
        (index, received, source) + vectors + weights + old,
        [
            fixed_block(index.shape),
            image_block((slots, width), 0),
            pl.BlockSpec(
                (pl.Squeezed(), slots, width), lambda i, s: (jnp.where(s[images] == 0, other, image), 0, 0)
            ),
        ]
        + [fixed_block(vector.shape) for vector in vectors]
        + [ANY] * (4 + len(old) - (made is not None))
        + ([] if made is None else [fixed_block(sums.shape)]),
        [jax.ShapeDtypeStruct((images,) + shapes[name][0], shapes[name][1]) for name in carry]
        + [jax.ShapeDtypeStruct((lines, width), f32), jax.ShapeDtypeStruct((1, slots, width), bf16)],
        [ANY] * len(carry) + [fixed_block((lines, width)), image_block((slots, width), 0)],
        weight_scratch(weights)
        + [pltpu.VMEM(*shapes[name]) for name in work]
        + [pltpu.SemaphoreType.DMA((len(carry),))],
        f"tick_{image}",
        {at + k: slot for k, slot in enumerate(slots_of)},
    )
    saved, made = results[: len(SAVED)], results[len(SAVED) : len(SAVED) + len(MADE)]
    return saved, made, results[-3], results[-2], results[-1]


def late_feed_forward(image, outputs, saved, made, output, sums, count, received, vectors, weights):
    images, rows, hidden = saved[SAVED.index(M)].shape
    slots, width = received.shape[1:]
    shapes = image_shapes(slots, rows, width, hidden)
    loads = (SLOPE, R, M)
    stores = (GZ, GB, Y)
    work = (SLOPE, R, M, E, GD, GZ, GB, Y)
    near_names = (W_DOWN, W_UP)
    old = [made[MADE.index(GZ)], made[MADE.index(GB)], output, sums]
    at = 1 + 1 + len(vectors) + len(loads) + len(near_names)

    def kernel(count_ref, received_ref, *rest):
        vecs, sources, hbm, previous, places, sums_ref, gr_ref, local, scratch, sem = split(
            rest, len(vectors), len(loads), 2, len(old), len(stores), None, None, 2, len(work), None
        )
        live = count_ref[image]
        refs = dict(zip(work, scratch)) | {GR: gr_ref}
        near = dict(zip(near_names, local))
        far = dict(zip(near_names, hbm))
        source = {name: ref.at[image] for name, ref in zip(loads, sources)}
        place = {name: ref.at[image] for name, ref in zip(stores, places)}
        vec = vector_reader(vecs)
        sums_ref[...] = previous[-1][...]
        early = first_section()

        @pl.when(early)
        def _():
            fetch = Copies(
                sem,
                {
                    E: (received_ref.at[0], refs[Y]),
                    W_DOWN: (far[W_DOWN], near[W_DOWN]),
                    SLOPE: (source[SLOPE], refs[SLOPE]),
                    W_UP: (far[W_UP], near[W_UP]),
                    R: (source[R], refs[R]),
                },
            )
            fetch.start()
            store = Copies(sem.at[pl.ds(5, 2)], {name: (refs[name], place[name]) for name in (GZ, GB)})
            fetch.wait(E)
            pad_rows(refs[E], refs[Y])
            feed_forward_back(refs, fetch.wait, store.start, vec, near, live, vector_adder(sums_ref))
            store.wait()

        @pl.when(jnp.logical_not(early))
        def _():
            fetch = Copies(sem, {W_DOWN: (far[W_DOWN], near[W_DOWN])})
            fetch.start()
            for which in outputs:
                load = Copies(
                    sem.at[pl.ds(1, 2)],
                    {name: (sources[loads.index(name)].at[which], refs[name]) for name in (R, M)},
                )
                load.start()
                fetch.wait()
                load.wait()
                output_part(refs, vec, near, count_ref[which])
                store = Copies(sem.at[pl.ds(4, 1)], {Y: (refs[Y], places[stores.index(Y)].at[which])})
                store.start()
                store.wait()

    gz, gb, output, sums, gr = call(
        kernel,
        1,
        count,
        (received,)
        + vectors
        + tuple(saved[SAVED.index(name)] for name in loads)
        + tuple(weights[WEIGHTS.index(name)] for name in near_names)
        + tuple(old),
        [ANY]
        + [fixed_block(vector.shape) for vector in vectors]
        + [ANY] * (len(loads) + len(near_names) + len(old) - 1)
        + [fixed_block(sums.shape)],
        [
            jax.ShapeDtypeStruct((images,) + shapes[GZ][0], bf16),
            jax.ShapeDtypeStruct((images,) + shapes[GB][0], bf16),
            jax.ShapeDtypeStruct((images,) + shapes[Y][0], bf16),
            jax.ShapeDtypeStruct(sums.shape, f32),
            jax.ShapeDtypeStruct((1,) + shapes[GR][0], f32),
        ],
        [ANY] * 3 + [fixed_block(sums.shape), image_block(shapes[GR][0], 0)],
        [pltpu.VMEM(weights[WEIGHTS.index(name)].shape, bf16) for name in near_names]
        + [pltpu.VMEM(*shapes[name]) for name in work]
        + [pltpu.SemaphoreType.DMA((7,))],
        f"late_feed_forward_{image}",
        {at + k: k for k in range(len(old))},
    )
    return [gz, gb] + list(made[2:]), output, sums, gr


def late_attention(image, saved, made, sums, gr, count, index, vectors, weights):
    images, slots, width = made[MADE.index(GRAD)].shape
    rows, hidden = saved[SAVED.index(M)].shape[1:]
    shapes = image_shapes(slots, rows, width, hidden)
    work = (GB, QKV, U, GO, GQKV, GA, GU, GRAD)
    near_names = (W_OUT, W_QKV)
    old = [made[MADE.index(GQKV)], made[MADE.index(GRAD)], sums]
    sources = (made[MADE.index(GB)], saved[SAVED.index(QKV)], saved[SAVED.index(U)])
    at = 1 + 2 + len(vectors) + len(sources) + len(near_names)

    def kernel(count_ref, index_ref, gr_ref, *rest):
        vecs, loads, hbm, previous, gqkv_ref, grad_ref, sums_ref, local, scratch, sem = split(
            rest, len(vectors), len(sources), 2, len(old), None, None, None, 2, len(work), None
        )
        live = count_ref[image]
        sums_ref[...] = previous[-1][...]
        refs = dict(zip(work, scratch)) | {GR: gr_ref}
        near = dict(zip(near_names, local))

        @pl.when(first_section())
        def _():
            fetch = Copies(
                sem,
                {
                    GB: (loads[0].at[image], refs[GB]),
                    W_OUT: (hbm[0], near[W_OUT]),
                    QKV: (loads[1].at[image], refs[QKV]),
                    W_QKV: (hbm[1], near[W_QKV]),
                    U: (loads[2].at[image], refs[U]),
                },
            )
            fetch.start()
            store = Copies(
                sem.at[pl.ds(5, 2)],
                {GQKV: (refs[GQKV], gqkv_ref.at[image]), GRAD: (refs[GRAD], grad_ref.at[image])},
            )
            attention_back(refs, fetch.wait, store.start, vector_reader(vecs), near, live, vector_adder(sums_ref))
            chosen = gather_matrix(index_ref[image : image + 1, :], live)
            refs[GRAD][...] = product(chosen, refs[GU][:slots, :], NN)[:slots, :].astype(bf16)
            store.start(GRAD)
            store.wait()

    gqkv, grad, sums = call(
        kernel,
        1,
        count,
        (index, gr)
        + vectors
        + sources
        + tuple(weights[WEIGHTS.index(name)] for name in near_names)
        + tuple(old),
        [fixed_block(index.shape), image_block((rows, width), 0)]
        + [fixed_block(vector.shape) for vector in vectors]
        + [ANY] * (len(sources) + len(near_names) + len(old) - 1)
        + [fixed_block(sums.shape)],
        [
            jax.ShapeDtypeStruct((images,) + shapes[GQKV][0], bf16),
            jax.ShapeDtypeStruct((images,) + shapes[GRAD][0], bf16),
            jax.ShapeDtypeStruct(sums.shape, f32),
        ],
        [ANY] * 2 + [fixed_block(sums.shape)],
        [pltpu.VMEM(weights[WEIGHTS.index(name)].shape, bf16) for name in near_names]
        + [pltpu.VMEM(*shapes[name]) for name in work]
        + [pltpu.SemaphoreType.DMA((7,))],
        f"late_attention_{image}",
        {at + k: k for k in range(len(old))},
    )
    return list(made[:2]) + [gqkv, grad], sums


def pick(table, at):
    value = table[0]
    for k in range(1, len(table)):
        value = jnp.where(at == k, table[k], value)
    return value


def weight_gradient(side, arrays, blocks, name):
    depth = arrays[0].shape[0]
    width = min(array.shape[1] for array in arrays)
    half = len(blocks) // 2

    def chosen(i, scalar_ref):
        bit = scalar_ref[0]
        return jnp.where(i < half, (1 - bit) * half + i, bit * half + i - half)

    def kernel(scalar_ref, *refs):
        send_ref, keep_ref = refs[-2:]
        step = pl.program_id(0)
        block = chosen(step, scalar_ref)
        for left, right in dict.fromkeys((left, right) for left, right, _ in blocks):
            here = functools.reduce(
                jnp.logical_or, [block == k for k, entry in enumerate(blocks) if entry[:2] == (left, right)]
            )

            @pl.when(here & (step < half))
            def _():
                send_ref[...] = product(refs[left][...], refs[right][...], TN).astype(bf16)

            @pl.when(here & (step >= half))
            def _():
                keep_ref[...] = product(refs[left][...], refs[right][...], TN).astype(bf16)

    def columns(at):
        table = [column if right == at else 0 for _, right, column in blocks]
        return pl.BlockSpec((depth, width), lambda i, s: (0, pick(table, chosen(i, s))))

    return call(
        kernel,
        2 * half,
        side,
        arrays,
        [columns(at) for at in range(len(arrays))],
        [jax.ShapeDtypeStruct((half * width, width), bf16)] * 2,
        [
            pl.BlockSpec((width, width), lambda i, s: (jnp.minimum(i, half - 1), 0)),
            pl.BlockSpec((width, width), lambda i, s: (jnp.maximum(i - half, 0), 0)),
        ],
        [],
        name,
        room=60,
    )


def down_gradient(side, count, m, cotangent, received):
    images, slots, width = cotangent.shape
    rows, hidden = m.shape[1:]
    blocks = hidden // width
    half = blocks // 2
    scalars = jnp.concatenate([side, count])

    def chosen(i, scalar_ref):
        bit = scalar_ref[0]
        return jnp.where(i < half, (1 - bit) * half + i, bit * half + i - half)

    def kernel(scalar_ref, m_ref, e_ref, *rest):
        arrived, (send_ref, keep_ref, gd_ref) = rest[:images], rest[images:]
        step = pl.program_id(0)
        early = first_section()

        @pl.when(step == 0)
        def _():
            for image in range(images):
                live = row_mask((slots, width), scalar_ref[1 + image])
                top = slice(image * rows, image * rows + slots)
                gd_ref[top, :] = jnp.where(live, jnp.where(early, arrived[image][...], e_ref[image]), jnp.zeros((), bf16))
                gd_ref[top.stop : (image + 1) * rows, :] = jnp.zeros((rows - slots, width), bf16)

        left = m_ref[...].reshape(images * rows, width)

        @pl.when(step < half)
        def _():
            send_ref[...] = product(left, gd_ref[...], TN).astype(bf16)

        @pl.when(step >= half)
        def _():
            keep_ref[...] = product(left, gd_ref[...], TN).astype(bf16)

    return call(
        kernel,
        blocks,
        scalars,
        (m, cotangent) + tuple(received),
        [
            pl.BlockSpec((images, rows, width), lambda i, s: (0, 0, chosen(i, s))),
            fixed_block(cotangent.shape),
        ]
        + [image_block((slots, width), 0)] * images,
        [jax.ShapeDtypeStruct((half * width, width), bf16)] * 2,
        [
            pl.BlockSpec((width, width), lambda i, s: (jnp.minimum(i, half - 1), 0)),
            pl.BlockSpec((width, width), lambda i, s: (jnp.maximum(i - half, 0), 0)),
        ],
        [pltpu.VMEM((images * rows, width), bf16)],
        "grad_down",
        room=60,
    )


def plain_call(kernel, ins, outs, scratch, name):
    return pl.pallas_call(
        kernel,
        out_shape=outs,
        in_specs=[ANY] * len(ins),
        out_specs=[pl.BlockSpec(memory_space=pltpu.VMEM)] * len(outs),
        scratch_shapes=scratch,
        compiler_params=pltpu.CompilerParams(vmem_limit_bytes=16 << 20),
        cost_estimate=pl.CostEstimate(flops=COST, bytes_accessed=COST, transcendentals=0),
        name=name,
    )(*ins)


def assembled(own, stride, pieces, places, shapes, before):
    shape = pieces[0].shape

    def kernel(*refs):
        sources, _, outs, (raw, wide, sem) = split(refs, 2, len(before), len(shapes), 3)
        core = lax.axis_index(REP) if own else 1 - lax.axis_index(REP)
        near = bit_of(DP, stride)
        loads = [pltpu.make_async_copy(source, raw.at[k], sem.at[k]) for k, source in enumerate(sources)]
        for load in loads:
            load.start()

        def stores(k, act):
            block = 2 * core + (near if k == 0 else 1 - near)
            for at, (which, row, column) in enumerate(places):
                rows, columns = pl.ds(row * shape[0], shape[0]), pl.ds(column * shape[1], shape[1])

                @pl.when(block == at)
                def _():
                    act(pltpu.make_async_copy(wide.at[k], outs[which].at[rows, columns], sem.at[2 + k]))

        for k in range(2):
            loads[k].wait()
            wide[k] = raw[k].astype(f32)
            stores(k, lambda copy: copy.start())
        for k in range(2):
            stores(k, lambda copy: copy.wait())

    return pl.pallas_call(
        kernel,
        out_shape=[jax.ShapeDtypeStruct(whole, f32) for whole in shapes],
        in_specs=[ANY] * (2 + len(before)),
        out_specs=[ANY] * len(shapes),
        scratch_shapes=[
            pltpu.VMEM((2,) + shape, bf16),
            pltpu.VMEM((2,) + shape, f32),
            pltpu.SemaphoreType.DMA((4,)),
        ],
        input_output_aliases={2 + k: k for k in range(len(before))},
        compiler_params=pltpu.CompilerParams(vmem_limit_bytes=16 << 20),
        cost_estimate=pl.CostEstimate(flops=COST, bytes_accessed=COST, transcendentals=0),
        name="assembled",
    )(*pieces, *before)


def swapped(value, axis, stride):
    length = lax.axis_size(axis)
    return lax.ppermute(value, axis, [(i, i ^ stride) for i in range(length)])


def bit_of(axis, stride):
    return (lax.axis_index(axis) // stride) % 2


def halved(keep, coming, stride):
    height, width = keep.shape[0] // 2, keep.shape[1]
    if height % ROW_TILE:
        bit = bit_of(DP, stride)
        pair = (keep.astype(f32) + coming.astype(f32)).astype(bf16)
        send = lax.dynamic_slice_in_dim(pair, (1 - bit) * height, height, axis=0)
        return send, lax.dynamic_slice_in_dim(pair, bit * height, height, axis=0)

    def kernel(keep_ref, coming_ref, send_ref, stay_ref, kept, came, sem):
        bit = bit_of(DP, stride)
        copies = []
        for at, half in enumerate((1 - bit, bit)):
            rows = pl.ds(pl.multiple_of(half * height, ROW_TILE), height)
            copies.append(pltpu.make_async_copy(keep_ref.at[rows, :], kept.at[at], sem.at[2 * at]))
            copies.append(pltpu.make_async_copy(coming_ref.at[rows, :], came.at[at], sem.at[2 * at + 1]))
        for copy in copies:
            copy.start()
        for copy in copies[:2]:
            copy.wait()
        send_ref[...] = (kept[0].astype(f32) + came[0].astype(f32)).astype(bf16)
        for copy in copies[2:]:
            copy.wait()
        stay_ref[...] = (kept[1].astype(f32) + came[1].astype(f32)).astype(bf16)

    shape = (height, width)
    return plain_call(
        kernel,
        (keep, coming),
        [jax.ShapeDtypeStruct(shape, bf16)] * 2,
        [
            pltpu.VMEM((2,) + shape, bf16),
            pltpu.VMEM((2,) + shape, bf16),
            pltpu.SemaphoreType.DMA((4,)),
        ],
        f"halved_{stride}",
    )


def summed(keep, coming, total):
    if keep.shape[0] % ROW_TILE:
        return ((keep.astype(f32) + coming.astype(f32)) / total).astype(bf16)

    def kernel(keep_ref, coming_ref, out_ref, kept, came, sem):
        copies = [
            pltpu.make_async_copy(keep_ref, kept, sem.at[0]),
            pltpu.make_async_copy(coming_ref, came, sem.at[1]),
        ]
        for copy in copies:
            copy.start()
        for copy in copies:
            copy.wait()
        out_ref[...] = ((kept[...].astype(f32) + came[...].astype(f32)) / total).astype(bf16)

    return plain_call(
        kernel,
        (keep, coming),
        [jax.ShapeDtypeStruct(keep.shape, bf16)],
        [pltpu.VMEM(keep.shape, bf16), pltpu.VMEM(keep.shape, bf16), pltpu.SemaphoreType.DMA((2,))],
        "summed",
    )[0]


def joined(mine, other, stride):
    height, width = mine.shape
    if height % ROW_TILE:
        first = bit_of(DP, stride) == 0
        return jnp.concatenate([jnp.where(first, mine, other), jnp.where(first, other, mine)], axis=0)

    def kernel(mine_ref, other_ref, out_ref, sem):
        bit = bit_of(DP, stride)
        copies = []
        for at, (half, source) in enumerate(((bit, mine_ref), (1 - bit, other_ref))):
            rows = pl.ds(pl.multiple_of(half * height, ROW_TILE), height)
            copies.append(pltpu.make_async_copy(source, out_ref.at[rows, :], sem.at[at]))
        for copy in copies:
            copy.start()
        for copy in copies:
            copy.wait()

    return plain_call(
        kernel,
        (mine, other),
        [jax.ShapeDtypeStruct((2 * height, width), bf16)],
        [pltpu.SemaphoreType.DMA((2,))],
        f"joined_{stride}",
    )[0]


def strides_of(size):
    return [1 << at for at in range(size.bit_length() - 1)]


class Line:
    def __init__(self):
        self.last = None

    def gate(self, value):
        if self.last is None:
            return value
        return lax.optimization_barrier((value, self.last))[0]

    def passed(self, value):
        self.last = value


class Exchange:
    def __init__(self, line, send, keep, strides, total):
        self.line, self.keep, self.strides, self.total = line, keep, strides, total
        self.at, self.half = 0, None
        self.coming = swapped(send, REP, 1)

    def advance(self):
        coming = self.line.gate(self.coming)
        count = len(self.strides)
        if self.at < count:
            stride = self.strides[self.at]
            send, self.keep = halved(self.keep, coming, stride)
            self.coming = swapped(send, DP, stride)
            self.line.passed(send)
        elif self.at == count:
            self.value = summed(self.keep, coming, self.total)
            self.coming = swapped(self.value, DP, self.strides[-1])
            self.line.passed(self.value)
        elif self.at < 2 * count:
            self.value = joined(self.value, coming, self.strides[2 * count - self.at])
            self.coming = swapped(self.value, DP, self.strides[2 * count - 1 - self.at])
            self.line.passed(self.value)
        elif self.at == 2 * count:
            self.half = (self.value, coming)
            self.others = swapped(lax.optimization_barrier(self.half)[0], REP, 1)
            self.coming = swapped(coming, REP, 1)
        else:
            self.half = (self.others, coming)
        self.at += 1


def added(value, coming):
    def kernel(value_ref, coming_ref, out_ref):
        out_ref[...] = value_ref[...] + coming_ref[...]

    return pl.pallas_call(
        kernel,
        out_shape=jax.ShapeDtypeStruct(value.shape, value.dtype),
        cost_estimate=pl.CostEstimate(flops=COST, bytes_accessed=COST, transcendentals=0),
        name="added",
    )(value, coming)


class Total:
    def __init__(self, line, value, strides):
        self.line, self.value = line, value
        self.partners = [(REP, 1)] + [(DP, stride) for stride in strides]
        self.at = 0
        self.coming = swapped(value, *self.partners[0])

    def advance(self):
        self.value = added(self.value, self.line.gate(self.coming))
        self.at += 1
        if self.at < len(self.partners):
            self.coming = swapped(self.value, *self.partners[self.at])
        self.line.passed(self.value)


def shards(
    boundary,
    keep_index,
    keep_count,
    gain_one,
    shift_one,
    w_qkv,
    bias_query,
    bias_value,
    w_out,
    bias_out,
    gain_two,
    shift_two,
    w_up,
    bias_up,
    w_down,
    bias_down,
):
    images = keep_index.shape[0]
    width = boundary.shape[-1]
    weights = (w_qkv[0], w_out[0], w_up[0], w_down[0])
    hidden = weights[2].shape[1]
    vectors = (gain_one, shift_one, bias_query, bias_value, bias_out, gain_two, shift_two, bias_down, bias_up)
    rows_in = boundary[0]

    line = Line()
    assert images == 3
    section = lax.axis_index(SECTION).astype(jnp.int32)
    scalars = jnp.concatenate([keep_count, section[None]])
    carry, received = None, []
    for image in range(2):
        carry, first_output = first_forward(image, carry, keep_count, keep_index, rows_in, vectors, weights)
        received.append(lax.ppermute(first_output, SECTION, [(0, 1)]))
    saved, output = carry[:-1], carry[-1]
    made, sums, returned = None, None, []
    for image, first, late in ((0, 2, None), (1, None, None), (2, None, 0)):
        saved, made, output, sums, sent = tick(
            first, image, late, saved, made, output, sums, scalars, keep_index, line.gate(received[image]),
            rows_in, vectors, weights,
        )
        line.passed(sent)
        both = [(1, 0)] + ([(0, 1)] if first is not None else [])
        returned.append(lax.ppermute(sent, SECTION, both))
        if first is not None:
            received.append(returned[-1])

    def flat(name):
        array = saved[SAVED.index(name)] if name in SAVED else made[MADE.index(name)]
        return array.reshape(-1, array.shape[-1])

    total = images * lax.axis_size((DP, REP))
    side = lax.axis_index(REP).astype(jnp.int32)[None]
    near_first = strides_of(lax.axis_size(DP))
    far_first = near_first[1::-1] + near_first[2:]
    square, many = (width, width), hidden // width
    forwards, attentions = [1, 2], [1, 2]
    residual = [None] * images
    exchanges, outs = {}, {}

    def begin(name, pair, strides):
        line.passed(pair[0])
        exchanges[name] = Exchange(line, *pair, strides, total)

    def feed_forward():
        nonlocal made, output, sums
        image = forwards.pop(0)
        made, output, sums, residual[image] = late_feed_forward(
            image, (0, 1) if image == 1 else (2,), saved, made, output, sums, keep_count, line.gate(returned[image]),
            vectors, weights,
        )
        line.passed(residual[image])

    def attention():
        nonlocal made, sums
        image = attentions.pop(0)
        made, sums = late_attention(
            image, saved, made, sums, line.gate(residual[image]), keep_count, keep_index, vectors, weights
        )
        line.passed(sums)

    def grad_down():
        pair = down_gradient(side, keep_count, line.gate(saved[SAVED.index(M)]), rows_in, returned)
        begin(DOWN, pair, near_first)

    def grad_up():
        blocks = [(0, 1, column) for column in range(many)]
        begin(UP, weight_gradient(side, (line.gate(flat(C)), flat(GZ)), blocks, "grad_up"), far_first)

    def grad_query_value():
        exchanges[SUMS] = Total(line, sums, near_first)
        pair = weight_gradient(side, (line.gate(flat(A)), flat(GQKV)), [(0, 1, 0), (0, 1, 2)], "grad_query_value")
        begin(QUERY_VALUE, pair, near_first)

    def grad_key_out():
        arrays = (line.gate(flat(A)), flat(GQKV), flat(O), flat(GB))
        pair = weight_gradient(side, arrays, [(0, 1, 1), (2, 3, 0)], "grad_key_out")
        begin(KEY_OUT, pair, near_first)

    def widen(name):
        places, kinds = {
            DOWN: ([(0, k, 0) for k in range(many)], {DOWN: (hidden, width)}),
            UP: ([(0, 0, k) for k in range(many)], {UP: (width, hidden)}),
            QUERY_VALUE: ([(0, 0, 0), (0, 1, 0), (0, 0, 2), (0, 1, 2)], {QKV: (width, 3 * width)}),
            KEY_OUT: ([(0, 0, 1), (0, 1, 1), (1, 0, 0), (1, 1, 0)], {QKV: (width, 3 * width), OUT: (width, width)}),
        }[name]
        exchange = exchanges[name]
        before = [outs[kind] for kind in kinds if kind in outs]
        first, second = exchange.half
        wholes = assembled(
            exchange.at == stages - 1,
            exchange.strides[0],
            (first, line.gate(second)),
            places,
            list(kinds.values()),
            before,
        )
        line.passed(wholes[0])
        outs.update(zip(kinds, wholes))

    steps = dict(zip("FAGUQK", (feed_forward, attention, grad_down, grad_up, grad_query_value, grad_key_out)))
    transfers = dict(zip("duqks", (DOWN, UP, QUERY_VALUE, KEY_OUT, SUMS)))
    stages = 2 * len(near_first) + 2
    plain = "FAFAGUQK" + "duqk" * stages + "s" * (stages // 2)
    for step in ORDER if (images, stages) == (3, 8) else plain:
        if step in steps:
            steps[step]()
            continue
        name = transfers[step]
        exchanges[name].advance()
        if name != SUMS and exchanges[name].half is not None:
            widen(name)
    assert all(exchange.at == (stages // 2 if name == SUMS else stages) for name, exchange in exchanges.items())
    sums = exchanges[SUMS].value / total
    small = [sums[at : at + 1] for at in VECTORS[:-1]]
    return (
        output[None],
        made[MADE.index(GRAD)][None],
        small[GAIN_ONE],
        small[SHIFT_ONE],
        outs[QKV][None],
        small[BIAS_QUERY],
        small[BIAS_VALUE],
        outs[OUT][None],
        small[BIAS_OUT],
        small[GAIN_TWO],
        small[SHIFT_TWO],
        outs[UP][None],
        sums[BIAS_UP : BIAS_UP + many].reshape(1, -1),
        outs[DOWN][None],
        small[BIAS_DOWN],
    )


def solution(mesh):
    per_image = (DP, REP)
    matrix, line = P(SECTION, None, None), P(SECTION, None)
    rows = P(SECTION, per_image, None, None)
    kinds = (line, line, matrix, line, line, matrix, line, line, line, matrix, line, matrix, line)
    return jax.shard_map(
        shards,
        mesh=mesh,
        in_specs=(rows, P(per_image, None), P(per_image)) + kinds,
        out_specs=(rows, rows) + kinds,
        check_vma=False,
    )
```

```python
import functools
from functools import partial
import math

import jax
import jax.numpy as jnp
from jax import lax
from jax.experimental import pallas as pl
from jax.experimental.pallas import tpu as pltpu
from jax.sharding import PartitionSpec as P

HEAD_DIM = 64
PAIR = 2 * HEAD_DIM
ROW_TILE = 16
COLUMNS = 256

norm_eps = 1e-06
masked_score = -1e30
f32 = jnp.float32
bf16 = jnp.bfloat16

NN = (((1,), (0,)), ((), ()))
NT = (((1,), (1,)), ((), ()))
TN = (((0,), (0,)), ((), ()))

VECTORS = range(9)
GAIN_ONE, SHIFT_ONE, BIAS_QUERY, BIAS_VALUE, BIAS_OUT, GAIN_TWO, SHIFT_TWO, BIAS_DOWN, BIAS_UP = VECTORS
SECTION, DP, REP = "section", "dp", "rep"
U, A, QKV, O, R, C, M, SLOPE, GD, GZ, GB, GR, GO, GQKV, GA, GU, E, Y, GRAD = range(19)
WEIGHTS = range(19, 23)
W_QKV, W_OUT, W_UP, W_DOWN = WEIGHTS
DOWN, UP, QUERY_VALUE, KEY_OUT, SUMS, OUT = range(100, 106)
ORDER = "FAGFUduAQdKudqukdqsukqdskuqdkqkuqsdksdquqkuk"
COST = 10**11
LATE_COST = 10**10
ANY = pl.BlockSpec(memory_space=pl.ANY)


def product(left, right, dims):
    return lax.dot_general(left, right, dims, preferred_element_type=f32)


def spans(size, step):
    return [slice(at, min(at + step, size)) for at in range(0, size, step)]


def column_sum(values):
    return jnp.sum(values, axis=0, keepdims=True)


def centre(values):
    centred = values - jnp.mean(values, axis=-1, keepdims=True)
    scale = lax.rsqrt(jnp.mean(centred * centred, axis=-1, keepdims=True) + norm_eps)
    return centred * scale, scale


class Copies:
    def __init__(self, sem, pairs):
        self.made = {
            name: pltpu.make_async_copy(source, target, sem.at[at])
            for at, (name, (source, target)) in enumerate(pairs.items())
        }

    def start(self, *names):
        for name in names or tuple(self.made):
            if name in self.made:
                self.made[name].start()

    def wait(self, *names):
        for name in names or tuple(self.made):
            if name in self.made:
                self.made.pop(name).wait()


def first_section():
    return lax.axis_index(SECTION) == 0


def row_mask(shape, count):
    return lax.broadcasted_iota(jnp.int32, shape, 0) < count


def gather_matrix(slots_of, count):
    slots = slots_of.shape[1]
    shape = (-(-slots // ROW_TILE) * ROW_TILE, slots)
    patch = lax.broadcasted_iota(jnp.int32, shape, 0)
    slot = lax.broadcasted_iota(jnp.int32, shape, 1)
    chosen = jnp.broadcast_to(slots_of, shape) == patch
    return jnp.where(chosen & (slot < count), 1.0, 0.0).astype(bf16)


def forward_part(r, wait, done, vec, weights, count):
    rows, width = r[U].shape[-2:]
    hidden = weights[W_UP].shape[1]
    for span in spans(rows, ROW_TILE):
        normal, _ = centre(r[U][span, :].astype(f32))
        r[A][span, :] = (normal * vec(GAIN_ONE) + vec(SHIFT_ONE)).astype(bf16)
    done(U, A)
    wait(W_QKV)
    for span in spans(3 * width, COLUMNS):
        packed = product(r[A][...], weights[W_QKV][:, span], NN)
        if span.start < width:
            packed = packed + vec(BIAS_QUERY, span)
        elif span.start >= 2 * width:
            packed = packed + vec(BIAS_VALUE, slice(span.start - 2 * width, span.stop - 2 * width))
        r[QKV][:, span] = packed.astype(bf16)
    done(QKV)
    low = (lax.broadcasted_iota(jnp.int32, (1, PAIR), 1) < HEAD_DIM).astype(bf16)
    lane = lax.broadcasted_iota(jnp.int32, (rows, PAIR), 1) < HEAD_DIM
    for at in range(0, width, PAIR):
        query = r[QKV][:, at : at + PAIR]
        key = r[QKV][:, width + at : width + at + PAIR]
        value = r[QKV][:, 2 * width + at : 2 * width + at + PAIR]
        both = jnp.concatenate([query * low, query * (1 - low)], axis=0)
        scores = product(both, key, NT) * (1.0 / math.sqrt(HEAD_DIM))
        live = lax.broadcasted_iota(jnp.int32, scores.shape, 1) < count
        scores = jnp.where(live, scores, masked_score)
        powers = jnp.exp(scores - jnp.max(scores, axis=-1, keepdims=True))
        chance = powers * (1.0 / jnp.sum(powers, axis=-1, keepdims=True))
        mixed = product(chance.astype(bf16), value, NN)
        r[O][:, at : at + PAIR] = jnp.where(lane, mixed[:rows], mixed[rows:]).astype(bf16)
    done(O)
    wait(W_OUT)
    for span in spans(width, COLUMNS):
        r[R][:, span] = r[U][:, span].astype(f32) + (
            product(r[O][...], weights[W_OUT][:, span], NN) + vec(BIAS_OUT, span)
        )
    for span in spans(rows, ROW_TILE):
        normal, _ = centre(r[R][span, :])
        r[C][span, :] = (normal * vec(GAIN_TWO) + vec(SHIFT_TWO)).astype(bf16)
    done(R, C)
    wait(W_UP)
    for span in spans(hidden, COLUMNS):
        z = product(r[C][...], weights[W_UP][:, span], NN) + vec(BIAS_UP, span)
        share = 0.5 * (1.0 + lax.erf(z * math.sqrt(0.5)))
        r[M][:, span] = (z * share).astype(bf16)
        r[SLOPE][:, span] = share + z * (jnp.exp(-0.5 * z * z) * (1.0 / math.sqrt(2 * math.pi)))
    done(M, SLOPE)


def output_part(r, vec, weights, count):
    rows, width = r[R].shape
    outer = r[Y].shape[0]
    for span in spans(width, COLUMNS):
        y = r[R][:, span] + (product(r[M][...], weights[W_DOWN][:, span], NN) + vec(BIAS_DOWN, span))
        r[Y][:, span] = jnp.where(row_mask(y.shape, count), y, 0.0).astype(bf16)[:outer]


def norm_back(normal, scale, gain, grad):
    x = grad * gain
    return scale * (
        x - jnp.mean(x, axis=-1, keepdims=True) - normal * jnp.mean(x * normal, axis=-1, keepdims=True)
    )


def feed_forward_back(r, wait, done, vec, weights, count, add):
    rows, width = r[R].shape
    hidden = weights[W_UP].shape[1]
    for span in spans(rows, ROW_TILE):
        live = lax.broadcasted_iota(jnp.int32, (ROW_TILE, width), 0) + span.start < count
        r[GD][span, :] = jnp.where(live, r[E][span, :], jnp.zeros((), bf16))
    add(BIAS_DOWN, lambda: column_sum(r[GD][...].astype(f32)))
    wait(W_DOWN, SLOPE)
    for span in spans(hidden, COLUMNS):
        gz = product(r[GD][...], weights[W_DOWN][span, :], NT) * r[SLOPE][:, span]
        r[GZ][:, span] = gz.astype(bf16)
        add(BIAS_UP, lambda: column_sum(r[GZ][:, span].astype(f32)), span)
    done(GZ)
    wait(W_UP, R)
    for span in spans(width, COLUMNS):
        r[GR][:, span] = product(r[GZ][...], weights[W_UP][span, :], NT)
    gain_sum, shift_sum = 0.0, 0.0
    for span in spans(rows, ROW_TILE):
        normal, scale = centre(r[R][span, :])
        gc = r[GR][span, :]
        gain_sum, shift_sum = gain_sum + gc * normal, shift_sum + gc
        gr = r[GD][span, :].astype(f32) + norm_back(normal, scale, vec(GAIN_TWO), gc)
        r[GR][span, :] = gr
        r[GB][span, :] = gr.astype(bf16)
    done(GB, GR)
    add(GAIN_TWO, lambda: column_sum(gain_sum))
    add(SHIFT_TWO, lambda: column_sum(shift_sum))
    add(BIAS_OUT, lambda: column_sum(r[GB][...].astype(f32)))


def attention_back(r, wait, done, vec, weights, count, add):
    rows, width = r[U].shape
    wait(GB, W_OUT)
    for span in spans(width, COLUMNS):
        r[GO][:, span] = product(r[GB][...], weights[W_OUT][span, :], NT).astype(bf16)
    wait(QKV)
    low = (lax.broadcasted_iota(jnp.int32, (1, PAIR), 1) < HEAD_DIM).astype(bf16)
    lane = lax.broadcasted_iota(jnp.int32, (rows, PAIR), 1) < HEAD_DIM
    score_scale = 1.0 / math.sqrt(HEAD_DIM)
    live = row_mask((rows, rows), count)
    for at in range(0, width, PAIR):
        query = r[QKV][:, at : at + PAIR]
        key = r[QKV][:, width + at : width + at + PAIR]
        value = r[QKV][:, 2 * width + at : 2 * width + at + PAIR]
        go = r[GO][:, at : at + PAIR]
        scores = product(jnp.concatenate([key * low, key * (1 - low)], axis=0), query, NT) * score_scale
        grads = product(jnp.concatenate([value * low, value * (1 - low)], axis=0), go, NT)
        chances, inner = [], []
        for head in range(2):
            score = jnp.where(live, scores[head * rows : (head + 1) * rows], masked_score)
            powers = jnp.exp(score - jnp.max(score, axis=0, keepdims=True))
            chance = powers * (1.0 / jnp.sum(powers, axis=0, keepdims=True))
            gp = grads[head * rows : (head + 1) * rows]
            gs = chance * (gp - jnp.sum(gp * chance, axis=0, keepdims=True))
            chances.append(chance.astype(bf16))
            inner.append(jnp.where(live, gs, 0.0).astype(bf16))
        gw = product(jnp.concatenate(chances, axis=0), go, NN)
        gk = product(jnp.concatenate(inner, axis=0), query, NN) * score_scale
        gq = [product(gs, key, TN) * score_scale for gs in inner]
        r[GQKV][:, at : at + PAIR] = jnp.where(lane, gq[0], gq[1]).astype(bf16)
        r[GQKV][:, width + at : width + at + PAIR] = jnp.where(lane, gk[:rows], gk[rows:]).astype(bf16)
        r[GQKV][:, 2 * width + at : 2 * width + at + PAIR] = jnp.where(lane, gw[:rows], gw[rows:]).astype(
            bf16
        )
    done(GQKV)
    add(BIAS_QUERY, lambda: column_sum(r[GQKV][:, :width].astype(f32)))
    add(BIAS_VALUE, lambda: column_sum(r[GQKV][:, 2 * width :].astype(f32)))
    wait(W_QKV, U, GR)
    for span in spans(width, COLUMNS):
        r[GA][:, span] = product(r[GQKV][...], weights[W_QKV][span, :], NT)
    gain_sum, shift_sum = 0.0, 0.0
    for span in spans(rows, ROW_TILE):
        normal, scale = centre(r[U][span, :].astype(f32))
        ga = r[GA][span, :]
        gain_sum, shift_sum = gain_sum + ga * normal, shift_sum + ga
        gu = r[GR][span, :] + norm_back(normal, scale, vec(GAIN_ONE), ga)
        r[GU][span, :] = gu.astype(bf16)
    add(GAIN_ONE, lambda: column_sum(gain_sum))
    add(SHIFT_ONE, lambda: column_sum(shift_sum))


def vector_reader(refs):
    named = dict(zip(VECTORS, refs))

    def vec(name, span=None):
        ref = named[name]
        return (ref[...] if span is None else ref[:, span]).astype(f32)

    return vec


def vector_adder(ref):
    def add(name, values, span=None):
        values = values()
        start = 0 if span is None else span.start
        row, start = VECTORS.index(name) + start // ref.shape[1], start % ref.shape[1]
        ref[row : row + 1, start : start + values.shape[1]] += values

    return add


def pad_rows(target, source):
    inner, rows = source.shape[0], target.shape[0]
    target[:inner, :] = source[...]
    if rows > inner:
        target[inner:, :] = jnp.zeros((rows - inner, target.shape[1]), target.dtype)


def padded_rows(slots):
    return -(-slots // ROW_TILE) * ROW_TILE


def image_block(shape, image):
    return pl.BlockSpec((pl.Squeezed(),) + tuple(shape), lambda *_: (image, 0, 0))


def fixed_block(shape):
    return pl.BlockSpec(tuple(shape), lambda *_: (0,) * len(shape))


def weight_scratch(weights):
    return [pltpu.VMEM(weight.shape, weight.dtype) for weight in weights] + [
        pltpu.SemaphoreType.DMA((len(weights),))
    ]


def fetch_weights(sem, hbm, local, order=WEIGHTS):
    found = dict(zip(WEIGHTS, zip(hbm, local)))
    return Copies(sem, {name: found[name] for name in order}), dict(zip(WEIGHTS, local))


def call(kernel, steps, scalars, ins, in_specs, outs, out_specs, scratch, name, aliases=None, room=60):
    return pl.pallas_call(
        kernel,
        out_shape=outs,
        grid_spec=pltpu.PrefetchScalarGridSpec(
            num_scalar_prefetch=1,
            grid=(steps,),
            in_specs=in_specs,
            out_specs=out_specs,
            scratch_shapes=scratch,
        ),
        compiler_params=pltpu.CompilerParams(
            dimension_semantics=("arbitrary",), vmem_limit_bytes=room << 20
        ),
        input_output_aliases=aliases or {},
        cost_estimate=pl.CostEstimate(flops=COST, bytes_accessed=COST, transcendentals=0),
        name=name,
    )(scalars, *ins)


def split(refs, *sizes):
    out, at = [], 0
    for size in sizes:
        out.append(refs[at] if size is None else refs[at : at + size])
        at += 1 if size is None else size
    assert at == len(refs)
    return out


def nothing(*_):
    return None


SAVED = (U, A, QKV, O, R, C, M, SLOPE)
MADE = (GZ, GB, GQKV, GRAD)


def image_shapes(slots, rows, width, hidden):
    narrow, wide = (rows, width), (rows, hidden)
    return {
        U: (narrow, bf16),
        A: (narrow, bf16),
        QKV: ((rows, 3 * width), bf16),
        O: (narrow, bf16),
        R: (narrow, f32),
        C: (narrow, bf16),
        M: (wide, bf16),
        SLOPE: (wide, f32),
        GD: (narrow, bf16),
        GZ: (wide, bf16),
        GB: (narrow, bf16),
        GR: (narrow, f32),
        GO: (narrow, bf16),
        GQKV: ((rows, 3 * width), bf16),
        GA: (narrow, f32),
        GU: (narrow, bf16),
        E: (narrow, bf16),
        Y: ((slots, width), bf16),
        GRAD: ((slots, width), bf16),
    }


def first_forward(image, carry, count, index, source, vectors, weights):
    images, slots, width = source.shape
    rows, hidden = padded_rows(slots), weights[2].shape[1]
    shapes = image_shapes(slots, rows, width, hidden)
    work = SAVED + (Y,)
    old = () if carry is None else tuple(carry)
    at = 1 + 2 + len(vectors) + 4

    def kernel(count_ref, index_ref, source_ref, *rest):
        vecs, hbm, _, places, y_ref, local, sem, scratch, padded, out_sem = split(
            rest, len(vectors), 4, len(old), len(work), None, 4, None, len(work), None, None
        )

        @pl.when(first_section())
        def _():
            fetch, near = fetch_weights(sem, hbm, local)
            fetch.start()
            kept = count_ref[image]
            refs = dict(zip(work, scratch))
            store = Copies(out_sem, {name: (refs[name], place.at[image]) for name, place in zip(work, places)})
            pad_rows(padded, source_ref)
            chosen = gather_matrix(index_ref[image : image + 1, :], kept)
            refs[U][:slots, :] = product(chosen, padded[...], TN).astype(bf16)
            refs[U][slots:, :] = jnp.zeros((rows - slots, width), bf16)
            vec = vector_reader(vecs)
            forward_part(refs, fetch.wait, store.start, vec, near, kept)
            fetch.wait(W_DOWN)
            output_part(refs, vec, near, kept)
            store.start(Y)
            y_ref[...] = refs[Y][...]
            store.wait()

    *carry, output = call(
        kernel,
        1,
        count,
        (index, source) + vectors + weights + old,
        [fixed_block(index.shape), image_block((slots, width), image)]
        + [fixed_block(vector.shape) for vector in vectors]
        + [ANY] * (4 + len(old)),
        [jax.ShapeDtypeStruct((images,) + shapes[name][0], shapes[name][1]) for name in work]
        + [jax.ShapeDtypeStruct((1, slots, width), bf16)],
        [ANY] * len(work) + [image_block((slots, width), 0)],
        weight_scratch(weights)
        + [pltpu.VMEM(*shapes[name]) for name in work]
        + [pltpu.VMEM((rows, width), bf16), pltpu.SemaphoreType.DMA((len(work),))],
        f"first_forward_{image}",
        {at + k: k for k in range(len(old))},
    )
    return carry, output


def tick(first, image, late, saved, made, output, sums, scalars, index, received, source, vectors, weights):
    images, slots, width = source.shape
    rows, hidden = padded_rows(slots), weights[2].shape[1]
    shapes = image_shapes(slots, rows, width, hidden)
    carry = SAVED + MADE + (Y,)
    lines = -(-(len(vectors) - 1 + hidden // width) // 8) * 8
    work = (E, GD, GR, GO, GA, GU) + carry
    old = tuple(saved) + (() if made is None else tuple(made)) + (output,) + (() if made is None else (sums,))
    slots_of = [k for k, name in enumerate(carry) if made is not None or name not in MADE]
    slots_of += [] if made is None else [len(carry)]
    at = 1 + 3 + len(vectors) + 4
    other = first if first is not None else late if late is not None else image

    def kernel(scalar_ref, index_ref, received_ref, source_ref, *rest):
        vecs, hbm, previous, places, sums_ref, send_ref, local, sem, scratch, out_sem = split(
            rest, len(vectors), 4, len(old), len(carry), None, None, 4, None, len(work), None
        )
        sums_ref[...] = jnp.zeros(sums_ref.shape, f32) if made is None else previous[-1][...]
        early = first_section()
        later = jnp.logical_not(early)
        here = jnp.where(early, other, image)
        live = scalar_ref[here]
        refs = dict(zip(work, scratch))
        place = {name: ref.at[here] for name, ref in zip(carry, places)}
        store = Copies(out_sem, {name: (refs[name], place[name]) for name in carry})
        vec, add = vector_reader(vecs), vector_adder(sums_ref)

        def gathered():
            pad_rows(refs[E], source_ref)
            chosen = gather_matrix(index_ref[first : first + 1, :], live)
            refs[U][:slots, :] = product(chosen, refs[E][...], TN).astype(bf16)
            refs[U][slots:, :] = jnp.zeros((rows - slots, width), bf16)

        def forward(fetch, near):
            forward_part(refs, fetch.wait, store.start, vec, near, live)
            fetch.wait(W_DOWN)

        def backward(near, wait=nothing):
            feed_forward_back(refs, wait, store.start, vec, near, live, add)
            attention_back(refs, wait, store.start, vec, near, live, add)

        def fetched():
            weights_in = fetch_weights(sem, hbm, local, (W_DOWN, W_UP, W_OUT, W_QKV))[0]
            return weights_in, Copies(out_sem, {name: (place[name], refs[name]) for name in (SLOPE, R, QKV, U)})

        def await_early(*names):
            @pl.when(early)
            def _():
                for copies in fetched():
                    copies.wait(*names)

        def sent():
            refs[GRAD][...] = refs[GU][:slots, :]
            store.start(GRAD)
            send_ref[...] = refs[GU][:slots, :]

        if first is not None:
            fetch, near = fetch_weights(sem, hbm, local)
            fetch.start()

            @pl.when(early)
            def _():
                gathered()

            @pl.when(later)
            def _():
                pad_rows(refs[U], received_ref.at[0])

            forward(fetch, near)

            @pl.when(early)
            def _():
                output_part(refs, vec, near, live)
                store.start(Y)
                send_ref[...] = refs[Y][...]
                Copies(out_sem, {name: (refs[name], place[name]) for name in carry}).wait(*SAVED, Y)

            @pl.when(later)
            def _():
                pad_rows(refs[E], source_ref)
                backward(near)
                sent()
                Copies(out_sem, {name: (refs[name], place[name]) for name in carry}).wait(*SAVED, *MADE)

            return

        @pl.when(later)
        def _():
            fetch, near = fetch_weights(sem, hbm, local)
            fetch.start()
            pad_rows(refs[U], received_ref.at[0])
            pad_rows(refs[E], source_ref)
            forward(fetch, near)
            if late is None:
                backward(near)
                sent()
                store.wait(*SAVED, *MADE)

        if late is None:
            return

        @pl.when(early)
        def _():
            for copies in fetched():
                copies.start()
            pad_rows(refs[E], received_ref.at[0])

        backward(dict(zip(WEIGHTS, local)), await_early)

        @pl.when(early)
        def _():
            chosen = gather_matrix(index_ref[late : late + 1, :], live)
            refs[GRAD][...] = product(chosen, refs[GU][:slots, :], NN)[:slots, :].astype(bf16)
            store.start(GRAD)

        @pl.when(later)
        def _():
            sent()
            Copies(out_sem, {name: (refs[name], place[name]) for name in SAVED}).wait()

        store.wait(*MADE)

    results = call(
        kernel,
        1,
        scalars,
        (index, received, source) + vectors + weights + old,
        [
            fixed_block(index.shape),
            pl.BlockSpec(memory_space=pltpu.VMEM),
            pl.BlockSpec(
                (pl.Squeezed(), slots, width), lambda i, s: (jnp.where(s[images] == 0, other, image), 0, 0)
            ),
        ]
        + [fixed_block(vector.shape) for vector in vectors]
        + [ANY] * (4 + len(old) - (made is not None))
        + ([] if made is None else [fixed_block(sums.shape)]),
        [jax.ShapeDtypeStruct((images,) + shapes[name][0], shapes[name][1]) for name in carry]
        + [jax.ShapeDtypeStruct((lines, width), f32), jax.ShapeDtypeStruct((1, slots, width), bf16)],
        [ANY] * len(carry) + [fixed_block((lines, width)), image_block((slots, width), 0)],
        weight_scratch(weights)
        + [pltpu.VMEM(*shapes[name]) for name in work]
        + [pltpu.SemaphoreType.DMA((len(carry),))],
        f"tick_{image}",
        {at + k: slot for k, slot in enumerate(slots_of)},
    )
    saved, made = results[: len(SAVED)], results[len(SAVED) : len(SAVED) + len(MADE)]
    return saved, made, results[-3], results[-2], results[-1]


def late_feed_forward(image, outputs, saved, made, output, sums, count, received, vectors, weights):
    images, rows, hidden = saved[SAVED.index(M)].shape
    slots, width = received.shape[1:]
    shapes = image_shapes(slots, rows, width, hidden)
    loads = (SLOPE, R, M)
    stores = (GZ, GB, Y)
    work = (SLOPE, R, M, E, GD, GZ, GB, Y)
    near_names = (W_DOWN, W_UP)
    old = [made[MADE.index(GZ)], made[MADE.index(GB)], output, sums]
    at = 1 + 1 + len(vectors) + len(loads) + len(near_names)

    def kernel(count_ref, received_ref, *rest):
        vecs, sources, hbm, previous, places, sums_ref, gr_ref, local, scratch, sem = split(
            rest, len(vectors), len(loads), 2, len(old), len(stores), None, None, 2, len(work), None
        )
        live = count_ref[image]
        refs = dict(zip(work, scratch)) | {GR: gr_ref}
        near = dict(zip(near_names, local))
        far = dict(zip(near_names, hbm))
        source = {name: ref.at[image] for name, ref in zip(loads, sources)}
        place = {name: ref.at[image] for name, ref in zip(stores, places)}
        vec = vector_reader(vecs)
        sums_ref[...] = previous[-1][...]
        early = first_section()

        @pl.when(early)
        def _():
            fetch = Copies(
                sem,
                {
                    W_DOWN: (far[W_DOWN], near[W_DOWN]),
                    SLOPE: (source[SLOPE], refs[SLOPE]),
                    W_UP: (far[W_UP], near[W_UP]),
                    R: (source[R], refs[R]),
                },
            )
            fetch.start()
            store = Copies(sem.at[pl.ds(5, 2)], {name: (refs[name], place[name]) for name in (GZ, GB)})
            pad_rows(refs[E], received_ref.at[0])
            feed_forward_back(refs, fetch.wait, store.start, vec, near, live, vector_adder(sums_ref))
            store.wait()

        @pl.when(jnp.logical_not(early))
        def _():
            fetch = Copies(sem, {W_DOWN: (far[W_DOWN], near[W_DOWN])})
            fetch.start()
            for which in outputs:
                load = Copies(
                    sem.at[pl.ds(1, 2)],
                    {name: (sources[loads.index(name)].at[which], refs[name]) for name in (R, M)},
                )
                load.start()
                fetch.wait()
                load.wait()
                output_part(refs, vec, near, count_ref[which])
                store = Copies(sem.at[pl.ds(4, 1)], {Y: (refs[Y], places[stores.index(Y)].at[which])})
                store.start()
                store.wait()

    gz, gb, output, sums, gr = call(
        kernel,
        1,
        count,
        (received,)
        + vectors
        + tuple(saved[SAVED.index(name)] for name in loads)
        + tuple(weights[WEIGHTS.index(name)] for name in near_names)
        + tuple(old),
        [pl.BlockSpec(memory_space=pltpu.VMEM)]
        + [fixed_block(vector.shape) for vector in vectors]
        + [ANY] * (len(loads) + len(near_names) + len(old) - 1)
        + [fixed_block(sums.shape)],
        [
            jax.ShapeDtypeStruct((images,) + shapes[GZ][0], bf16),
            jax.ShapeDtypeStruct((images,) + shapes[GB][0], bf16),
            jax.ShapeDtypeStruct((images,) + shapes[Y][0], bf16),
            jax.ShapeDtypeStruct(sums.shape, f32),
            jax.ShapeDtypeStruct((1,) + shapes[GR][0], f32),
        ],
        [ANY] * 3 + [fixed_block(sums.shape), image_block(shapes[GR][0], 0)],
        [pltpu.VMEM(weights[WEIGHTS.index(name)].shape, bf16) for name in near_names]
        + [pltpu.VMEM(*shapes[name]) for name in work]
        + [pltpu.SemaphoreType.DMA((7,))],
        f"late_feed_forward_{image}",
        {at + k: k for k in range(len(old))},
    )
    return [gz, gb] + list(made[2:]), output, sums, gr


def late_attention(image, saved, made, sums, gr, count, index, vectors, weights):
    images, slots, width = made[MADE.index(GRAD)].shape
    rows, hidden = saved[SAVED.index(M)].shape[1:]
    shapes = image_shapes(slots, rows, width, hidden)
    work = (GB, QKV, U, GO, GQKV, GA, GU, GRAD)
    near_names = (W_OUT, W_QKV)
    old = [made[MADE.index(GQKV)], made[MADE.index(GRAD)], sums]
    sources = (made[MADE.index(GB)], saved[SAVED.index(QKV)], saved[SAVED.index(U)])
    at = 1 + 2 + len(vectors) + len(sources) + len(near_names)

    def kernel(count_ref, index_ref, gr_ref, *rest):
        vecs, loads, hbm, previous, gqkv_ref, grad_ref, sums_ref, local, scratch, sem = split(
            rest, len(vectors), len(sources), 2, len(old), None, None, None, 2, len(work), None
        )
        live = count_ref[image]
        sums_ref[...] = previous[-1][...]
        refs = dict(zip(work, scratch)) | {GR: gr_ref}
        near = dict(zip(near_names, local))

        @pl.when(first_section())
        def _():
            fetch = Copies(
                sem,
                {
                    GB: (loads[0].at[image], refs[GB]),
                    W_OUT: (hbm[0], near[W_OUT]),
                    QKV: (loads[1].at[image], refs[QKV]),
                    W_QKV: (hbm[1], near[W_QKV]),
                    U: (loads[2].at[image], refs[U]),
                },
            )
            fetch.start()
            store = Copies(
                sem.at[pl.ds(5, 2)],
                {GQKV: (refs[GQKV], gqkv_ref.at[image]), GRAD: (refs[GRAD], grad_ref.at[image])},
            )
            attention_back(refs, fetch.wait, store.start, vector_reader(vecs), near, live, vector_adder(sums_ref))
            chosen = gather_matrix(index_ref[image : image + 1, :], live)
            refs[GRAD][...] = product(chosen, refs[GU][:slots, :], NN)[:slots, :].astype(bf16)
            store.start(GRAD)
            store.wait()

    gqkv, grad, sums = call(
        kernel,
        1,
        count,
        (index, gr)
        + vectors
        + sources
        + tuple(weights[WEIGHTS.index(name)] for name in near_names)
        + tuple(old),
        [fixed_block(index.shape), image_block((rows, width), 0)]
        + [fixed_block(vector.shape) for vector in vectors]
        + [ANY] * (len(sources) + len(near_names) + len(old) - 1)
        + [fixed_block(sums.shape)],
        [
            jax.ShapeDtypeStruct((images,) + shapes[GQKV][0], bf16),
            jax.ShapeDtypeStruct((images,) + shapes[GRAD][0], bf16),
            jax.ShapeDtypeStruct(sums.shape, f32),
        ],
        [ANY] * 2 + [fixed_block(sums.shape)],
        [pltpu.VMEM(weights[WEIGHTS.index(name)].shape, bf16) for name in near_names]
        + [pltpu.VMEM(*shapes[name]) for name in work]
        + [pltpu.SemaphoreType.DMA((7,))],
        f"late_attention_{image}",
        {at + k: k for k in range(len(old))},
    )
    return list(made[:2]) + [gqkv, grad], sums


def pick(table, at):
    value = table[0]
    for k in range(1, len(table)):
        value = jnp.where(at == k, table[k], value)
    return value


def weight_gradient(side, arrays, blocks, name):
    depth = arrays[0].shape[0]
    width = min(array.shape[1] for array in arrays)
    half = len(blocks) // 2

    def chosen(i, scalar_ref):
        bit = scalar_ref[0]
        return jnp.where(i < half, (1 - bit) * half + i, bit * half + i - half)

    def kernel(scalar_ref, *refs):
        send_ref, keep_ref = refs[-2:]
        step = pl.program_id(0)
        block = chosen(step, scalar_ref)
        for left, right in dict.fromkeys((left, right) for left, right, _ in blocks):
            here = functools.reduce(
                jnp.logical_or, [block == k for k, entry in enumerate(blocks) if entry[:2] == (left, right)]
            )

            @pl.when(here & (step < half))
            def _():
                send_ref[...] = product(refs[left][...], refs[right][...], TN).astype(bf16)

            @pl.when(here & (step >= half))
            def _():
                keep_ref[...] = product(refs[left][...], refs[right][...], TN).astype(bf16)

    def columns(at):
        table = [column if right == at else 0 for _, right, column in blocks]
        return pl.BlockSpec((depth, width), lambda i, s: (0, pick(table, chosen(i, s))))

    return call(
        kernel,
        2 * half,
        side,
        arrays,
        [columns(at) for at in range(len(arrays))],
        [jax.ShapeDtypeStruct((half * width, width), bf16)] * 2,
        [
            pl.BlockSpec((width, width), lambda i, s: (jnp.minimum(i, half - 1), 0)),
            pl.BlockSpec((width, width), lambda i, s: (jnp.maximum(i - half, 0), 0)),
        ],
        [],
        name,
        room=60,
    )


def down_gradient(side, count, m, cotangent, received):
    images, slots, width = cotangent.shape
    rows, hidden = m.shape[1:]
    blocks = hidden // width
    half = blocks // 2
    scalars = jnp.concatenate([side, count])

    def chosen(i, scalar_ref):
        bit = scalar_ref[0]
        return jnp.where(i < half, (1 - bit) * half + i, bit * half + i - half)

    def kernel(scalar_ref, m_ref, e_ref, *rest):
        arrived, (send_ref, keep_ref, gd_ref) = rest[:images], rest[images:]
        step = pl.program_id(0)
        early = first_section()

        @pl.when(step == 0)
        def _():
            for image in range(images):
                live = row_mask((slots, width), scalar_ref[1 + image])
                top = slice(image * rows, image * rows + slots)
                gd_ref[top, :] = jnp.where(live, jnp.where(early, arrived[image][...], e_ref[image]), jnp.zeros((), bf16))
                gd_ref[top.stop : (image + 1) * rows, :] = jnp.zeros((rows - slots, width), bf16)

        left = m_ref[...].reshape(images * rows, width)

        @pl.when(step < half)
        def _():
            send_ref[...] = product(left, gd_ref[...], TN).astype(bf16)

        @pl.when(step >= half)
        def _():
            keep_ref[...] = product(left, gd_ref[...], TN).astype(bf16)

    return call(
        kernel,
        blocks,
        scalars,
        (m, cotangent) + tuple(received),
        [
            pl.BlockSpec((images, rows, width), lambda i, s: (0, 0, chosen(i, s))),
            fixed_block(cotangent.shape),
        ]
        + [image_block((slots, width), 0)] * images,
        [jax.ShapeDtypeStruct((half * width, width), bf16)] * 2,
        [
            pl.BlockSpec((width, width), lambda i, s: (jnp.minimum(i, half - 1), 0)),
            pl.BlockSpec((width, width), lambda i, s: (jnp.maximum(i - half, 0), 0)),
        ],
        [pltpu.VMEM((images * rows, width), bf16)],
        "grad_down",
        room=60,
    )


def plain_call(kernel, ins, outs, scratch, name, out_specs=None):
    return pl.pallas_call(
        kernel,
        out_shape=outs,
        in_specs=[ANY] * len(ins),
        out_specs=out_specs or [pl.BlockSpec(memory_space=pltpu.VMEM)] * len(outs),
        scratch_shapes=scratch,
        compiler_params=pltpu.CompilerParams(vmem_limit_bytes=16 << 20),
        cost_estimate=pl.CostEstimate(flops=COST, bytes_accessed=COST, transcendentals=0),
        name=name,
    )(*ins)


def assembled(own, stride, pieces, places, shapes, before):
    shape = pieces[0].shape

    def kernel(*refs):
        sources, _, outs, (raw, wide, sem) = split(refs, 2, len(before), len(shapes), 3)
        core = lax.axis_index(REP) if own else 1 - lax.axis_index(REP)
        near = bit_of(DP, stride)
        loads = [pltpu.make_async_copy(source, raw.at[k], sem.at[k]) for k, source in enumerate(sources)]
        for load in loads:
            load.start()

        def stores(k, act):
            block = 2 * core + (near if k == 0 else 1 - near)
            for at, (which, row, column) in enumerate(places):
                rows, columns = pl.ds(row * shape[0], shape[0]), pl.ds(column * shape[1], shape[1])

                @pl.when(block == at)
                def _():
                    act(pltpu.make_async_copy(wide.at[k], outs[which].at[rows, columns], sem.at[2 + k]))

        for k in range(2):
            loads[k].wait()
            wide[k] = raw[k].astype(f32)
            stores(k, lambda copy: copy.start())
        for k in range(2):
            stores(k, lambda copy: copy.wait())

    return pl.pallas_call(
        kernel,
        out_shape=[jax.ShapeDtypeStruct(whole, f32) for whole in shapes],
        in_specs=[ANY] * (2 + len(before)),
        out_specs=[ANY] * len(shapes),
        scratch_shapes=[
            pltpu.VMEM((2,) + shape, bf16),
            pltpu.VMEM((2,) + shape, f32),
            pltpu.SemaphoreType.DMA((4,)),
        ],
        input_output_aliases={2 + k: k for k in range(len(before))},
        compiler_params=pltpu.CompilerParams(vmem_limit_bytes=16 << 20),
        cost_estimate=pl.CostEstimate(flops=LATE_COST, bytes_accessed=LATE_COST, transcendentals=0),
        name="assembled",
    )(*pieces, *before)


def in_vmem(value):
    return pltpu.with_memory_space_constraint(value, pltpu.VMEM)


def swapped(value, axis, stride):
    length = lax.axis_size(axis)
    return lax.ppermute(value, axis, [(i, i ^ stride) for i in range(length)])


def bit_of(axis, stride):
    return (lax.axis_index(axis) // stride) % 2


def halved(keep, coming, stride):
    height, width = keep.shape[0] // 2, keep.shape[1]
    if height % ROW_TILE:
        bit = bit_of(DP, stride)
        pair = (keep.astype(f32) + coming.astype(f32)).astype(bf16)
        send = lax.dynamic_slice_in_dim(pair, (1 - bit) * height, height, axis=0)
        return send, lax.dynamic_slice_in_dim(pair, bit * height, height, axis=0)

    def kernel(keep_ref, coming_ref, send_ref, stay_ref, kept, came, made, sem):
        bit = bit_of(DP, stride)
        copies = []
        for at, half in enumerate((1 - bit, bit)):
            rows = pl.ds(pl.multiple_of(half * height, ROW_TILE), height)
            copies.append(pltpu.make_async_copy(keep_ref.at[rows, :], kept.at[at], sem.at[2 * at]))
            copies.append(pltpu.make_async_copy(coming_ref.at[rows, :], came.at[at], sem.at[2 * at + 1]))
        for copy in copies:
            copy.start()
        for copy in copies[:2]:
            copy.wait()
        made[...] = (kept[0].astype(f32) + came[0].astype(f32)).astype(bf16)
        store = pltpu.make_async_copy(made, send_ref, sem.at[4])
        store.start()
        for copy in copies[2:]:
            copy.wait()
        stay_ref[...] = (kept[1].astype(f32) + came[1].astype(f32)).astype(bf16)
        store.wait()

    shape = (height, width)
    return plain_call(
        kernel,
        (keep, coming),
        [jax.ShapeDtypeStruct(shape, bf16)] * 2,
        [
            pltpu.VMEM((2,) + shape, bf16),
            pltpu.VMEM((2,) + shape, bf16),
            pltpu.VMEM(shape, bf16),
            pltpu.SemaphoreType.DMA((5,)),
        ],
        f"halved_{stride}",
        [ANY, pl.BlockSpec(memory_space=pltpu.VMEM)],
    )


def summed(keep, coming, total):
    if keep.shape[0] % ROW_TILE:
        return ((keep.astype(f32) + coming.astype(f32)) / total).astype(bf16)

    def kernel(keep_ref, coming_ref, out_ref, kept, came, sem):
        copies = [
            pltpu.make_async_copy(keep_ref, kept, sem.at[0]),
            pltpu.make_async_copy(coming_ref, came, sem.at[1]),
        ]
        for copy in copies:
            copy.start()
        for copy in copies:
            copy.wait()
        out_ref[...] = ((kept[...].astype(f32) + came[...].astype(f32)) / total).astype(bf16)

    return plain_call(
        kernel,
        (keep, coming),
        [jax.ShapeDtypeStruct(keep.shape, bf16)],
        [pltpu.VMEM(keep.shape, bf16), pltpu.VMEM(keep.shape, bf16), pltpu.SemaphoreType.DMA((2,))],
        "summed",
    )[0]


def joined(mine, other, stride):
    height, width = mine.shape
    if height % ROW_TILE:
        first = bit_of(DP, stride) == 0
        return jnp.concatenate([jnp.where(first, mine, other), jnp.where(first, other, mine)], axis=0)

    def kernel(mine_ref, other_ref, out_ref, held, sem):
        bit = bit_of(DP, stride)
        loads, stores = [], []
        for at, (half, source) in enumerate(((bit, mine_ref), (1 - bit, other_ref))):
            rows = pl.ds(pl.multiple_of(half * height, ROW_TILE), height)
            loads.append(pltpu.make_async_copy(source, held.at[at], sem.at[at]))
            stores.append(pltpu.make_async_copy(held.at[at], out_ref.at[rows, :], sem.at[2 + at]))
        for load in loads:
            load.start()
        for load, store in zip(loads, stores):
            load.wait()
            store.start()
        for store in stores:
            store.wait()

    return plain_call(
        kernel,
        (mine, other),
        [jax.ShapeDtypeStruct((2 * height, width), bf16)],
        [pltpu.VMEM((2, height, width), bf16), pltpu.SemaphoreType.DMA((4,))],
        f"joined_{stride}",
        [ANY],
    )[0]


def strides_of(size):
    return [1 << at for at in range(size.bit_length() - 1)]


class Line:
    def __init__(self):
        self.last = None

    def gate(self, value):
        if self.last is None:
            return value
        return lax.optimization_barrier((value, self.last))[0]

    def passed(self, value):
        self.last = value


class Exchange:
    def __init__(self, line, send, keep, strides, total):
        self.line, self.keep, self.strides, self.total = line, keep, strides, total
        self.at, self.half = 0, None
        self.coming = swapped(send, REP, 1)

    def advance(self):
        coming = self.line.gate(self.coming)
        count = len(self.strides)
        if self.at < count:
            stride = self.strides[self.at]
            send, self.keep = halved(self.keep, coming, stride)
            self.coming = swapped(send, DP, stride)
            self.line.passed(send)
        elif self.at == count:
            self.value = summed(self.keep, coming, self.total)
            self.coming = swapped(self.value, DP, self.strides[-1])
            self.line.passed(self.value)
        elif self.at < 2 * count:
            self.value = joined(self.value, coming, self.strides[2 * count - self.at])
            self.coming = swapped(self.value, DP, self.strides[2 * count - 1 - self.at])
            self.line.passed(self.value)
        elif self.at == 2 * count:
            self.half = (self.value, coming)
            self.others = swapped(lax.optimization_barrier(self.half)[0], REP, 1)
            self.coming = swapped(coming, REP, 1)
        else:
            self.half = (self.others, coming)
        self.at += 1


def added(value, coming):
    def kernel(value_ref, coming_ref, out_ref):
        out_ref[...] = value_ref[...] + coming_ref[...]

    return pl.pallas_call(
        kernel,
        out_shape=jax.ShapeDtypeStruct(value.shape, value.dtype),
        cost_estimate=pl.CostEstimate(flops=LATE_COST, bytes_accessed=LATE_COST, transcendentals=0),
        name="added",
    )(value, coming)


class Total:
    def __init__(self, line, value, strides):
        self.line, self.value = line, value
        self.partners = [(REP, 1)] + [(DP, stride) for stride in strides]
        self.at = 0
        self.coming = swapped(value, *self.partners[0])

    def advance(self):
        self.value = added(self.value, self.line.gate(self.coming))
        self.at += 1
        if self.at < len(self.partners):
            self.coming = swapped(self.value, *self.partners[self.at])
        self.line.passed(self.value)


def shards(
    boundary,
    keep_index,
    keep_count,
    gain_one,
    shift_one,
    w_qkv,
    bias_query,
    bias_value,
    w_out,
    bias_out,
    gain_two,
    shift_two,
    w_up,
    bias_up,
    w_down,
    bias_down,
):
    images = keep_index.shape[0]
    width = boundary.shape[-1]
    weights = (w_qkv[0], w_out[0], w_up[0], w_down[0])
    hidden = weights[2].shape[1]
    vectors = (gain_one, shift_one, bias_query, bias_value, bias_out, gain_two, shift_two, bias_down, bias_up)
    rows_in = boundary[0]

    line = Line()
    assert images == 3
    section = lax.axis_index(SECTION).astype(jnp.int32)
    scalars = jnp.concatenate([keep_count, section[None]])
    carry, received = None, []
    for image in range(2):
        carry, first_output = first_forward(image, carry, keep_count, keep_index, rows_in, vectors, weights)
        received.append(lax.ppermute(first_output, SECTION, [(0, 1)]))
    saved, output = carry[:-1], carry[-1]
    made, sums, returned = None, None, []
    for image, first, late in ((0, 2, None), (1, None, None), (2, None, 0)):
        saved, made, output, sums, sent = tick(
            first, image, late, saved, made, output, sums, scalars, keep_index, in_vmem(line.gate(received[image])),
            rows_in, vectors, weights,
        )
        line.passed(sent)
        both = [(1, 0)] + ([(0, 1)] if first is not None else [])
        returned.append(lax.ppermute(sent, SECTION, both))
        if first is not None:
            received.append(returned[-1])

    def flat(name):
        array = saved[SAVED.index(name)] if name in SAVED else made[MADE.index(name)]
        return array.reshape(-1, array.shape[-1])

    total = images * lax.axis_size((DP, REP))
    side = lax.axis_index(REP).astype(jnp.int32)[None]
    near_first = strides_of(lax.axis_size(DP))
    far_first = near_first[1::-1] + near_first[2:]
    square, many = (width, width), hidden // width
    forwards, attentions = [1, 2], [1, 2]
    residual = [None] * images
    exchanges, outs = {}, {}

    def begin(name, pair, strides):
        line.passed(pair[0])
        exchanges[name] = Exchange(line, *pair, strides, total)

    def feed_forward():
        nonlocal made, output, sums
        image = forwards.pop(0)
        made, output, sums, residual[image] = late_feed_forward(
            image, (0, 1) if image == 1 else (2,), saved, made, output, sums, keep_count, in_vmem(line.gate(returned[image])),
            vectors, weights,
        )
        line.passed(residual[image])

    def attention():
        nonlocal made, sums
        image = attentions.pop(0)
        made, sums = late_attention(
            image, saved, made, sums, line.gate(residual[image]), keep_count, keep_index, vectors, weights
        )
        line.passed(sums)

    def grad_down():
        pair = down_gradient(side, keep_count, line.gate(saved[SAVED.index(M)]), rows_in, returned)
        begin(DOWN, pair, near_first)

    def grad_up():
        blocks = [(0, 1, column) for column in range(many)]
        begin(UP, weight_gradient(side, (line.gate(flat(C)), flat(GZ)), blocks, "grad_up"), far_first)

    def grad_query_value():
        exchanges[SUMS] = Total(line, sums, near_first)
        pair = weight_gradient(side, (line.gate(flat(A)), flat(GQKV)), [(0, 1, 0), (0, 1, 2)], "grad_query_value")
        begin(QUERY_VALUE, pair, near_first)

    def grad_key_out():
        arrays = (line.gate(flat(A)), flat(GQKV), flat(O), flat(GB))
        pair = weight_gradient(side, arrays, [(0, 1, 1), (2, 3, 0)], "grad_key_out")
        begin(KEY_OUT, pair, near_first)

    def widen(name):
        places, kinds = {
            DOWN: ([(0, k, 0) for k in range(many)], {DOWN: (hidden, width)}),
            UP: ([(0, 0, k) for k in range(many)], {UP: (width, hidden)}),
            QUERY_VALUE: ([(0, 0, 0), (0, 1, 0), (0, 0, 2), (0, 1, 2)], {QKV: (width, 3 * width)}),
            KEY_OUT: ([(0, 0, 1), (0, 1, 1), (1, 0, 0), (1, 1, 0)], {QKV: (width, 3 * width), OUT: (width, width)}),
        }[name]
        exchange = exchanges[name]
        before = [outs[kind] for kind in kinds if kind in outs]
        first, second = exchange.half
        wholes = assembled(
            exchange.at == stages - 1,
            exchange.strides[0],
            (first, line.gate(second)),
            places,
            list(kinds.values()),
            before,
        )
        line.passed(wholes[0])
        outs.update(zip(kinds, wholes))

    steps = dict(zip("FAGUQK", (feed_forward, attention, grad_down, grad_up, grad_query_value, grad_key_out)))
    transfers = dict(zip("duqks", (DOWN, UP, QUERY_VALUE, KEY_OUT, SUMS)))
    stages = 2 * len(near_first) + 2
    plain = "FAFAGUQK" + "duqk" * stages + "s" * (stages // 2)
    for step in ORDER if (images, stages) == (3, 8) else plain:
        if step in steps:
            steps[step]()
            continue
        name = transfers[step]
        exchanges[name].advance()
        if name != SUMS and exchanges[name].half is not None:
            widen(name)
    assert all(exchange.at == (stages // 2 if name == SUMS else stages) for name, exchange in exchanges.items())
    sums = exchanges[SUMS].value / total
    small = [sums[at : at + 1] for at in VECTORS[:-1]]
    return (
        output[None],
        made[MADE.index(GRAD)][None],
        small[GAIN_ONE],
        small[SHIFT_ONE],
        outs[QKV][None],
        small[BIAS_QUERY],
        small[BIAS_VALUE],
        outs[OUT][None],
        small[BIAS_OUT],
        small[GAIN_TWO],
        small[SHIFT_TWO],
        outs[UP][None],
        sums[BIAS_UP : BIAS_UP + many].reshape(1, -1),
        outs[DOWN][None],
        small[BIAS_DOWN],
    )


def solution(mesh):
    per_image = (DP, REP)
    matrix, line = P(SECTION, None, None), P(SECTION, None)
    rows = P(SECTION, per_image, None, None)
    kinds = (line, line, matrix, line, line, matrix, line, line, line, matrix, line, matrix, line)
    return jax.shard_map(
        shards,
        mesh=mesh,
        in_specs=(rows, P(per_image, None), P(per_image)) + kinds,
        out_specs=(rows, rows) + kinds,
        check_vma=False,
    )
```

```python
import functools
from functools import partial
import math

import jax
import jax.numpy as jnp
from jax import lax
from jax.experimental import pallas as pl
from jax.experimental.pallas import tpu as pltpu
from jax.sharding import PartitionSpec as P

HEAD_DIM = 64
PAIR = 2 * HEAD_DIM
ROW_TILE = 16
COLUMNS = 256

norm_eps = 1e-06
masked_score = -1e30
f32 = jnp.float32
bf16 = jnp.bfloat16

NN = (((1,), (0,)), ((), ()))
NT = (((1,), (1,)), ((), ()))
TN = (((0,), (0,)), ((), ()))

VECTORS = range(9)
GAIN_ONE, SHIFT_ONE, BIAS_QUERY, BIAS_VALUE, BIAS_OUT, GAIN_TWO, SHIFT_TWO, BIAS_DOWN, BIAS_UP = VECTORS
SECTION, DP, REP = "section", "dp", "rep"
U, A, QKV, O, R, C, M, SLOPE, GD, GZ, GB, GR, GO, GQKV, GA, GU, E, Y, GRAD = range(19)
WEIGHTS = range(19, 23)
W_QKV, W_OUT, W_UP, W_DOWN = WEIGHTS
DOWN, UP, QUERY_VALUE, KEY_OUT, SUMS, OUT = range(100, 106)
ORDER = "FAGFUduAQdKudqukdqsukqdskuqdkqkuqsdksdquqkuk"
COST = 10**11
LATE_COST = 10**10
ANY = pl.BlockSpec(memory_space=pl.ANY)


def product(left, right, dims):
    return lax.dot_general(left, right, dims, preferred_element_type=f32)


def spans(size, step):
    return [slice(at, min(at + step, size)) for at in range(0, size, step)]


def column_sum(values):
    return jnp.sum(values, axis=0, keepdims=True)


def centre(values):
    centred = values - jnp.mean(values, axis=-1, keepdims=True)
    scale = lax.rsqrt(jnp.mean(centred * centred, axis=-1, keepdims=True) + norm_eps)
    return centred * scale, scale


class Copies:
    def __init__(self, sem, pairs):
        self.made = {
            name: pltpu.make_async_copy(source, target, sem.at[at])
            for at, (name, (source, target)) in enumerate(pairs.items())
        }

    def start(self, *names):
        for name in names or tuple(self.made):
            if name in self.made:
                self.made[name].start()

    def wait(self, *names):
        for name in names or tuple(self.made):
            if name in self.made:
                self.made.pop(name).wait()


def first_section():
    return lax.axis_index(SECTION) == 0


def row_mask(shape, count):
    return lax.broadcasted_iota(jnp.int32, shape, 0) < count


def gather_matrix(slots_of, count):
    slots = slots_of.shape[1]
    shape = (-(-slots // ROW_TILE) * ROW_TILE, slots)
    patch = lax.broadcasted_iota(jnp.int32, shape, 0)
    slot = lax.broadcasted_iota(jnp.int32, shape, 1)
    chosen = jnp.broadcast_to(slots_of, shape) == patch
    return jnp.where(chosen & (slot < count), 1.0, 0.0).astype(bf16)


def forward_part(r, wait, done, vec, weights, count):
    rows, width = r[U].shape[-2:]
    hidden = weights[W_UP].shape[1]
    for span in spans(rows, ROW_TILE):
        normal, _ = centre(r[U][span, :].astype(f32))
        r[A][span, :] = (normal * vec(GAIN_ONE) + vec(SHIFT_ONE)).astype(bf16)
    done(U, A)
    wait(W_QKV)
    for span in spans(3 * width, COLUMNS):
        packed = product(r[A][...], weights[W_QKV][:, span], NN)
        if span.start < width:
            packed = packed + vec(BIAS_QUERY, span)
        elif span.start >= 2 * width:
            packed = packed + vec(BIAS_VALUE, slice(span.start - 2 * width, span.stop - 2 * width))
        r[QKV][:, span] = packed.astype(bf16)
    done(QKV)
    low = (lax.broadcasted_iota(jnp.int32, (1, PAIR), 1) < HEAD_DIM).astype(bf16)
    lane = lax.broadcasted_iota(jnp.int32, (rows, PAIR), 1) < HEAD_DIM
    for at in range(0, width, PAIR):
        query = r[QKV][:, at : at + PAIR]
        key = r[QKV][:, width + at : width + at + PAIR]
        value = r[QKV][:, 2 * width + at : 2 * width + at + PAIR]
        both = jnp.concatenate([query * low, query * (1 - low)], axis=0)
        scores = product(both, key, NT) * (1.0 / math.sqrt(HEAD_DIM))
        live = lax.broadcasted_iota(jnp.int32, scores.shape, 1) < count
        scores = jnp.where(live, scores, masked_score)
        powers = jnp.exp(scores - jnp.max(scores, axis=-1, keepdims=True))
        chance = powers * (1.0 / jnp.sum(powers, axis=-1, keepdims=True))
        mixed = product(chance.astype(bf16), value, NN)
        r[O][:, at : at + PAIR] = jnp.where(lane, mixed[:rows], mixed[rows:]).astype(bf16)
    done(O)
    wait(W_OUT)
    for span in spans(width, COLUMNS):
        r[R][:, span] = r[U][:, span].astype(f32) + (
            product(r[O][...], weights[W_OUT][:, span], NN) + vec(BIAS_OUT, span)
        )
    for span in spans(rows, ROW_TILE):
        normal, _ = centre(r[R][span, :])
        r[C][span, :] = (normal * vec(GAIN_TWO) + vec(SHIFT_TWO)).astype(bf16)
    done(R, C)
    wait(W_UP)
    for span in spans(hidden, COLUMNS):
        z = product(r[C][...], weights[W_UP][:, span], NN) + vec(BIAS_UP, span)
        share = 0.5 * (1.0 + lax.erf(z * math.sqrt(0.5)))
        r[M][:, span] = (z * share).astype(bf16)
        r[SLOPE][:, span] = share + z * (jnp.exp(-0.5 * z * z) * (1.0 / math.sqrt(2 * math.pi)))
    done(M, SLOPE)


def output_part(r, vec, weights, count):
    rows, width = r[R].shape
    outer = r[Y].shape[0]
    for span in spans(width, COLUMNS):
        y = r[R][:, span] + (product(r[M][...], weights[W_DOWN][:, span], NN) + vec(BIAS_DOWN, span))
        r[Y][:, span] = jnp.where(row_mask(y.shape, count), y, 0.0).astype(bf16)[:outer]


def norm_back(normal, scale, gain, grad):
    x = grad * gain
    return scale * (
        x - jnp.mean(x, axis=-1, keepdims=True) - normal * jnp.mean(x * normal, axis=-1, keepdims=True)
    )


def feed_forward_back(r, wait, done, vec, weights, count, add):
    rows, width = r[R].shape
    hidden = weights[W_UP].shape[1]
    for span in spans(rows, ROW_TILE):
        live = lax.broadcasted_iota(jnp.int32, (ROW_TILE, width), 0) + span.start < count
        r[GD][span, :] = jnp.where(live, r[E][span, :], jnp.zeros((), bf16))
    add(BIAS_DOWN, lambda: column_sum(r[GD][...].astype(f32)))
    wait(W_DOWN, SLOPE)
    for span in spans(hidden, COLUMNS):
        gz = product(r[GD][...], weights[W_DOWN][span, :], NT) * r[SLOPE][:, span]
        r[GZ][:, span] = gz.astype(bf16)
        add(BIAS_UP, lambda: column_sum(r[GZ][:, span].astype(f32)), span)
    done(GZ)
    wait(W_UP, R)
    for span in spans(width, COLUMNS):
        r[GR][:, span] = product(r[GZ][...], weights[W_UP][span, :], NT)
    gain_sum, shift_sum = 0.0, 0.0
    for span in spans(rows, ROW_TILE):
        normal, scale = centre(r[R][span, :])
        gc = r[GR][span, :]
        gain_sum, shift_sum = gain_sum + gc * normal, shift_sum + gc
        gr = r[GD][span, :].astype(f32) + norm_back(normal, scale, vec(GAIN_TWO), gc)
        r[GR][span, :] = gr
        r[GB][span, :] = gr.astype(bf16)
    done(GB, GR)
    add(GAIN_TWO, lambda: column_sum(gain_sum))
    add(SHIFT_TWO, lambda: column_sum(shift_sum))
    add(BIAS_OUT, lambda: column_sum(r[GB][...].astype(f32)))


def attention_back(r, wait, done, vec, weights, count, add):
    rows, width = r[U].shape
    wait(GB, W_OUT)
    for span in spans(width, COLUMNS):
        r[GO][:, span] = product(r[GB][...], weights[W_OUT][span, :], NT).astype(bf16)
    wait(QKV)
    low = (lax.broadcasted_iota(jnp.int32, (1, PAIR), 1) < HEAD_DIM).astype(bf16)
    lane = lax.broadcasted_iota(jnp.int32, (rows, PAIR), 1) < HEAD_DIM
    score_scale = 1.0 / math.sqrt(HEAD_DIM)
    live = row_mask((rows, rows), count)
    for at in range(0, width, PAIR):
        query = r[QKV][:, at : at + PAIR]
        key = r[QKV][:, width + at : width + at + PAIR]
        value = r[QKV][:, 2 * width + at : 2 * width + at + PAIR]
        go = r[GO][:, at : at + PAIR]
        scores = product(jnp.concatenate([key * low, key * (1 - low)], axis=0), query, NT) * score_scale
        grads = product(jnp.concatenate([value * low, value * (1 - low)], axis=0), go, NT)
        chances, inner = [], []
        for head in range(2):
            score = jnp.where(live, scores[head * rows : (head + 1) * rows], masked_score)
            powers = jnp.exp(score - jnp.max(score, axis=0, keepdims=True))
            chance = powers * (1.0 / jnp.sum(powers, axis=0, keepdims=True))
            gp = grads[head * rows : (head + 1) * rows]
            gs = chance * (gp - jnp.sum(gp * chance, axis=0, keepdims=True))
            chances.append(chance.astype(bf16))
            inner.append(jnp.where(live, gs, 0.0).astype(bf16))
        gw = product(jnp.concatenate(chances, axis=0), go, NN)
        gk = product(jnp.concatenate(inner, axis=0), query, NN) * score_scale
        gq = [product(gs, key, TN) * score_scale for gs in inner]
        r[GQKV][:, at : at + PAIR] = jnp.where(lane, gq[0], gq[1]).astype(bf16)
        r[GQKV][:, width + at : width + at + PAIR] = jnp.where(lane, gk[:rows], gk[rows:]).astype(bf16)
        r[GQKV][:, 2 * width + at : 2 * width + at + PAIR] = jnp.where(lane, gw[:rows], gw[rows:]).astype(
            bf16
        )
    done(GQKV)
    add(BIAS_QUERY, lambda: column_sum(r[GQKV][:, :width].astype(f32)))
    add(BIAS_VALUE, lambda: column_sum(r[GQKV][:, 2 * width :].astype(f32)))
    wait(W_QKV, U, GR)
    for span in spans(width, COLUMNS):
        r[GA][:, span] = product(r[GQKV][...], weights[W_QKV][span, :], NT)
    gain_sum, shift_sum = 0.0, 0.0
    for span in spans(rows, ROW_TILE):
        normal, scale = centre(r[U][span, :].astype(f32))
        ga = r[GA][span, :]
        gain_sum, shift_sum = gain_sum + ga * normal, shift_sum + ga
        gu = r[GR][span, :] + norm_back(normal, scale, vec(GAIN_ONE), ga)
        r[GU][span, :] = gu.astype(bf16)
    add(GAIN_ONE, lambda: column_sum(gain_sum))
    add(SHIFT_ONE, lambda: column_sum(shift_sum))


def vector_reader(refs):
    named = dict(zip(VECTORS, refs))

    def vec(name, span=None):
        ref = named[name]
        return (ref[...] if span is None else ref[:, span]).astype(f32)

    return vec


def vector_adder(ref):
    def add(name, values, span=None):
        values = values()
        start = 0 if span is None else span.start
        row, start = VECTORS.index(name) + start // ref.shape[1], start % ref.shape[1]
        ref[row : row + 1, start : start + values.shape[1]] += values

    return add


def pad_rows(target, source):
    inner, rows = source.shape[0], target.shape[0]
    target[:inner, :] = source[...]
    if rows > inner:
        target[inner:, :] = jnp.zeros((rows - inner, target.shape[1]), target.dtype)


def padded_rows(slots):
    return -(-slots // ROW_TILE) * ROW_TILE


def image_block(shape, image):
    return pl.BlockSpec((pl.Squeezed(),) + tuple(shape), lambda *_: (image, 0, 0))


def fixed_block(shape):
    return pl.BlockSpec(tuple(shape), lambda *_: (0,) * len(shape))


def weight_scratch(weights):
    return [pltpu.VMEM(weight.shape, weight.dtype) for weight in weights] + [
        pltpu.SemaphoreType.DMA((len(weights),))
    ]


def fetch_weights(sem, hbm, local, order=WEIGHTS):
    found = dict(zip(WEIGHTS, zip(hbm, local)))
    return Copies(sem, {name: found[name] for name in order}), dict(zip(WEIGHTS, local))


def call(kernel, steps, scalars, ins, in_specs, outs, out_specs, scratch, name, aliases=None, room=60):
    return pl.pallas_call(
        kernel,
        out_shape=outs,
        grid_spec=pltpu.PrefetchScalarGridSpec(
            num_scalar_prefetch=1,
            grid=(steps,),
            in_specs=in_specs,
            out_specs=out_specs,
            scratch_shapes=scratch,
        ),
        compiler_params=pltpu.CompilerParams(
            dimension_semantics=("arbitrary",), vmem_limit_bytes=room << 20
        ),
        input_output_aliases=aliases or {},
        cost_estimate=pl.CostEstimate(flops=COST, bytes_accessed=COST, transcendentals=0),
        name=name,
    )(scalars, *ins)


def split(refs, *sizes):
    out, at = [], 0
    for size in sizes:
        out.append(refs[at] if size is None else refs[at : at + size])
        at += 1 if size is None else size
    assert at == len(refs)
    return out


def nothing(*_):
    return None


SAVED = (U, A, QKV, O, R, C, M, SLOPE)
MADE = (GZ, GB, GQKV, GRAD)


def image_shapes(slots, rows, width, hidden):
    narrow, wide = (rows, width), (rows, hidden)
    return {
        U: (narrow, bf16),
        A: (narrow, bf16),
        QKV: ((rows, 3 * width), bf16),
        O: (narrow, bf16),
        R: (narrow, f32),
        C: (narrow, bf16),
        M: (wide, bf16),
        SLOPE: (wide, f32),
        GD: (narrow, bf16),
        GZ: (wide, bf16),
        GB: (narrow, bf16),
        GR: (narrow, f32),
        GO: (narrow, bf16),
        GQKV: ((rows, 3 * width), bf16),
        GA: (narrow, f32),
        GU: (narrow, bf16),
        E: (narrow, bf16),
        Y: ((slots, width), bf16),
        GRAD: ((slots, width), bf16),
    }


def first_forward(image, carry, count, index, source, vectors, weights):
    images, slots, width = source.shape
    rows, hidden = padded_rows(slots), weights[2].shape[1]
    shapes = image_shapes(slots, rows, width, hidden)
    work = SAVED + (Y,)
    old = () if carry is None else tuple(carry)
    at = 1 + 2 + len(vectors) + 4

    def kernel(count_ref, index_ref, source_ref, *rest):
        vecs, hbm, _, places, y_ref, local, sem, scratch, padded, out_sem = split(
            rest, len(vectors), 4, len(old), len(work), None, 4, None, len(work), None, None
        )

        @pl.when(first_section())
        def _():
            fetch, near = fetch_weights(sem, hbm, local)
            fetch.start()
            kept = count_ref[image]
            refs = dict(zip(work, scratch))
            store = Copies(out_sem, {name: (refs[name], place.at[image]) for name, place in zip(work, places)})
            pad_rows(padded, source_ref)
            chosen = gather_matrix(index_ref[image : image + 1, :], kept)
            refs[U][:slots, :] = product(chosen, padded[...], TN).astype(bf16)
            refs[U][slots:, :] = jnp.zeros((rows - slots, width), bf16)
            vec = vector_reader(vecs)
            forward_part(refs, fetch.wait, store.start, vec, near, kept)
            fetch.wait(W_DOWN)
            output_part(refs, vec, near, kept)
            store.start(Y)
            y_ref[...] = refs[Y][...]
            store.wait()

    *carry, output = call(
        kernel,
        1,
        count,
        (index, source) + vectors + weights + old,
        [fixed_block(index.shape), image_block((slots, width), image)]
        + [fixed_block(vector.shape) for vector in vectors]
        + [ANY] * (4 + len(old)),
        [jax.ShapeDtypeStruct((images,) + shapes[name][0], shapes[name][1]) for name in work]
        + [jax.ShapeDtypeStruct((1, slots, width), bf16)],
        [ANY] * len(work) + [image_block((slots, width), 0)],
        weight_scratch(weights)
        + [pltpu.VMEM(*shapes[name]) for name in work]
        + [pltpu.VMEM((rows, width), bf16), pltpu.SemaphoreType.DMA((len(work),))],
        f"first_forward_{image}",
        {at + k: k for k in range(len(old))},
    )
    return carry, output


def tick(first, image, late, saved, made, output, sums, scalars, index, received, source, vectors, weights):
    images, slots, width = source.shape
    rows, hidden = padded_rows(slots), weights[2].shape[1]
    shapes = image_shapes(slots, rows, width, hidden)
    carry = SAVED + MADE + (Y,)
    lines = -(-(len(vectors) - 1 + hidden // width) // 8) * 8
    work = (E, GD, GR, GO, GA, GU) + carry
    old = tuple(saved) + (() if made is None else tuple(made)) + (output,) + (() if made is None else (sums,))
    slots_of = [k for k, name in enumerate(carry) if made is not None or name not in MADE]
    slots_of += [] if made is None else [len(carry)]
    at = 1 + 3 + len(vectors) + 4
    other = first if first is not None else late if late is not None else image

    def kernel(scalar_ref, index_ref, received_ref, source_ref, *rest):
        vecs, hbm, previous, places, sums_ref, send_ref, local, sem, scratch, out_sem = split(
            rest, len(vectors), 4, len(old), len(carry), None, None, 4, None, len(work), None
        )
        sums_ref[...] = jnp.zeros(sums_ref.shape, f32) if made is None else previous[-1][...]
        early = first_section()
        later = jnp.logical_not(early)
        here = jnp.where(early, other, image)
        live = scalar_ref[here]
        refs = dict(zip(work, scratch))
        place = {name: ref.at[here] for name, ref in zip(carry, places)}
        store = Copies(out_sem, {name: (refs[name], place[name]) for name in carry})
        vec, add = vector_reader(vecs), vector_adder(sums_ref)

        def gathered():
            pad_rows(refs[E], source_ref)
            chosen = gather_matrix(index_ref[first : first + 1, :], live)
            refs[U][:slots, :] = product(chosen, refs[E][...], TN).astype(bf16)
            refs[U][slots:, :] = jnp.zeros((rows - slots, width), bf16)

        def forward(fetch, near):
            forward_part(refs, fetch.wait, store.start, vec, near, live)
            fetch.wait(W_DOWN)

        def backward(near, wait=nothing):
            feed_forward_back(refs, wait, store.start, vec, near, live, add)
            attention_back(refs, wait, store.start, vec, near, live, add)

        def fetched():
            weights_in = fetch_weights(sem, hbm, local, (W_DOWN, W_UP, W_OUT, W_QKV))[0]
            return weights_in, Copies(out_sem, {name: (place[name], refs[name]) for name in (SLOPE, R, QKV, U)})

        def await_early(*names):
            @pl.when(early)
            def _():
                for copies in fetched():
                    copies.wait(*names)

        def sent():
            refs[GRAD][...] = refs[GU][:slots, :]
            store.start(GRAD)
            send_ref[...] = refs[GU][:slots, :]

        if first is not None:
            fetch, near = fetch_weights(sem, hbm, local)
            fetch.start()

            @pl.when(early)
            def _():
                gathered()

            @pl.when(later)
            def _():
                pad_rows(refs[U], received_ref.at[0])

            forward(fetch, near)

            @pl.when(early)
            def _():
                output_part(refs, vec, near, live)
                store.start(Y)
                send_ref[...] = refs[Y][...]
                Copies(out_sem, {name: (refs[name], place[name]) for name in carry}).wait(*SAVED, Y)

            @pl.when(later)
            def _():
                pad_rows(refs[E], source_ref)
                backward(near)
                sent()
                Copies(out_sem, {name: (refs[name], place[name]) for name in carry}).wait(*SAVED, *MADE)

            return

        @pl.when(later)
        def _():
            fetch, near = fetch_weights(sem, hbm, local)
            fetch.start()
            pad_rows(refs[U], received_ref.at[0])
            pad_rows(refs[E], source_ref)
            forward(fetch, near)
            if late is None:
                backward(near)
                sent()
                store.wait(*SAVED, *MADE)

        if late is None:
            return

        @pl.when(early)
        def _():
            for copies in fetched():
                copies.start()
            pad_rows(refs[E], received_ref.at[0])

        backward(dict(zip(WEIGHTS, local)), await_early)

        @pl.when(early)
        def _():
            chosen = gather_matrix(index_ref[late : late + 1, :], live)
            refs[GRAD][...] = product(chosen, refs[GU][:slots, :], NN)[:slots, :].astype(bf16)
            store.start(GRAD)

        @pl.when(later)
        def _():
            sent()
            Copies(out_sem, {name: (refs[name], place[name]) for name in SAVED}).wait()

        store.wait(*MADE)

    results = call(
        kernel,
        1,
        scalars,
        (index, received, source) + vectors + weights + old,
        [
            fixed_block(index.shape),
            pl.BlockSpec(memory_space=pltpu.VMEM),
            pl.BlockSpec(
                (pl.Squeezed(), slots, width), lambda i, s: (jnp.where(s[images] == 0, other, image), 0, 0)
            ),
        ]
        + [fixed_block(vector.shape) for vector in vectors]
        + [ANY] * (4 + len(old) - (made is not None))
        + ([] if made is None else [fixed_block(sums.shape)]),
        [jax.ShapeDtypeStruct((images,) + shapes[name][0], shapes[name][1]) for name in carry]
        + [jax.ShapeDtypeStruct((lines, width), f32), jax.ShapeDtypeStruct((1, slots, width), bf16)],
        [ANY] * len(carry) + [fixed_block((lines, width)), image_block((slots, width), 0)],
        weight_scratch(weights)
        + [pltpu.VMEM(*shapes[name]) for name in work]
        + [pltpu.SemaphoreType.DMA((len(carry),))],
        f"tick_{image}",
        {at + k: slot for k, slot in enumerate(slots_of)},
    )
    saved, made = results[: len(SAVED)], results[len(SAVED) : len(SAVED) + len(MADE)]
    return saved, made, results[-3], results[-2], results[-1]


def late_feed_forward(image, outputs, saved, made, output, sums, count, received, vectors, weights):
    images, rows, hidden = saved[SAVED.index(M)].shape
    slots, width = received.shape[1:]
    shapes = image_shapes(slots, rows, width, hidden)
    loads = (SLOPE, R, M)
    stores = (GZ, GB, Y)
    work = (SLOPE, R, M, E, GD, GZ, GB, Y)
    near_names = (W_DOWN, W_UP)
    old = [made[MADE.index(GZ)], made[MADE.index(GB)], output, sums]
    at = 1 + 1 + len(vectors) + len(loads) + len(near_names)

    def kernel(count_ref, received_ref, *rest):
        vecs, sources, hbm, previous, places, sums_ref, gr_ref, local, scratch, sem = split(
            rest, len(vectors), len(loads), 2, len(old), len(stores), None, None, 2, len(work), None
        )
        live = count_ref[image]
        refs = dict(zip(work, scratch)) | {GR: gr_ref}
        near = dict(zip(near_names, local))
        far = dict(zip(near_names, hbm))
        source = {name: ref.at[image] for name, ref in zip(loads, sources)}
        place = {name: ref.at[image] for name, ref in zip(stores, places)}
        vec = vector_reader(vecs)
        sums_ref[...] = previous[-1][...]
        early = first_section()

        @pl.when(early)
        def _():
            fetch = Copies(
                sem,
                {
                    W_DOWN: (far[W_DOWN], near[W_DOWN]),
                    SLOPE: (source[SLOPE], refs[SLOPE]),
                    W_UP: (far[W_UP], near[W_UP]),
                    R: (source[R], refs[R]),
                },
            )
            fetch.start()
            store = Copies(sem.at[pl.ds(5, 2)], {name: (refs[name], place[name]) for name in (GZ, GB)})
            pad_rows(refs[E], received_ref.at[0])
            feed_forward_back(refs, fetch.wait, store.start, vec, near, live, vector_adder(sums_ref))
            store.wait()

        @pl.when(jnp.logical_not(early))
        def _():
            fetch = Copies(sem, {W_DOWN: (far[W_DOWN], near[W_DOWN])})
            fetch.start()
            for which in outputs:
                load = Copies(
                    sem.at[pl.ds(1, 2)],
                    {name: (sources[loads.index(name)].at[which], refs[name]) for name in (R, M)},
                )
                load.start()
                fetch.wait()
                load.wait()
                output_part(refs, vec, near, count_ref[which])
                store = Copies(sem.at[pl.ds(4, 1)], {Y: (refs[Y], places[stores.index(Y)].at[which])})
                store.start()
                store.wait()

    gz, gb, output, sums, gr = call(
        kernel,
        1,
        count,
        (received,)
        + vectors
        + tuple(saved[SAVED.index(name)] for name in loads)
        + tuple(weights[WEIGHTS.index(name)] for name in near_names)
        + tuple(old),
        [pl.BlockSpec(memory_space=pltpu.VMEM)]
        + [fixed_block(vector.shape) for vector in vectors]
        + [ANY] * (len(loads) + len(near_names) + len(old) - 1)
        + [fixed_block(sums.shape)],
        [
            jax.ShapeDtypeStruct((images,) + shapes[GZ][0], bf16),
            jax.ShapeDtypeStruct((images,) + shapes[GB][0], bf16),
            jax.ShapeDtypeStruct((images,) + shapes[Y][0], bf16),
            jax.ShapeDtypeStruct(sums.shape, f32),
            jax.ShapeDtypeStruct((1,) + shapes[GR][0], f32),
        ],
        [ANY] * 3 + [fixed_block(sums.shape), image_block(shapes[GR][0], 0)],
        [pltpu.VMEM(weights[WEIGHTS.index(name)].shape, bf16) for name in near_names]
        + [pltpu.VMEM(*shapes[name]) for name in work]
        + [pltpu.SemaphoreType.DMA((7,))],
        f"late_feed_forward_{image}",
        {at + k: k for k in range(len(old))},
    )
    return [gz, gb] + list(made[2:]), output, sums, gr


def late_attention(image, saved, made, sums, gr, count, index, vectors, weights):
    images, slots, width = made[MADE.index(GRAD)].shape
    rows, hidden = saved[SAVED.index(M)].shape[1:]
    shapes = image_shapes(slots, rows, width, hidden)
    work = (GB, QKV, U, GO, GQKV, GA, GU, GRAD)
    near_names = (W_OUT, W_QKV)
    old = [made[MADE.index(GQKV)], made[MADE.index(GRAD)], sums]
    sources = (made[MADE.index(GB)], saved[SAVED.index(QKV)], saved[SAVED.index(U)])
    at = 1 + 2 + len(vectors) + len(sources) + len(near_names)

    def kernel(count_ref, index_ref, gr_ref, *rest):
        vecs, loads, hbm, previous, gqkv_ref, grad_ref, sums_ref, local, scratch, sem = split(
            rest, len(vectors), len(sources), 2, len(old), None, None, None, 2, len(work), None
        )
        live = count_ref[image]
        sums_ref[...] = previous[-1][...]
        refs = dict(zip(work, scratch)) | {GR: gr_ref}
        near = dict(zip(near_names, local))

        @pl.when(first_section())
        def _():
            fetch = Copies(
                sem,
                {
                    GB: (loads[0].at[image], refs[GB]),
                    W_OUT: (hbm[0], near[W_OUT]),
                    QKV: (loads[1].at[image], refs[QKV]),
                    W_QKV: (hbm[1], near[W_QKV]),
                    U: (loads[2].at[image], refs[U]),
                },
            )
            fetch.start()
            store = Copies(
                sem.at[pl.ds(5, 2)],
                {GQKV: (refs[GQKV], gqkv_ref.at[image]), GRAD: (refs[GRAD], grad_ref.at[image])},
            )
            attention_back(refs, fetch.wait, store.start, vector_reader(vecs), near, live, vector_adder(sums_ref))
            chosen = gather_matrix(index_ref[image : image + 1, :], live)
            refs[GRAD][...] = product(chosen, refs[GU][:slots, :], NN)[:slots, :].astype(bf16)
            store.start(GRAD)
            store.wait()

    gqkv, grad, sums = call(
        kernel,
        1,
        count,
        (index, gr)
        + vectors
        + sources
        + tuple(weights[WEIGHTS.index(name)] for name in near_names)
        + tuple(old),
        [fixed_block(index.shape), image_block((rows, width), 0)]
        + [fixed_block(vector.shape) for vector in vectors]
        + [ANY] * (len(sources) + len(near_names) + len(old) - 1)
        + [fixed_block(sums.shape)],
        [
            jax.ShapeDtypeStruct((images,) + shapes[GQKV][0], bf16),
            jax.ShapeDtypeStruct((images,) + shapes[GRAD][0], bf16),
            jax.ShapeDtypeStruct(sums.shape, f32),
        ],
        [ANY] * 2 + [fixed_block(sums.shape)],
        [pltpu.VMEM(weights[WEIGHTS.index(name)].shape, bf16) for name in near_names]
        + [pltpu.VMEM(*shapes[name]) for name in work]
        + [pltpu.SemaphoreType.DMA((7,))],
        f"late_attention_{image}",
        {at + k: k for k in range(len(old))},
    )
    return list(made[:2]) + [gqkv, grad], sums


def pick(table, at):
    value = table[0]
    for k in range(1, len(table)):
        value = jnp.where(at == k, table[k], value)
    return value


def weight_gradient(side, arrays, blocks, name):
    depth = arrays[0].shape[0]
    width = min(array.shape[1] for array in arrays)
    half = len(blocks) // 2

    def chosen(i, scalar_ref):
        bit = scalar_ref[0]
        return jnp.where(i < half, (1 - bit) * half + i, bit * half + i - half)

    def kernel(scalar_ref, *refs):
        send_ref, keep_ref = refs[-2:]
        step = pl.program_id(0)
        block = chosen(step, scalar_ref)
        for left, right in dict.fromkeys((left, right) for left, right, _ in blocks):
            here = functools.reduce(
                jnp.logical_or, [block == k for k, entry in enumerate(blocks) if entry[:2] == (left, right)]
            )

            @pl.when(here & (step < half))
            def _():
                send_ref[...] = product(refs[left][...], refs[right][...], TN).astype(bf16)

            @pl.when(here & (step >= half))
            def _():
                keep_ref[...] = product(refs[left][...], refs[right][...], TN).astype(bf16)

    def columns(at):
        table = [column if right == at else 0 for _, right, column in blocks]
        return pl.BlockSpec((depth, width), lambda i, s: (0, pick(table, chosen(i, s))))

    return call(
        kernel,
        2 * half,
        side,
        arrays,
        [columns(at) for at in range(len(arrays))],
        [jax.ShapeDtypeStruct((half * width, width), bf16)] * 2,
        [
            pl.BlockSpec((width, width), lambda i, s: (jnp.minimum(i, half - 1), 0)),
            pl.BlockSpec((width, width), lambda i, s: (jnp.maximum(i - half, 0), 0)),
        ],
        [],
        name,
        room=60,
    )


def down_gradient(side, count, m, cotangent, received):
    images, slots, width = cotangent.shape
    rows, hidden = m.shape[1:]
    blocks = hidden // width
    half = blocks // 2
    scalars = jnp.concatenate([side, count])

    def chosen(i, scalar_ref):
        bit = scalar_ref[0]
        return jnp.where(i < half, (1 - bit) * half + i, bit * half + i - half)

    def kernel(scalar_ref, m_ref, e_ref, *rest):
        arrived, (send_ref, keep_ref, gd_ref) = rest[:images], rest[images:]
        step = pl.program_id(0)
        early = first_section()

        @pl.when(step == 0)
        def _():
            for image in range(images):
                live = row_mask((slots, width), scalar_ref[1 + image])
                top = slice(image * rows, image * rows + slots)
                gd_ref[top, :] = jnp.where(live, jnp.where(early, arrived[image][...], e_ref[image]), jnp.zeros((), bf16))
                gd_ref[top.stop : (image + 1) * rows, :] = jnp.zeros((rows - slots, width), bf16)

        left = m_ref[...].reshape(images * rows, width)

        @pl.when(step < half)
        def _():
            send_ref[...] = product(left, gd_ref[...], TN).astype(bf16)

        @pl.when(step >= half)
        def _():
            keep_ref[...] = product(left, gd_ref[...], TN).astype(bf16)

    return call(
        kernel,
        blocks,
        scalars,
        (m, cotangent) + tuple(received),
        [
            pl.BlockSpec((images, rows, width), lambda i, s: (0, 0, chosen(i, s))),
            fixed_block(cotangent.shape),
        ]
        + [image_block((slots, width), 0)] * images,
        [jax.ShapeDtypeStruct((half * width, width), bf16)] * 2,
        [
            pl.BlockSpec((width, width), lambda i, s: (jnp.minimum(i, half - 1), 0)),
            pl.BlockSpec((width, width), lambda i, s: (jnp.maximum(i - half, 0), 0)),
        ],
        [pltpu.VMEM((images * rows, width), bf16)],
        "grad_down",
        room=60,
    )


def plain_call(kernel, ins, outs, name):
    return pl.pallas_call(
        kernel,
        out_shape=outs,
        in_specs=[pl.BlockSpec(memory_space=pltpu.VMEM)] * len(ins),
        out_specs=[pl.BlockSpec(memory_space=pltpu.VMEM)] * len(outs),
        compiler_params=pltpu.CompilerParams(vmem_limit_bytes=16 << 20),
        cost_estimate=pl.CostEstimate(flops=COST, bytes_accessed=COST, transcendentals=0),
        name=name,
    )(*(in_vmem(value) for value in ins))


def assembled(own, stride, pieces, places, shapes, before):
    shape = pieces[0].shape

    def kernel(*refs):
        sources, _, outs, (raw, wide, sem) = split(refs, 2, len(before), len(shapes), 3)
        core = lax.axis_index(REP) if own else 1 - lax.axis_index(REP)
        near = bit_of(DP, stride)
        loads = [pltpu.make_async_copy(source, raw.at[k], sem.at[k]) for k, source in enumerate(sources)]
        for load in loads:
            load.start()

        def stores(k, act):
            block = 2 * core + (near if k == 0 else 1 - near)
            for at, (which, row, column) in enumerate(places):
                rows, columns = pl.ds(row * shape[0], shape[0]), pl.ds(column * shape[1], shape[1])

                @pl.when(block == at)
                def _():
                    act(pltpu.make_async_copy(wide.at[k], outs[which].at[rows, columns], sem.at[2 + k]))

        for k in range(2):
            loads[k].wait()
            wide[k] = raw[k].astype(f32)
            stores(k, lambda copy: copy.start())
        for k in range(2):
            stores(k, lambda copy: copy.wait())

    return pl.pallas_call(
        kernel,
        out_shape=[jax.ShapeDtypeStruct(whole, f32) for whole in shapes],
        in_specs=[ANY] * (2 + len(before)),
        out_specs=[ANY] * len(shapes),
        scratch_shapes=[
            pltpu.VMEM((2,) + shape, bf16),
            pltpu.VMEM((2,) + shape, f32),
            pltpu.SemaphoreType.DMA((4,)),
        ],
        input_output_aliases={2 + k: k for k in range(len(before))},
        compiler_params=pltpu.CompilerParams(vmem_limit_bytes=16 << 20),
        cost_estimate=pl.CostEstimate(flops=LATE_COST, bytes_accessed=LATE_COST, transcendentals=0),
        name="assembled",
    )(*pieces, *before)


def in_vmem(value):
    return pltpu.with_memory_space_constraint(value, pltpu.VMEM)


def swapped(value, axis, stride):
    length = lax.axis_size(axis)
    return lax.ppermute(value, axis, [(i, i ^ stride) for i in range(length)])


def bit_of(axis, stride):
    return (lax.axis_index(axis) // stride) % 2


def halved(keep, coming, stride):
    height, width = keep.shape[0] // 2, keep.shape[1]
    if height % ROW_TILE:
        bit = bit_of(DP, stride)
        pair = (keep.astype(f32) + coming.astype(f32)).astype(bf16)
        send = lax.dynamic_slice_in_dim(pair, (1 - bit) * height, height, axis=0)
        return send, lax.dynamic_slice_in_dim(pair, bit * height, height, axis=0)

    def kernel(keep_ref, coming_ref, send_ref, stay_ref):
        bit = bit_of(DP, stride)
        for half, out_ref in ((1 - bit, send_ref), (bit, stay_ref)):
            rows = pl.ds(pl.multiple_of(half * height, ROW_TILE), height)
            out_ref[...] = (keep_ref[rows, :].astype(f32) + coming_ref[rows, :].astype(f32)).astype(bf16)

    shape = jax.ShapeDtypeStruct((height, width), bf16)
    return plain_call(kernel, (keep, coming), [shape] * 2, f"halved_{stride}")


def summed(keep, coming, total):
    if keep.shape[0] % ROW_TILE:
        return ((keep.astype(f32) + coming.astype(f32)) / total).astype(bf16)

    def kernel(keep_ref, coming_ref, out_ref):
        out_ref[...] = ((keep_ref[...].astype(f32) + coming_ref[...].astype(f32)) / total).astype(bf16)

    return plain_call(kernel, (keep, coming), [jax.ShapeDtypeStruct(keep.shape, bf16)], "summed")[0]


def joined(mine, other, stride):
    height, width = mine.shape
    if height % ROW_TILE:
        first = bit_of(DP, stride) == 0
        return jnp.concatenate([jnp.where(first, mine, other), jnp.where(first, other, mine)], axis=0)

    def kernel(mine_ref, other_ref, out_ref):
        bit = bit_of(DP, stride)
        for half, source in ((bit, mine_ref), (1 - bit, other_ref)):
            out_ref[pl.ds(pl.multiple_of(half * height, ROW_TILE), height), :] = source[...]

    shape = jax.ShapeDtypeStruct((2 * height, width), bf16)
    return plain_call(kernel, (mine, other), [shape], f"joined_{stride}")[0]


def strides_of(size):
    return [1 << at for at in range(size.bit_length() - 1)]


class Line:
    def __init__(self):
        self.last = None

    def gate(self, value):
        if self.last is None:
            return value
        return lax.optimization_barrier((value, self.last))[0]

    def passed(self, value):
        self.last = value


class Exchange:
    def __init__(self, line, send, keep, strides, total):
        self.line, self.keep, self.strides, self.total = line, keep, strides, total
        self.at, self.half = 0, None
        self.coming = swapped(send, REP, 1)

    def advance(self):
        coming = self.line.gate(self.coming)
        count = len(self.strides)
        if self.at < count:
            stride = self.strides[self.at]
            send, self.keep = halved(self.keep, coming, stride)
            self.coming = swapped(send, DP, stride)
            self.line.passed(send)
        elif self.at == count:
            self.value = summed(self.keep, coming, self.total)
            self.coming = swapped(self.value, DP, self.strides[-1])
            self.line.passed(self.value)
        elif self.at < 2 * count:
            self.value = joined(self.value, coming, self.strides[2 * count - self.at])
            self.coming = swapped(self.value, DP, self.strides[2 * count - 1 - self.at])
            self.line.passed(self.value)
        elif self.at == 2 * count:
            self.half = (self.value, coming)
            self.others = swapped(lax.optimization_barrier(self.half)[0], REP, 1)
            self.coming = swapped(coming, REP, 1)
        else:
            self.half = (self.others, coming)
        self.at += 1


def added(value, coming):
    def kernel(value_ref, coming_ref, out_ref):
        out_ref[...] = value_ref[...] + coming_ref[...]

    return pl.pallas_call(
        kernel,
        out_shape=jax.ShapeDtypeStruct(value.shape, value.dtype),
        cost_estimate=pl.CostEstimate(flops=LATE_COST, bytes_accessed=LATE_COST, transcendentals=0),
        name="added",
    )(value, coming)


class Total:
    def __init__(self, line, value, strides):
        self.line, self.value = line, value
        self.partners = [(REP, 1)] + [(DP, stride) for stride in strides]
        self.at = 0
        self.coming = swapped(value, *self.partners[0])

    def advance(self):
        self.value = added(self.value, self.line.gate(self.coming))
        self.at += 1
        if self.at < len(self.partners):
            self.coming = swapped(self.value, *self.partners[self.at])
        self.line.passed(self.value)


def shards(
    boundary,
    keep_index,
    keep_count,
    gain_one,
    shift_one,
    w_qkv,
    bias_query,
    bias_value,
    w_out,
    bias_out,
    gain_two,
    shift_two,
    w_up,
    bias_up,
    w_down,
    bias_down,
):
    images = keep_index.shape[0]
    width = boundary.shape[-1]
    weights = (w_qkv[0], w_out[0], w_up[0], w_down[0])
    hidden = weights[2].shape[1]
    vectors = (gain_one, shift_one, bias_query, bias_value, bias_out, gain_two, shift_two, bias_down, bias_up)
    rows_in = boundary[0]

    line = Line()
    assert images == 3
    section = lax.axis_index(SECTION).astype(jnp.int32)
    scalars = jnp.concatenate([keep_count, section[None]])
    carry, received = None, []
    for image in range(2):
        carry, first_output = first_forward(image, carry, keep_count, keep_index, rows_in, vectors, weights)
        received.append(lax.ppermute(first_output, SECTION, [(0, 1)]))
    saved, output = carry[:-1], carry[-1]
    made, sums, returned = None, None, []
    for image, first, late in ((0, 2, None), (1, None, None), (2, None, 0)):
        saved, made, output, sums, sent = tick(
            first, image, late, saved, made, output, sums, scalars, keep_index, in_vmem(line.gate(received[image])),
            rows_in, vectors, weights,
        )
        line.passed(sent)
        both = [(1, 0)] + ([(0, 1)] if first is not None else [])
        returned.append(lax.ppermute(sent, SECTION, both))
        if first is not None:
            received.append(returned[-1])

    def flat(name):
        array = saved[SAVED.index(name)] if name in SAVED else made[MADE.index(name)]
        return array.reshape(-1, array.shape[-1])

    total = images * lax.axis_size((DP, REP))
    side = lax.axis_index(REP).astype(jnp.int32)[None]
    near_first = strides_of(lax.axis_size(DP))
    far_first = near_first[1::-1] + near_first[2:]
    square, many = (width, width), hidden // width
    forwards, attentions = [1, 2], [1, 2]
    residual = [None] * images
    exchanges, outs = {}, {}

    def begin(name, pair, strides):
        line.passed(pair[0])
        exchanges[name] = Exchange(line, *pair, strides, total)

    def feed_forward():
        nonlocal made, output, sums
        image = forwards.pop(0)
        made, output, sums, residual[image] = late_feed_forward(
            image, (0, 1) if image == 1 else (2,), saved, made, output, sums, keep_count, in_vmem(line.gate(returned[image])),
            vectors, weights,
        )
        line.passed(residual[image])

    def attention():
        nonlocal made, sums
        image = attentions.pop(0)
        made, sums = late_attention(
            image, saved, made, sums, line.gate(residual[image]), keep_count, keep_index, vectors, weights
        )
        line.passed(sums)

    def grad_down():
        pair = down_gradient(side, keep_count, line.gate(saved[SAVED.index(M)]), rows_in, returned)
        begin(DOWN, pair, near_first)

    def grad_up():
        blocks = [(0, 1, column) for column in range(many)]
        begin(UP, weight_gradient(side, (line.gate(flat(C)), flat(GZ)), blocks, "grad_up"), far_first)

    def grad_query_value():
        exchanges[SUMS] = Total(line, sums, near_first)
        pair = weight_gradient(side, (line.gate(flat(A)), flat(GQKV)), [(0, 1, 0), (0, 1, 2)], "grad_query_value")
        begin(QUERY_VALUE, pair, near_first)

    def grad_key_out():
        arrays = (line.gate(flat(A)), flat(GQKV), flat(O), flat(GB))
        pair = weight_gradient(side, arrays, [(0, 1, 1), (2, 3, 0)], "grad_key_out")
        begin(KEY_OUT, pair, near_first)

    def widen(name):
        places, kinds = {
            DOWN: ([(0, k, 0) for k in range(many)], {DOWN: (hidden, width)}),
            UP: ([(0, 0, k) for k in range(many)], {UP: (width, hidden)}),
            QUERY_VALUE: ([(0, 0, 0), (0, 1, 0), (0, 0, 2), (0, 1, 2)], {QKV: (width, 3 * width)}),
            KEY_OUT: ([(0, 0, 1), (0, 1, 1), (1, 0, 0), (1, 1, 0)], {QKV: (width, 3 * width), OUT: (width, width)}),
        }[name]
        exchange = exchanges[name]
        before = [outs[kind] for kind in kinds if kind in outs]
        first, second = exchange.half
        wholes = assembled(
            exchange.at == stages - 1,
            exchange.strides[0],
            (first, line.gate(second)),
            places,
            list(kinds.values()),
            before,
        )
        line.passed(wholes[0])
        outs.update(zip(kinds, wholes))

    steps = dict(zip("FAGUQK", (feed_forward, attention, grad_down, grad_up, grad_query_value, grad_key_out)))
    transfers = dict(zip("duqks", (DOWN, UP, QUERY_VALUE, KEY_OUT, SUMS)))
    stages = 2 * len(near_first) + 2
    plain = "FAFAGUQK" + "duqk" * stages + "s" * (stages // 2)
    for step in ORDER if (images, stages) == (3, 8) else plain:
        if step in steps:
            steps[step]()
            continue
        name = transfers[step]
        exchanges[name].advance()
        if name != SUMS and exchanges[name].half is not None:
            widen(name)
    assert all(exchange.at == (stages // 2 if name == SUMS else stages) for name, exchange in exchanges.items())
    sums = exchanges[SUMS].value / total
    small = [sums[at : at + 1] for at in VECTORS[:-1]]
    return (
        output[None],
        made[MADE.index(GRAD)][None],
        small[GAIN_ONE],
        small[SHIFT_ONE],
        outs[QKV][None],
        small[BIAS_QUERY],
        small[BIAS_VALUE],
        outs[OUT][None],
        small[BIAS_OUT],
        small[GAIN_TWO],
        small[SHIFT_TWO],
        outs[UP][None],
        sums[BIAS_UP : BIAS_UP + many].reshape(1, -1),
        outs[DOWN][None],
        small[BIAS_DOWN],
    )


def solution(mesh):
    per_image = (DP, REP)
    matrix, line = P(SECTION, None, None), P(SECTION, None)
    rows = P(SECTION, per_image, None, None)
    kinds = (line, line, matrix, line, line, matrix, line, line, line, matrix, line, matrix, line)
    return jax.shard_map(
        shards,
        mesh=mesh,
        in_specs=(rows, P(per_image, None), P(per_image)) + kinds,
        out_specs=(rows, rows) + kinds,
        check_vma=False,
    )
```

```python
import functools
from functools import partial
import math

import jax
import jax.numpy as jnp
from jax import lax
from jax.experimental import pallas as pl
from jax.experimental.pallas import tpu as pltpu
from jax.sharding import PartitionSpec as P

HEAD_DIM = 64
PAIR = 2 * HEAD_DIM
ROW_TILE = 16
COLUMNS = 256

norm_eps = 1e-06
masked_score = -1e30
f32 = jnp.float32
bf16 = jnp.bfloat16

NN = (((1,), (0,)), ((), ()))
NT = (((1,), (1,)), ((), ()))
TN = (((0,), (0,)), ((), ()))

VECTORS = range(9)
GAIN_ONE, SHIFT_ONE, BIAS_QUERY, BIAS_VALUE, BIAS_OUT, GAIN_TWO, SHIFT_TWO, BIAS_DOWN, BIAS_UP = VECTORS
SECTION, DP, REP = "section", "dp", "rep"
U, A, QKV, O, R, C, M, SLOPE, GD, GZ, GB, GR, GO, GQKV, GA, GU, E, Y, GRAD = range(19)
WEIGHTS = range(19, 23)
W_QKV, W_OUT, W_UP, W_DOWN = WEIGHTS
DOWN, UP, QUERY_VALUE, KEY_OUT, SUMS, OUT = range(100, 106)
ORDER = "FAGFUduAQdKudqukdqsukqdskuqdkqkuqsdkdqusqkuk"
COST = 10**11
LATE_COST = 10**10
ANY = pl.BlockSpec(memory_space=pl.ANY)


def product(left, right, dims):
    return lax.dot_general(left, right, dims, preferred_element_type=f32)


def spans(size, step):
    return [slice(at, min(at + step, size)) for at in range(0, size, step)]


def column_sum(values):
    return jnp.sum(values, axis=0, keepdims=True)


def centre(values):
    centred = values - jnp.mean(values, axis=-1, keepdims=True)
    scale = lax.rsqrt(jnp.mean(centred * centred, axis=-1, keepdims=True) + norm_eps)
    return centred * scale, scale


class Copies:
    def __init__(self, sem, pairs):
        self.made = {
            name: pltpu.make_async_copy(source, target, sem.at[at])
            for at, (name, (source, target)) in enumerate(pairs.items())
        }

    def start(self, *names):
        for name in names or tuple(self.made):
            if name in self.made:
                self.made[name].start()

    def wait(self, *names):
        for name in names or tuple(self.made):
            if name in self.made:
                self.made.pop(name).wait()


def first_section():
    return lax.axis_index(SECTION) == 0


def row_mask(shape, count):
    return lax.broadcasted_iota(jnp.int32, shape, 0) < count


def gather_matrix(slots_of, count):
    slots = slots_of.shape[1]
    shape = (-(-slots // ROW_TILE) * ROW_TILE, slots)
    patch = lax.broadcasted_iota(jnp.int32, shape, 0)
    slot = lax.broadcasted_iota(jnp.int32, shape, 1)
    chosen = jnp.broadcast_to(slots_of, shape) == patch
    return jnp.where(chosen & (slot < count), 1.0, 0.0).astype(bf16)


def forward_part(r, wait, done, vec, weights, count):
    rows, width = r[U].shape[-2:]
    hidden = weights[W_UP].shape[1]
    for span in spans(rows, ROW_TILE):
        normal, _ = centre(r[U][span, :].astype(f32))
        r[A][span, :] = (normal * vec(GAIN_ONE) + vec(SHIFT_ONE)).astype(bf16)
    done(U, A)
    wait(W_QKV)
    for span in spans(3 * width, COLUMNS):
        packed = product(r[A][...], weights[W_QKV][:, span], NN)
        if span.start < width:
            packed = packed + vec(BIAS_QUERY, span)
        elif span.start >= 2 * width:
            packed = packed + vec(BIAS_VALUE, slice(span.start - 2 * width, span.stop - 2 * width))
        r[QKV][:, span] = packed.astype(bf16)
    done(QKV)
    low = (lax.broadcasted_iota(jnp.int32, (1, PAIR), 1) < HEAD_DIM).astype(bf16)
    lane = lax.broadcasted_iota(jnp.int32, (rows, PAIR), 1) < HEAD_DIM
    for at in range(0, width, PAIR):
        query = r[QKV][:, at : at + PAIR]
        key = r[QKV][:, width + at : width + at + PAIR]
        value = r[QKV][:, 2 * width + at : 2 * width + at + PAIR]
        both = jnp.concatenate([query * low, query * (1 - low)], axis=0)
        scores = product(both, key, NT) * (1.0 / math.sqrt(HEAD_DIM))
        live = lax.broadcasted_iota(jnp.int32, scores.shape, 1) < count
        scores = jnp.where(live, scores, masked_score)
        powers = jnp.exp(scores - jnp.max(scores, axis=-1, keepdims=True))
        chance = powers * (1.0 / jnp.sum(powers, axis=-1, keepdims=True))
        mixed = product(chance.astype(bf16), value, NN)
        r[O][:, at : at + PAIR] = jnp.where(lane, mixed[:rows], mixed[rows:]).astype(bf16)
    done(O)
    wait(W_OUT)
    for span in spans(width, COLUMNS):
        r[R][:, span] = r[U][:, span].astype(f32) + (
            product(r[O][...], weights[W_OUT][:, span], NN) + vec(BIAS_OUT, span)
        )
    for span in spans(rows, ROW_TILE):
        normal, _ = centre(r[R][span, :])
        r[C][span, :] = (normal * vec(GAIN_TWO) + vec(SHIFT_TWO)).astype(bf16)
    done(R, C)
    wait(W_UP)
    for span in spans(hidden, COLUMNS):
        z = product(r[C][...], weights[W_UP][:, span], NN) + vec(BIAS_UP, span)
        share = 0.5 * (1.0 + lax.erf(z * math.sqrt(0.5)))
        r[M][:, span] = (z * share).astype(bf16)
        r[SLOPE][:, span] = share + z * (jnp.exp(-0.5 * z * z) * (1.0 / math.sqrt(2 * math.pi)))
    done(M, SLOPE)


def output_part(r, vec, weights, count):
    rows, width = r[R].shape
    outer = r[Y].shape[0]
    for span in spans(width, COLUMNS):
        y = r[R][:, span] + (product(r[M][...], weights[W_DOWN][:, span], NN) + vec(BIAS_DOWN, span))
        r[Y][:, span] = jnp.where(row_mask(y.shape, count), y, 0.0).astype(bf16)[:outer]


def norm_back(normal, scale, gain, grad):
    x = grad * gain
    return scale * (
        x - jnp.mean(x, axis=-1, keepdims=True) - normal * jnp.mean(x * normal, axis=-1, keepdims=True)
    )


def feed_forward_back(r, wait, done, vec, weights, count, add):
    rows, width = r[R].shape
    hidden = weights[W_UP].shape[1]
    for span in spans(rows, ROW_TILE):
        live = lax.broadcasted_iota(jnp.int32, (ROW_TILE, width), 0) + span.start < count
        r[GD][span, :] = jnp.where(live, r[E][span, :], jnp.zeros((), bf16))
    add(BIAS_DOWN, lambda: column_sum(r[GD][...].astype(f32)))
    wait(W_DOWN, SLOPE)
    for span in spans(hidden, COLUMNS):
        gz = product(r[GD][...], weights[W_DOWN][span, :], NT) * r[SLOPE][:, span]
        r[GZ][:, span] = gz.astype(bf16)
        add(BIAS_UP, lambda: column_sum(r[GZ][:, span].astype(f32)), span)
    done(GZ)
    wait(W_UP, R)
    for span in spans(width, COLUMNS):
        r[GR][:, span] = product(r[GZ][...], weights[W_UP][span, :], NT)
    gain_sum, shift_sum = 0.0, 0.0
    for span in spans(rows, ROW_TILE):
        normal, scale = centre(r[R][span, :])
        gc = r[GR][span, :]
        gain_sum, shift_sum = gain_sum + gc * normal, shift_sum + gc
        gr = r[GD][span, :].astype(f32) + norm_back(normal, scale, vec(GAIN_TWO), gc)
        r[GR][span, :] = gr
        r[GB][span, :] = gr.astype(bf16)
    done(GB, GR)
    add(GAIN_TWO, lambda: column_sum(gain_sum))
    add(SHIFT_TWO, lambda: column_sum(shift_sum))
    add(BIAS_OUT, lambda: column_sum(r[GB][...].astype(f32)))


def attention_back(r, wait, done, vec, weights, count, add):
    rows, width = r[U].shape
    wait(GB, W_OUT)
    for span in spans(width, COLUMNS):
        r[GO][:, span] = product(r[GB][...], weights[W_OUT][span, :], NT).astype(bf16)
    wait(QKV)
    low = (lax.broadcasted_iota(jnp.int32, (1, PAIR), 1) < HEAD_DIM).astype(bf16)
    lane = lax.broadcasted_iota(jnp.int32, (rows, PAIR), 1) < HEAD_DIM
    score_scale = 1.0 / math.sqrt(HEAD_DIM)
    live = row_mask((rows, rows), count)
    for at in range(0, width, PAIR):
        query = r[QKV][:, at : at + PAIR]
        key = r[QKV][:, width + at : width + at + PAIR]
        value = r[QKV][:, 2 * width + at : 2 * width + at + PAIR]
        go = r[GO][:, at : at + PAIR]
        scores = product(jnp.concatenate([key * low, key * (1 - low)], axis=0), query, NT) * score_scale
        grads = product(jnp.concatenate([value * low, value * (1 - low)], axis=0), go, NT)
        chances, inner = [], []
        for head in range(2):
            score = jnp.where(live, scores[head * rows : (head + 1) * rows], masked_score)
            powers = jnp.exp(score - jnp.max(score, axis=0, keepdims=True))
            chance = powers * (1.0 / jnp.sum(powers, axis=0, keepdims=True))
            gp = grads[head * rows : (head + 1) * rows]
            gs = chance * (gp - jnp.sum(gp * chance, axis=0, keepdims=True))
            chances.append(chance.astype(bf16))
            inner.append(jnp.where(live, gs, 0.0).astype(bf16))
        gw = product(jnp.concatenate(chances, axis=0), go, NN)
        gk = product(jnp.concatenate(inner, axis=0), query, NN) * score_scale
        gq = [product(gs, key, TN) * score_scale for gs in inner]
        r[GQKV][:, at : at + PAIR] = jnp.where(lane, gq[0], gq[1]).astype(bf16)
        r[GQKV][:, width + at : width + at + PAIR] = jnp.where(lane, gk[:rows], gk[rows:]).astype(bf16)
        r[GQKV][:, 2 * width + at : 2 * width + at + PAIR] = jnp.where(lane, gw[:rows], gw[rows:]).astype(
            bf16
        )
    done(GQKV)
    add(BIAS_QUERY, lambda: column_sum(r[GQKV][:, :width].astype(f32)))
    add(BIAS_VALUE, lambda: column_sum(r[GQKV][:, 2 * width :].astype(f32)))
    wait(W_QKV, U, GR)
    for span in spans(width, COLUMNS):
        r[GA][:, span] = product(r[GQKV][...], weights[W_QKV][span, :], NT)
    gain_sum, shift_sum = 0.0, 0.0
    for span in spans(rows, ROW_TILE):
        normal, scale = centre(r[U][span, :].astype(f32))
        ga = r[GA][span, :]
        gain_sum, shift_sum = gain_sum + ga * normal, shift_sum + ga
        gu = r[GR][span, :] + norm_back(normal, scale, vec(GAIN_ONE), ga)
        r[GU][span, :] = gu.astype(bf16)
    add(GAIN_ONE, lambda: column_sum(gain_sum))
    add(SHIFT_ONE, lambda: column_sum(shift_sum))


def vector_reader(refs):
    named = dict(zip(VECTORS, refs))

    def vec(name, span=None):
        ref = named[name]
        return (ref[...] if span is None else ref[:, span]).astype(f32)

    return vec


def vector_adder(ref):
    def add(name, values, span=None):
        values = values()
        start = 0 if span is None else span.start
        row, start = VECTORS.index(name) + start // ref.shape[1], start % ref.shape[1]
        ref[row : row + 1, start : start + values.shape[1]] += values

    return add


def pad_rows(target, source):
    inner, rows = source.shape[0], target.shape[0]
    target[:inner, :] = source[...]
    if rows > inner:
        target[inner:, :] = jnp.zeros((rows - inner, target.shape[1]), target.dtype)


def padded_rows(slots):
    return -(-slots // ROW_TILE) * ROW_TILE


def image_block(shape, image):
    return pl.BlockSpec((pl.Squeezed(),) + tuple(shape), lambda *_: (image, 0, 0))


def fixed_block(shape):
    return pl.BlockSpec(tuple(shape), lambda *_: (0,) * len(shape))


def weight_scratch(weights):
    return [pltpu.VMEM(weight.shape, weight.dtype) for weight in weights] + [
        pltpu.SemaphoreType.DMA((len(weights),))
    ]


def fetch_weights(sem, hbm, local, order=WEIGHTS):
    found = dict(zip(WEIGHTS, zip(hbm, local)))
    return Copies(sem, {name: found[name] for name in order}), dict(zip(WEIGHTS, local))


def call(kernel, steps, scalars, ins, in_specs, outs, out_specs, scratch, name, aliases=None, room=60):
    return pl.pallas_call(
        kernel,
        out_shape=outs,
        grid_spec=pltpu.PrefetchScalarGridSpec(
            num_scalar_prefetch=1,
            grid=(steps,),
            in_specs=in_specs,
            out_specs=out_specs,
            scratch_shapes=scratch,
        ),
        compiler_params=pltpu.CompilerParams(
            dimension_semantics=("arbitrary",), vmem_limit_bytes=room << 20
        ),
        input_output_aliases=aliases or {},
        cost_estimate=pl.CostEstimate(flops=COST, bytes_accessed=COST, transcendentals=0),
        name=name,
    )(scalars, *ins)


def split(refs, *sizes):
    out, at = [], 0
    for size in sizes:
        out.append(refs[at] if size is None else refs[at : at + size])
        at += 1 if size is None else size
    assert at == len(refs)
    return out


def nothing(*_):
    return None


SAVED = (U, A, QKV, O, R, C, M, SLOPE)
MADE = (GZ, GB, GQKV, GRAD)


def image_shapes(slots, rows, width, hidden):
    narrow, wide = (rows, width), (rows, hidden)
    return {
        U: (narrow, bf16),
        A: (narrow, bf16),
        QKV: ((rows, 3 * width), bf16),
        O: (narrow, bf16),
        R: (narrow, f32),
        C: (narrow, bf16),
        M: (wide, bf16),
        SLOPE: (wide, f32),
        GD: (narrow, bf16),
        GZ: (wide, bf16),
        GB: (narrow, bf16),
        GR: (narrow, f32),
        GO: (narrow, bf16),
        GQKV: ((rows, 3 * width), bf16),
        GA: (narrow, f32),
        GU: (narrow, bf16),
        E: (narrow, bf16),
        Y: ((slots, width), bf16),
        GRAD: ((slots, width), bf16),
    }


def first_forward(image, carry, count, index, source, vectors, weights):
    images, slots, width = source.shape
    rows, hidden = padded_rows(slots), weights[2].shape[1]
    shapes = image_shapes(slots, rows, width, hidden)
    work = SAVED + (Y,)
    old = () if carry is None else tuple(carry)
    at = 1 + 2 + len(vectors) + 4

    def kernel(count_ref, index_ref, source_ref, *rest):
        vecs, hbm, _, places, y_ref, local, sem, scratch, padded, out_sem = split(
            rest, len(vectors), 4, len(old), len(work), None, 4, None, len(work), None, None
        )

        @pl.when(first_section())
        def _():
            fetch, near = fetch_weights(sem, hbm, local)
            fetch.start()
            kept = count_ref[image]
            refs = dict(zip(work, scratch))
            store = Copies(out_sem, {name: (refs[name], place.at[image]) for name, place in zip(work, places)})
            pad_rows(padded, source_ref)
            chosen = gather_matrix(index_ref[image : image + 1, :], kept)
            refs[U][:slots, :] = product(chosen, padded[...], TN).astype(bf16)
            refs[U][slots:, :] = jnp.zeros((rows - slots, width), bf16)
            vec = vector_reader(vecs)
            forward_part(refs, fetch.wait, store.start, vec, near, kept)
            fetch.wait(W_DOWN)
            output_part(refs, vec, near, kept)
            store.start(Y)
            y_ref[...] = refs[Y][...]
            store.wait()

    *carry, output = call(
        kernel,
        1,
        count,
        (index, source) + vectors + weights + old,
        [fixed_block(index.shape), image_block((slots, width), image)]
        + [fixed_block(vector.shape) for vector in vectors]
        + [ANY] * (4 + len(old)),
        [jax.ShapeDtypeStruct((images,) + shapes[name][0], shapes[name][1]) for name in work]
        + [jax.ShapeDtypeStruct((1, slots, width), bf16)],
        [ANY] * len(work) + [image_block((slots, width), 0)],
        weight_scratch(weights)
        + [pltpu.VMEM(*shapes[name]) for name in work]
        + [pltpu.VMEM((rows, width), bf16), pltpu.SemaphoreType.DMA((len(work),))],
        f"first_forward_{image}",
        {at + k: k for k in range(len(old))},
    )
    return carry, output


def tick(first, image, late, saved, made, output, sums, scalars, index, received, source, vectors, weights):
    images, slots, width = source.shape
    rows, hidden = padded_rows(slots), weights[2].shape[1]
    shapes = image_shapes(slots, rows, width, hidden)
    carry = SAVED + MADE + (Y,)
    lines = -(-(len(vectors) - 1 + hidden // width) // 8) * 8
    work = (E, GD, GR, GO, GA, GU) + carry
    old = tuple(saved) + (() if made is None else tuple(made)) + (output,) + (() if made is None else (sums,))
    slots_of = [k for k, name in enumerate(carry) if made is not None or name not in MADE]
    slots_of += [] if made is None else [len(carry)]
    at = 1 + 3 + len(vectors) + 4
    other = first if first is not None else late if late is not None else image

    def kernel(scalar_ref, index_ref, received_ref, source_ref, *rest):
        vecs, hbm, previous, places, sums_ref, send_ref, local, sem, scratch, out_sem = split(
            rest, len(vectors), 4, len(old), len(carry), None, None, 4, None, len(work), None
        )
        sums_ref[...] = jnp.zeros(sums_ref.shape, f32) if made is None else previous[-1][...]
        early = first_section()
        later = jnp.logical_not(early)
        here = jnp.where(early, other, image)
        live = scalar_ref[here]
        refs = dict(zip(work, scratch))
        place = {name: ref.at[here] for name, ref in zip(carry, places)}
        store = Copies(out_sem, {name: (refs[name], place[name]) for name in carry})
        vec, add = vector_reader(vecs), vector_adder(sums_ref)

        def gathered():
            pad_rows(refs[E], source_ref)
            chosen = gather_matrix(index_ref[first : first + 1, :], live)
            refs[U][:slots, :] = product(chosen, refs[E][...], TN).astype(bf16)
            refs[U][slots:, :] = jnp.zeros((rows - slots, width), bf16)

        def forward(fetch, near):
            forward_part(refs, fetch.wait, store.start, vec, near, live)
            fetch.wait(W_DOWN)

        def backward(near, wait=nothing):
            feed_forward_back(refs, wait, store.start, vec, near, live, add)
            attention_back(refs, wait, store.start, vec, near, live, add)

        def fetched():
            weights_in = fetch_weights(sem, hbm, local, (W_DOWN, W_UP, W_OUT, W_QKV))[0]
            return weights_in, Copies(out_sem, {name: (place[name], refs[name]) for name in (SLOPE, R, QKV, U)})

        def await_early(*names):
            @pl.when(early)
            def _():
                for copies in fetched():
                    copies.wait(*names)

        def sent():
            refs[GRAD][...] = refs[GU][:slots, :]
            store.start(GRAD)
            send_ref[...] = refs[GU][:slots, :]

        if first is not None:
            fetch, near = fetch_weights(sem, hbm, local)
            fetch.start()

            @pl.when(early)
            def _():
                gathered()

            @pl.when(later)
            def _():
                pad_rows(refs[U], received_ref.at[0])

            forward(fetch, near)

            @pl.when(early)
            def _():
                output_part(refs, vec, near, live)
                store.start(Y)
                send_ref[...] = refs[Y][...]
                Copies(out_sem, {name: (refs[name], place[name]) for name in carry}).wait(*SAVED, Y)

            @pl.when(later)
            def _():
                pad_rows(refs[E], source_ref)
                backward(near)
                sent()
                Copies(out_sem, {name: (refs[name], place[name]) for name in carry}).wait(*SAVED, *MADE)

            return

        @pl.when(later)
        def _():
            fetch, near = fetch_weights(sem, hbm, local)
            fetch.start()
            pad_rows(refs[U], received_ref.at[0])
            pad_rows(refs[E], source_ref)
            forward(fetch, near)
            if late is None:
                backward(near)
                sent()
                store.wait(*SAVED, *MADE)

        if late is None:
            return

        @pl.when(early)
        def _():
            for copies in fetched():
                copies.start()
            pad_rows(refs[E], received_ref.at[0])

        backward(dict(zip(WEIGHTS, local)), await_early)

        @pl.when(early)
        def _():
            chosen = gather_matrix(index_ref[late : late + 1, :], live)
            refs[GRAD][...] = product(chosen, refs[GU][:slots, :], NN)[:slots, :].astype(bf16)
            store.start(GRAD)

        @pl.when(later)
        def _():
            sent()
            Copies(out_sem, {name: (refs[name], place[name]) for name in SAVED}).wait()

        store.wait(*MADE)

    results = call(
        kernel,
        1,
        scalars,
        (index, received, source) + vectors + weights + old,
        [
            fixed_block(index.shape),
            pl.BlockSpec(memory_space=pltpu.VMEM),
            pl.BlockSpec(
                (pl.Squeezed(), slots, width), lambda i, s: (jnp.where(s[images] == 0, other, image), 0, 0)
            ),
        ]
        + [fixed_block(vector.shape) for vector in vectors]
        + [ANY] * (4 + len(old) - (made is not None))
        + ([] if made is None else [fixed_block(sums.shape)]),
        [jax.ShapeDtypeStruct((images,) + shapes[name][0], shapes[name][1]) for name in carry]
        + [jax.ShapeDtypeStruct((lines, width), f32), jax.ShapeDtypeStruct((1, slots, width), bf16)],
        [ANY] * len(carry) + [fixed_block((lines, width)), image_block((slots, width), 0)],
        weight_scratch(weights)
        + [pltpu.VMEM(*shapes[name]) for name in work]
        + [pltpu.SemaphoreType.DMA((len(carry),))],
        f"tick_{image}",
        {at + k: slot for k, slot in enumerate(slots_of)},
    )
    saved, made = results[: len(SAVED)], results[len(SAVED) : len(SAVED) + len(MADE)]
    return saved, made, results[-3], results[-2], results[-1]


def late_feed_forward(image, outputs, saved, made, output, sums, count, received, vectors, weights):
    images, rows, hidden = saved[SAVED.index(M)].shape
    slots, width = received.shape[1:]
    shapes = image_shapes(slots, rows, width, hidden)
    loads = (SLOPE, R, M)
    stores = (GZ, GB, Y)
    work = (SLOPE, R, M, E, GD, GZ, GB, Y)
    near_names = (W_DOWN, W_UP)
    old = [made[MADE.index(GZ)], made[MADE.index(GB)], output, sums]
    at = 1 + 1 + len(vectors) + len(loads) + len(near_names)

    def kernel(count_ref, received_ref, *rest):
        vecs, sources, hbm, previous, places, sums_ref, gr_ref, local, scratch, sem = split(
            rest, len(vectors), len(loads), 2, len(old), len(stores), None, None, 2, len(work), None
        )
        live = count_ref[image]
        refs = dict(zip(work, scratch)) | {GR: gr_ref}
        near = dict(zip(near_names, local))
        far = dict(zip(near_names, hbm))
        source = {name: ref.at[image] for name, ref in zip(loads, sources)}
        place = {name: ref.at[image] for name, ref in zip(stores, places)}
        vec = vector_reader(vecs)
        sums_ref[...] = previous[-1][...]
        early = first_section()

        @pl.when(early)
        def _():
            fetch = Copies(
                sem,
                {
                    W_DOWN: (far[W_DOWN], near[W_DOWN]),
                    SLOPE: (source[SLOPE], refs[SLOPE]),
                    W_UP: (far[W_UP], near[W_UP]),
                    R: (source[R], refs[R]),
                },
            )
            fetch.start()
            store = Copies(sem.at[pl.ds(5, 2)], {name: (refs[name], place[name]) for name in (GZ, GB)})
            pad_rows(refs[E], received_ref.at[0])
            feed_forward_back(refs, fetch.wait, store.start, vec, near, live, vector_adder(sums_ref))
            store.wait()

        @pl.when(jnp.logical_not(early))
        def _():
            fetch = Copies(sem, {W_DOWN: (far[W_DOWN], near[W_DOWN])})
            fetch.start()
            for which in outputs:
                load = Copies(
                    sem.at[pl.ds(1, 2)],
                    {name: (sources[loads.index(name)].at[which], refs[name]) for name in (R, M)},
                )
                load.start()
                fetch.wait()
                load.wait()
                output_part(refs, vec, near, count_ref[which])
                store = Copies(sem.at[pl.ds(4, 1)], {Y: (refs[Y], places[stores.index(Y)].at[which])})
                store.start()
                store.wait()

    gz, gb, output, sums, gr = call(
        kernel,
        1,
        count,
        (received,)
        + vectors
        + tuple(saved[SAVED.index(name)] for name in loads)
        + tuple(weights[WEIGHTS.index(name)] for name in near_names)
        + tuple(old),
        [pl.BlockSpec(memory_space=pltpu.VMEM)]
        + [fixed_block(vector.shape) for vector in vectors]
        + [ANY] * (len(loads) + len(near_names) + len(old) - 1)
        + [fixed_block(sums.shape)],
        [
            jax.ShapeDtypeStruct((images,) + shapes[GZ][0], bf16),
            jax.ShapeDtypeStruct((images,) + shapes[GB][0], bf16),
            jax.ShapeDtypeStruct((images,) + shapes[Y][0], bf16),
            jax.ShapeDtypeStruct(sums.shape, f32),
            jax.ShapeDtypeStruct((1,) + shapes[GR][0], f32),
        ],
        [ANY] * 3 + [fixed_block(sums.shape), image_block(shapes[GR][0], 0)],
        [pltpu.VMEM(weights[WEIGHTS.index(name)].shape, bf16) for name in near_names]
        + [pltpu.VMEM(*shapes[name]) for name in work]
        + [pltpu.SemaphoreType.DMA((7,))],
        f"late_feed_forward_{image}",
        {at + k: k for k in range(len(old))},
    )
    return [gz, gb] + list(made[2:]), output, sums, gr


def late_attention(image, saved, made, sums, gr, count, index, vectors, weights):
    images, slots, width = made[MADE.index(GRAD)].shape
    rows, hidden = saved[SAVED.index(M)].shape[1:]
    shapes = image_shapes(slots, rows, width, hidden)
    work = (GB, QKV, U, GO, GQKV, GA, GU, GRAD)
    near_names = (W_OUT, W_QKV)
    old = [made[MADE.index(GQKV)], made[MADE.index(GRAD)], sums]
    sources = (made[MADE.index(GB)], saved[SAVED.index(QKV)], saved[SAVED.index(U)])
    at = 1 + 2 + len(vectors) + len(sources) + len(near_names)

    def kernel(count_ref, index_ref, gr_ref, *rest):
        vecs, loads, hbm, previous, gqkv_ref, grad_ref, sums_ref, local, scratch, sem = split(
            rest, len(vectors), len(sources), 2, len(old), None, None, None, 2, len(work), None
        )
        live = count_ref[image]
        sums_ref[...] = previous[-1][...]
        refs = dict(zip(work, scratch)) | {GR: gr_ref}
        near = dict(zip(near_names, local))

        @pl.when(first_section())
        def _():
            fetch = Copies(
                sem,
                {
                    GB: (loads[0].at[image], refs[GB]),
                    W_OUT: (hbm[0], near[W_OUT]),
                    QKV: (loads[1].at[image], refs[QKV]),
                    W_QKV: (hbm[1], near[W_QKV]),
                    U: (loads[2].at[image], refs[U]),
                },
            )
            fetch.start()
            store = Copies(
                sem.at[pl.ds(5, 2)],
                {GQKV: (refs[GQKV], gqkv_ref.at[image]), GRAD: (refs[GRAD], grad_ref.at[image])},
            )
            attention_back(refs, fetch.wait, store.start, vector_reader(vecs), near, live, vector_adder(sums_ref))
            chosen = gather_matrix(index_ref[image : image + 1, :], live)
            refs[GRAD][...] = product(chosen, refs[GU][:slots, :], NN)[:slots, :].astype(bf16)
            store.start(GRAD)
            store.wait()

    gqkv, grad, sums = call(
        kernel,
        1,
        count,
        (index, gr)
        + vectors
        + sources
        + tuple(weights[WEIGHTS.index(name)] for name in near_names)
        + tuple(old),
        [fixed_block(index.shape), image_block((rows, width), 0)]
        + [fixed_block(vector.shape) for vector in vectors]
        + [ANY] * (len(sources) + len(near_names) + len(old) - 1)
        + [fixed_block(sums.shape)],
        [
            jax.ShapeDtypeStruct((images,) + shapes[GQKV][0], bf16),
            jax.ShapeDtypeStruct((images,) + shapes[GRAD][0], bf16),
            jax.ShapeDtypeStruct(sums.shape, f32),
        ],
        [ANY] * 2 + [fixed_block(sums.shape)],
        [pltpu.VMEM(weights[WEIGHTS.index(name)].shape, bf16) for name in near_names]
        + [pltpu.VMEM(*shapes[name]) for name in work]
        + [pltpu.SemaphoreType.DMA((7,))],
        f"late_attention_{image}",
        {at + k: k for k in range(len(old))},
    )
    return list(made[:2]) + [gqkv, grad], sums


def pick(table, at):
    value = table[0]
    for k in range(1, len(table)):
        value = jnp.where(at == k, table[k], value)
    return value


def weight_gradient(side, arrays, blocks, name):
    depth = arrays[0].shape[0]
    width = min(array.shape[1] for array in arrays)
    half = len(blocks) // 2

    def chosen(i, scalar_ref):
        bit = scalar_ref[0]
        return jnp.where(i < half, (1 - bit) * half + i, bit * half + i - half)

    def kernel(scalar_ref, *refs):
        send_ref, keep_ref = refs[-2:]
        step = pl.program_id(0)
        block = chosen(step, scalar_ref)
        for left, right in dict.fromkeys((left, right) for left, right, _ in blocks):
            here = functools.reduce(
                jnp.logical_or, [block == k for k, entry in enumerate(blocks) if entry[:2] == (left, right)]
            )

            @pl.when(here & (step < half))
            def _():
                send_ref[...] = product(refs[left][...], refs[right][...], TN).astype(bf16)

            @pl.when(here & (step >= half))
            def _():
                keep_ref[...] = product(refs[left][...], refs[right][...], TN).astype(bf16)

    def columns(at):
        table = [column if right == at else 0 for _, right, column in blocks]
        return pl.BlockSpec((depth, width), lambda i, s: (0, pick(table, chosen(i, s))))

    return call(
        kernel,
        2 * half,
        side,
        arrays,
        [columns(at) for at in range(len(arrays))],
        [jax.ShapeDtypeStruct((half * width, width), bf16)] * 2,
        [
            pl.BlockSpec((width, width), lambda i, s: (jnp.minimum(i, half - 1), 0)),
            pl.BlockSpec((width, width), lambda i, s: (jnp.maximum(i - half, 0), 0)),
        ],
        [],
        name,
        room=60,
    )


def down_gradient(side, count, m, cotangent, received):
    images, slots, width = cotangent.shape
    rows, hidden = m.shape[1:]
    blocks = hidden // width
    half = blocks // 2
    scalars = jnp.concatenate([side, count])

    def chosen(i, scalar_ref):
        bit = scalar_ref[0]
        return jnp.where(i < half, (1 - bit) * half + i, bit * half + i - half)

    def kernel(scalar_ref, m_ref, e_ref, *rest):
        arrived, (send_ref, keep_ref, gd_ref) = rest[:images], rest[images:]
        step = pl.program_id(0)
        early = first_section()

        @pl.when(step == 0)
        def _():
            for image in range(images):
                live = row_mask((slots, width), scalar_ref[1 + image])
                top = slice(image * rows, image * rows + slots)
                gd_ref[top, :] = jnp.where(live, jnp.where(early, arrived[image][...], e_ref[image]), jnp.zeros((), bf16))
                gd_ref[top.stop : (image + 1) * rows, :] = jnp.zeros((rows - slots, width), bf16)

        left = m_ref[...].reshape(images * rows, width)

        @pl.when(step < half)
        def _():
            send_ref[...] = product(left, gd_ref[...], TN).astype(bf16)

        @pl.when(step >= half)
        def _():
            keep_ref[...] = product(left, gd_ref[...], TN).astype(bf16)

    return call(
        kernel,
        blocks,
        scalars,
        (m, cotangent) + tuple(received),
        [
            pl.BlockSpec((images, rows, width), lambda i, s: (0, 0, chosen(i, s))),
            fixed_block(cotangent.shape),
        ]
        + [image_block((slots, width), 0)] * images,
        [jax.ShapeDtypeStruct((half * width, width), bf16)] * 2,
        [
            pl.BlockSpec((width, width), lambda i, s: (jnp.minimum(i, half - 1), 0)),
            pl.BlockSpec((width, width), lambda i, s: (jnp.maximum(i - half, 0), 0)),
        ],
        [pltpu.VMEM((images * rows, width), bf16)],
        "grad_down",
        room=60,
    )


def plain_call(kernel, ins, outs, name):
    return pl.pallas_call(
        kernel,
        out_shape=outs,
        in_specs=[pl.BlockSpec(memory_space=pltpu.VMEM)] * len(ins),
        out_specs=[pl.BlockSpec(memory_space=pltpu.VMEM)] * len(outs),
        compiler_params=pltpu.CompilerParams(vmem_limit_bytes=16 << 20),
        cost_estimate=pl.CostEstimate(flops=COST, bytes_accessed=COST, transcendentals=0),
        name=name,
    )(*(in_vmem(value) for value in ins))


def assembled(own, stride, pieces, places, shapes, before):
    shape = pieces[0].shape

    def kernel(*refs):
        sources, _, outs, (raw, wide, sem) = split(refs, 2, len(before), len(shapes), 3)
        core = lax.axis_index(REP) if own else 1 - lax.axis_index(REP)
        near = bit_of(DP, stride)
        loads = [pltpu.make_async_copy(source, raw.at[k], sem.at[k]) for k, source in enumerate(sources)]
        for load in loads:
            load.start()

        def stores(k, act):
            block = 2 * core + (near if k == 0 else 1 - near)
            for at, (which, row, column) in enumerate(places):
                rows, columns = pl.ds(row * shape[0], shape[0]), pl.ds(column * shape[1], shape[1])

                @pl.when(block == at)
                def _():
                    act(pltpu.make_async_copy(wide.at[k], outs[which].at[rows, columns], sem.at[2 + k]))

        for k in range(2):
            loads[k].wait()
            wide[k] = raw[k].astype(f32)
            stores(k, lambda copy: copy.start())
        for k in range(2):
            stores(k, lambda copy: copy.wait())

    return pl.pallas_call(
        kernel,
        out_shape=[jax.ShapeDtypeStruct(whole, f32) for whole in shapes],
        in_specs=[ANY] * (2 + len(before)),
        out_specs=[ANY] * len(shapes),
        scratch_shapes=[
            pltpu.VMEM((2,) + shape, bf16),
            pltpu.VMEM((2,) + shape, f32),
            pltpu.SemaphoreType.DMA((4,)),
        ],
        input_output_aliases={2 + k: k for k in range(len(before))},
        compiler_params=pltpu.CompilerParams(vmem_limit_bytes=16 << 20),
        cost_estimate=pl.CostEstimate(flops=LATE_COST, bytes_accessed=LATE_COST, transcendentals=0),
        name="assembled",
    )(*pieces, *before)


def in_vmem(value):
    return pltpu.with_memory_space_constraint(value, pltpu.VMEM)


def swapped(value, axis, stride):
    length = lax.axis_size(axis)
    return lax.ppermute(value, axis, [(i, i ^ stride) for i in range(length)])


def bit_of(axis, stride):
    return (lax.axis_index(axis) // stride) % 2


def halved(keep, coming, stride):
    height, width = keep.shape[0] // 2, keep.shape[1]
    if height % ROW_TILE:
        bit = bit_of(DP, stride)
        pair = (keep.astype(f32) + coming.astype(f32)).astype(bf16)
        send = lax.dynamic_slice_in_dim(pair, (1 - bit) * height, height, axis=0)
        return send, lax.dynamic_slice_in_dim(pair, bit * height, height, axis=0)

    def kernel(keep_ref, coming_ref, send_ref, stay_ref):
        bit = bit_of(DP, stride)
        for half, out_ref in ((1 - bit, send_ref), (bit, stay_ref)):
            rows = pl.ds(pl.multiple_of(half * height, ROW_TILE), height)
            out_ref[...] = (keep_ref[rows, :].astype(f32) + coming_ref[rows, :].astype(f32)).astype(bf16)

    shape = jax.ShapeDtypeStruct((height, width), bf16)
    return plain_call(kernel, (keep, coming), [shape] * 2, f"halved_{stride}")


def summed(keep, coming, total):
    if keep.shape[0] % ROW_TILE:
        return ((keep.astype(f32) + coming.astype(f32)) / total).astype(bf16)

    def kernel(keep_ref, coming_ref, out_ref):
        out_ref[...] = ((keep_ref[...].astype(f32) + coming_ref[...].astype(f32)) / total).astype(bf16)

    return plain_call(kernel, (keep, coming), [jax.ShapeDtypeStruct(keep.shape, bf16)], "summed")[0]


def joined(mine, other, stride):
    height, width = mine.shape
    if height % ROW_TILE:
        first = bit_of(DP, stride) == 0
        return jnp.concatenate([jnp.where(first, mine, other), jnp.where(first, other, mine)], axis=0)

    def kernel(mine_ref, other_ref, out_ref):
        bit = bit_of(DP, stride)
        for half, source in ((bit, mine_ref), (1 - bit, other_ref)):
            out_ref[pl.ds(pl.multiple_of(half * height, ROW_TILE), height), :] = source[...]

    shape = jax.ShapeDtypeStruct((2 * height, width), bf16)
    return plain_call(kernel, (mine, other), [shape], f"joined_{stride}")[0]


def strides_of(size):
    return [1 << at for at in range(size.bit_length() - 1)]


class Line:
    def __init__(self):
        self.last = None

    def gate(self, value):
        if self.last is None:
            return value
        return lax.optimization_barrier((value, self.last))[0]

    def passed(self, value):
        self.last = value


class Exchange:
    def __init__(self, line, send, keep, strides, total):
        self.line, self.keep, self.strides, self.total = line, keep, strides, total
        self.at, self.half = 0, None
        self.coming = swapped(send, REP, 1)

    def advance(self):
        coming = self.line.gate(self.coming)
        count = len(self.strides)
        if self.at < count:
            stride = self.strides[self.at]
            send, self.keep = halved(self.keep, coming, stride)
            self.coming = swapped(send, DP, stride)
            self.line.passed(send)
        elif self.at == count:
            self.value = summed(self.keep, coming, self.total)
            self.coming = swapped(self.value, DP, self.strides[-1])
            self.line.passed(self.value)
        elif self.at < 2 * count:
            self.value = joined(self.value, coming, self.strides[2 * count - self.at])
            self.coming = swapped(self.value, DP, self.strides[2 * count - 1 - self.at])
            self.line.passed(self.value)
        elif self.at == 2 * count:
            self.half = (self.value, coming)
            self.others = swapped(lax.optimization_barrier(self.half)[0], REP, 1)
            self.coming = swapped(coming, REP, 1)
        else:
            self.half = (self.others, coming)
        self.at += 1


def added(value, coming):
    def kernel(value_ref, coming_ref, out_ref):
        out_ref[...] = value_ref[...] + coming_ref[...]

    return pl.pallas_call(
        kernel,
        out_shape=jax.ShapeDtypeStruct(value.shape, value.dtype),
        cost_estimate=pl.CostEstimate(flops=LATE_COST, bytes_accessed=LATE_COST, transcendentals=0),
        name="added",
    )(value, coming)


class Total:
    def __init__(self, line, value, strides):
        self.line, self.value = line, value
        self.partners = [(REP, 1)] + [(DP, stride) for stride in strides]
        self.at = 0
        self.coming = swapped(value, *self.partners[0])

    def advance(self):
        self.value = added(self.value, self.line.gate(self.coming))
        self.at += 1
        if self.at < len(self.partners):
            self.coming = swapped(self.value, *self.partners[self.at])
        self.line.passed(self.value)


def shards(
    boundary,
    keep_index,
    keep_count,
    gain_one,
    shift_one,
    w_qkv,
    bias_query,
    bias_value,
    w_out,
    bias_out,
    gain_two,
    shift_two,
    w_up,
    bias_up,
    w_down,
    bias_down,
):
    images = keep_index.shape[0]
    width = boundary.shape[-1]
    weights = (w_qkv[0], w_out[0], w_up[0], w_down[0])
    hidden = weights[2].shape[1]
    vectors = (gain_one, shift_one, bias_query, bias_value, bias_out, gain_two, shift_two, bias_down, bias_up)
    rows_in = boundary[0]

    line = Line()
    assert images == 3
    section = lax.axis_index(SECTION).astype(jnp.int32)
    scalars = jnp.concatenate([keep_count, section[None]])
    carry, received = None, []
    for image in range(2):
        carry, first_output = first_forward(image, carry, keep_count, keep_index, rows_in, vectors, weights)
        received.append(lax.ppermute(first_output, SECTION, [(0, 1)]))
    saved, output = carry[:-1], carry[-1]
    made, sums, returned = None, None, []
    for image, first, late in ((0, 2, None), (1, None, None), (2, None, 0)):
        saved, made, output, sums, sent = tick(
            first, image, late, saved, made, output, sums, scalars, keep_index, in_vmem(line.gate(received[image])),
            rows_in, vectors, weights,
        )
        line.passed(sent)
        both = [(1, 0)] + ([(0, 1)] if first is not None else [])
        returned.append(lax.ppermute(sent, SECTION, both))
        if first is not None:
            received.append(returned[-1])

    def flat(name):
        array = saved[SAVED.index(name)] if name in SAVED else made[MADE.index(name)]
        return array.reshape(-1, array.shape[-1])

    total = images * lax.axis_size((DP, REP))
    side = lax.axis_index(REP).astype(jnp.int32)[None]
    near_first = strides_of(lax.axis_size(DP))
    far_first = near_first[1::-1] + near_first[2:]
    square, many = (width, width), hidden // width
    forwards, attentions = [1, 2], [1, 2]
    residual = [None] * images
    exchanges, outs = {}, {}

    def begin(name, pair, strides):
        line.passed(pair[0])
        exchanges[name] = Exchange(line, *pair, strides, total)

    def feed_forward():
        nonlocal made, output, sums
        image = forwards.pop(0)
        made, output, sums, residual[image] = late_feed_forward(
            image, (0, 1) if image == 1 else (2,), saved, made, output, sums, keep_count, in_vmem(line.gate(returned[image])),
            vectors, weights,
        )
        line.passed(residual[image])

    def attention():
        nonlocal made, sums
        image = attentions.pop(0)
        made, sums = late_attention(
            image, saved, made, sums, line.gate(residual[image]), keep_count, keep_index, vectors, weights
        )
        line.passed(sums)

    def grad_down():
        pair = down_gradient(side, keep_count, line.gate(saved[SAVED.index(M)]), rows_in, returned)
        begin(DOWN, pair, near_first)

    def grad_up():
        blocks = [(0, 1, column) for column in range(many)]
        begin(UP, weight_gradient(side, (line.gate(flat(C)), flat(GZ)), blocks, "grad_up"), far_first)

    def grad_query_value():
        exchanges[SUMS] = Total(line, sums, near_first)
        pair = weight_gradient(side, (line.gate(flat(A)), flat(GQKV)), [(0, 1, 0), (0, 1, 2)], "grad_query_value")
        begin(QUERY_VALUE, pair, near_first)

    def grad_key_out():
        arrays = (line.gate(flat(A)), flat(GQKV), flat(O), flat(GB))
        pair = weight_gradient(side, arrays, [(0, 1, 1), (2, 3, 0)], "grad_key_out")
        begin(KEY_OUT, pair, near_first)

    def widen(name):
        places, kinds = {
            DOWN: ([(0, k, 0) for k in range(many)], {DOWN: (hidden, width)}),
            UP: ([(0, 0, k) for k in range(many)], {UP: (width, hidden)}),
            QUERY_VALUE: ([(0, 0, 0), (0, 1, 0), (0, 0, 2), (0, 1, 2)], {QKV: (width, 3 * width)}),
            KEY_OUT: ([(0, 0, 1), (0, 1, 1), (1, 0, 0), (1, 1, 0)], {QKV: (width, 3 * width), OUT: (width, width)}),
        }[name]
        exchange = exchanges[name]
        before = [outs[kind] for kind in kinds if kind in outs]
        first, second = exchange.half
        wholes = assembled(
            exchange.at == stages - 1,
            exchange.strides[0],
            (first, line.gate(second)),
            places,
            list(kinds.values()),
            before,
        )
        line.passed(wholes[0])
        outs.update(zip(kinds, wholes))

    steps = dict(zip("FAGUQK", (feed_forward, attention, grad_down, grad_up, grad_query_value, grad_key_out)))
    transfers = dict(zip("duqks", (DOWN, UP, QUERY_VALUE, KEY_OUT, SUMS)))
    stages = 2 * len(near_first) + 2
    plain = "FAFAGUQK" + "duqk" * stages + "s" * (stages // 2)
    for step in ORDER if (images, stages) == (3, 8) else plain:
        if step in steps:
            steps[step]()
            continue
        name = transfers[step]
        exchanges[name].advance()
        if name != SUMS and exchanges[name].half is not None:
            widen(name)
    assert all(exchange.at == (stages // 2 if name == SUMS else stages) for name, exchange in exchanges.items())
    sums = exchanges[SUMS].value / total
    small = [sums[at : at + 1] for at in VECTORS[:-1]]
    return (
        output[None],
        made[MADE.index(GRAD)][None],
        small[GAIN_ONE],
        small[SHIFT_ONE],
        outs[QKV][None],
        small[BIAS_QUERY],
        small[BIAS_VALUE],
        outs[OUT][None],
        small[BIAS_OUT],
        small[GAIN_TWO],
        small[SHIFT_TWO],
        outs[UP][None],
        sums[BIAS_UP : BIAS_UP + many].reshape(1, -1),
        outs[DOWN][None],
        small[BIAS_DOWN],
    )


def solution(mesh):
    per_image = (DP, REP)
    matrix, line = P(SECTION, None, None), P(SECTION, None)
    rows = P(SECTION, per_image, None, None)
    kinds = (line, line, matrix, line, line, matrix, line, line, line, matrix, line, matrix, line)
    return jax.shard_map(
        shards,
        mesh=mesh,
        in_specs=(rows, P(per_image, None), P(per_image)) + kinds,
        out_specs=(rows, rows) + kinds,
        check_vma=False,
    )
```

```python
import functools
from functools import partial
import math

import jax
import jax.numpy as jnp
from jax import lax
from jax.experimental import pallas as pl
from jax.experimental.pallas import tpu as pltpu
from jax.sharding import PartitionSpec as P

HEAD_DIM = 64
PAIR = 2 * HEAD_DIM
ROW_TILE = 16
COLUMNS = 256

norm_eps = 1e-06
masked_score = -1e30
f32 = jnp.float32
bf16 = jnp.bfloat16

NN = (((1,), (0,)), ((), ()))
NT = (((1,), (1,)), ((), ()))
TN = (((0,), (0,)), ((), ()))

VECTORS = range(9)
GAIN_ONE, SHIFT_ONE, BIAS_QUERY, BIAS_VALUE, BIAS_OUT, GAIN_TWO, SHIFT_TWO, BIAS_DOWN, BIAS_UP = VECTORS
SECTION, DP, REP = "section", "dp", "rep"
U, A, QKV, O, R, C, M, SLOPE, GD, GZ, GB, GR, GO, GQKV, GA, GU, E, Y, GRAD = range(19)
WEIGHTS = range(19, 23)
W_QKV, W_OUT, W_UP, W_DOWN = WEIGHTS
DOWN, UP, QUERY_VALUE, KEY_OUT, SUMS, OUT = range(100, 106)
ORDER = "FAGFUduAQdKudqukdqsukqdskuqdskqkuqdkdqusqkuk"
COST = 10**11
LATE_COST = 10**10
ANY = pl.BlockSpec(memory_space=pl.ANY)


def product(left, right, dims):
    return lax.dot_general(left, right, dims, preferred_element_type=f32)


def spans(size, step):
    return [slice(at, min(at + step, size)) for at in range(0, size, step)]


def column_sum(values):
    return jnp.sum(values, axis=0, keepdims=True)


def centre(values):
    centred = values - jnp.mean(values, axis=-1, keepdims=True)
    scale = lax.rsqrt(jnp.mean(centred * centred, axis=-1, keepdims=True) + norm_eps)
    return centred * scale, scale


class Copies:
    def __init__(self, sem, pairs):
        self.made = {
            name: pltpu.make_async_copy(source, target, sem.at[at])
            for at, (name, (source, target)) in enumerate(pairs.items())
        }

    def start(self, *names):
        for name in names or tuple(self.made):
            if name in self.made:
                self.made[name].start()

    def wait(self, *names):
        for name in names or tuple(self.made):
            if name in self.made:
                self.made.pop(name).wait()


def first_section():
    return lax.axis_index(SECTION) == 0


def row_mask(shape, count):
    return lax.broadcasted_iota(jnp.int32, shape, 0) < count


def gather_matrix(slots_of, count):
    slots = slots_of.shape[1]
    shape = (-(-slots // ROW_TILE) * ROW_TILE, slots)
    patch = lax.broadcasted_iota(jnp.int32, shape, 0)
    slot = lax.broadcasted_iota(jnp.int32, shape, 1)
    chosen = jnp.broadcast_to(slots_of, shape) == patch
    return jnp.where(chosen & (slot < count), 1.0, 0.0).astype(bf16)


def forward_part(r, wait, done, vec, weights, count):
    rows, width = r[U].shape[-2:]
    hidden = weights[W_UP].shape[1]
    for span in spans(rows, ROW_TILE):
        normal, _ = centre(r[U][span, :].astype(f32))
        r[A][span, :] = (normal * vec(GAIN_ONE) + vec(SHIFT_ONE)).astype(bf16)
    done(U, A)
    wait(W_QKV)
    for span in spans(3 * width, COLUMNS):
        packed = product(r[A][...], weights[W_QKV][:, span], NN)
        if span.start < width:
            packed = packed + vec(BIAS_QUERY, span)
        elif span.start >= 2 * width:
            packed = packed + vec(BIAS_VALUE, slice(span.start - 2 * width, span.stop - 2 * width))
        r[QKV][:, span] = packed.astype(bf16)
    done(QKV)
    low = (lax.broadcasted_iota(jnp.int32, (1, PAIR), 1) < HEAD_DIM).astype(bf16)
    lane = lax.broadcasted_iota(jnp.int32, (rows, PAIR), 1) < HEAD_DIM
    for at in range(0, width, PAIR):
        query = r[QKV][:, at : at + PAIR]
        key = r[QKV][:, width + at : width + at + PAIR]
        value = r[QKV][:, 2 * width + at : 2 * width + at + PAIR]
        both = jnp.concatenate([query * low, query * (1 - low)], axis=0)
        scores = product(both, key, NT) * (1.0 / math.sqrt(HEAD_DIM))
        live = lax.broadcasted_iota(jnp.int32, scores.shape, 1) < count
        scores = jnp.where(live, scores, masked_score)
        powers = jnp.exp(scores - jnp.max(scores, axis=-1, keepdims=True))
        chance = powers * (1.0 / jnp.sum(powers, axis=-1, keepdims=True))
        mixed = product(chance.astype(bf16), value, NN)
        r[O][:, at : at + PAIR] = jnp.where(lane, mixed[:rows], mixed[rows:]).astype(bf16)
    done(O)
    wait(W_OUT)
    for span in spans(width, COLUMNS):
        r[R][:, span] = r[U][:, span].astype(f32) + (
            product(r[O][...], weights[W_OUT][:, span], NN) + vec(BIAS_OUT, span)
        )
    for span in spans(rows, ROW_TILE):
        normal, _ = centre(r[R][span, :])
        r[C][span, :] = (normal * vec(GAIN_TWO) + vec(SHIFT_TWO)).astype(bf16)
    done(R, C)
    wait(W_UP)
    for span in spans(hidden, COLUMNS):
        z = product(r[C][...], weights[W_UP][:, span], NN) + vec(BIAS_UP, span)
        share = 0.5 * (1.0 + lax.erf(z * math.sqrt(0.5)))
        r[M][:, span] = (z * share).astype(bf16)
        r[SLOPE][:, span] = share + z * (jnp.exp(-0.5 * z * z) * (1.0 / math.sqrt(2 * math.pi)))
    done(M, SLOPE)


def output_part(r, vec, weights, count):
    rows, width = r[R].shape
    outer = r[Y].shape[0]
    for span in spans(width, COLUMNS):
        y = r[R][:, span] + (product(r[M][...], weights[W_DOWN][:, span], NN) + vec(BIAS_DOWN, span))
        r[Y][:, span] = jnp.where(row_mask(y.shape, count), y, 0.0).astype(bf16)[:outer]


def norm_back(normal, scale, gain, grad):
    x = grad * gain
    return scale * (
        x - jnp.mean(x, axis=-1, keepdims=True) - normal * jnp.mean(x * normal, axis=-1, keepdims=True)
    )


def feed_forward_back(r, wait, done, vec, weights, count, add):
    rows, width = r[R].shape
    hidden = weights[W_UP].shape[1]
    for span in spans(rows, ROW_TILE):
        live = lax.broadcasted_iota(jnp.int32, (ROW_TILE, width), 0) + span.start < count
        r[GD][span, :] = jnp.where(live, r[E][span, :], jnp.zeros((), bf16))
    add(BIAS_DOWN, lambda: column_sum(r[GD][...].astype(f32)))
    wait(W_DOWN, SLOPE)
    for span in spans(hidden, COLUMNS):
        gz = product(r[GD][...], weights[W_DOWN][span, :], NT) * r[SLOPE][:, span]
        r[GZ][:, span] = gz.astype(bf16)
        add(BIAS_UP, lambda: column_sum(r[GZ][:, span].astype(f32)), span)
    done(GZ)
    wait(W_UP, R)
    for span in spans(width, COLUMNS):
        r[GR][:, span] = product(r[GZ][...], weights[W_UP][span, :], NT)
    gain_sum, shift_sum = 0.0, 0.0
    for span in spans(rows, ROW_TILE):
        normal, scale = centre(r[R][span, :])
        gc = r[GR][span, :]
        gain_sum, shift_sum = gain_sum + gc * normal, shift_sum + gc
        gr = r[GD][span, :].astype(f32) + norm_back(normal, scale, vec(GAIN_TWO), gc)
        r[GR][span, :] = gr
        r[GB][span, :] = gr.astype(bf16)
    done(GB, GR)
    add(GAIN_TWO, lambda: column_sum(gain_sum))
    add(SHIFT_TWO, lambda: column_sum(shift_sum))
    add(BIAS_OUT, lambda: column_sum(r[GB][...].astype(f32)))


def attention_back(r, wait, done, vec, weights, count, add):
    rows, width = r[U].shape
    wait(GB, W_OUT)
    for span in spans(width, COLUMNS):
        r[GO][:, span] = product(r[GB][...], weights[W_OUT][span, :], NT).astype(bf16)
    wait(QKV)
    low = (lax.broadcasted_iota(jnp.int32, (1, PAIR), 1) < HEAD_DIM).astype(bf16)
    lane = lax.broadcasted_iota(jnp.int32, (rows, PAIR), 1) < HEAD_DIM
    score_scale = 1.0 / math.sqrt(HEAD_DIM)
    live = row_mask((rows, rows), count)
    for at in range(0, width, PAIR):
        query = r[QKV][:, at : at + PAIR]
        key = r[QKV][:, width + at : width + at + PAIR]
        value = r[QKV][:, 2 * width + at : 2 * width + at + PAIR]
        go = r[GO][:, at : at + PAIR]
        scores = product(jnp.concatenate([key * low, key * (1 - low)], axis=0), query, NT) * score_scale
        grads = product(jnp.concatenate([value * low, value * (1 - low)], axis=0), go, NT)
        chances, inner = [], []
        for head in range(2):
            score = jnp.where(live, scores[head * rows : (head + 1) * rows], masked_score)
            powers = jnp.exp(score - jnp.max(score, axis=0, keepdims=True))
            chance = powers * (1.0 / jnp.sum(powers, axis=0, keepdims=True))
            gp = grads[head * rows : (head + 1) * rows]
            gs = chance * (gp - jnp.sum(gp * chance, axis=0, keepdims=True))
            chances.append(chance.astype(bf16))
            inner.append(jnp.where(live, gs, 0.0).astype(bf16))
        gw = product(jnp.concatenate(chances, axis=0), go, NN)
        gk = product(jnp.concatenate(inner, axis=0), query, NN) * score_scale
        gq = [product(gs, key, TN) * score_scale for gs in inner]
        r[GQKV][:, at : at + PAIR] = jnp.where(lane, gq[0], gq[1]).astype(bf16)
        r[GQKV][:, width + at : width + at + PAIR] = jnp.where(lane, gk[:rows], gk[rows:]).astype(bf16)
        r[GQKV][:, 2 * width + at : 2 * width + at + PAIR] = jnp.where(lane, gw[:rows], gw[rows:]).astype(
            bf16
        )
    done(GQKV)
    add(BIAS_QUERY, lambda: column_sum(r[GQKV][:, :width].astype(f32)))
    add(BIAS_VALUE, lambda: column_sum(r[GQKV][:, 2 * width :].astype(f32)))
    wait(W_QKV, U, GR)
    for span in spans(width, COLUMNS):
        r[GA][:, span] = product(r[GQKV][...], weights[W_QKV][span, :], NT)
    gain_sum, shift_sum = 0.0, 0.0
    for span in spans(rows, ROW_TILE):
        normal, scale = centre(r[U][span, :].astype(f32))
        ga = r[GA][span, :]
        gain_sum, shift_sum = gain_sum + ga * normal, shift_sum + ga
        gu = r[GR][span, :] + norm_back(normal, scale, vec(GAIN_ONE), ga)
        r[GU][span, :] = gu.astype(bf16)
    add(GAIN_ONE, lambda: column_sum(gain_sum))
    add(SHIFT_ONE, lambda: column_sum(shift_sum))


def vector_reader(refs):
    named = dict(zip(VECTORS, refs))

    def vec(name, span=None):
        ref = named[name]
        return (ref[...] if span is None else ref[:, span]).astype(f32)

    return vec


def vector_adder(ref):
    def add(name, values, span=None):
        values = values()
        start = 0 if span is None else span.start
        row, start = VECTORS.index(name) + start // ref.shape[1], start % ref.shape[1]
        ref[row : row + 1, start : start + values.shape[1]] += values

    return add


def pad_rows(target, source):
    inner, rows = source.shape[0], target.shape[0]
    target[:inner, :] = source[...]
    if rows > inner:
        target[inner:, :] = jnp.zeros((rows - inner, target.shape[1]), target.dtype)


def padded_rows(slots):
    return -(-slots // ROW_TILE) * ROW_TILE


def image_block(shape, image):
    return pl.BlockSpec((pl.Squeezed(),) + tuple(shape), lambda *_: (image, 0, 0))


def fixed_block(shape):
    return pl.BlockSpec(tuple(shape), lambda *_: (0,) * len(shape))


def weight_scratch(weights):
    return [pltpu.VMEM(weight.shape, weight.dtype) for weight in weights] + [
        pltpu.SemaphoreType.DMA((len(weights),))
    ]


def fetch_weights(sem, hbm, local, order=WEIGHTS):
    found = dict(zip(WEIGHTS, zip(hbm, local)))
    return Copies(sem, {name: found[name] for name in order}), dict(zip(WEIGHTS, local))


def call(kernel, steps, scalars, ins, in_specs, outs, out_specs, scratch, name, aliases=None, room=60):
    return pl.pallas_call(
        kernel,
        out_shape=outs,
        grid_spec=pltpu.PrefetchScalarGridSpec(
            num_scalar_prefetch=1,
            grid=(steps,),
            in_specs=in_specs,
            out_specs=out_specs,
            scratch_shapes=scratch,
        ),
        compiler_params=pltpu.CompilerParams(
            dimension_semantics=("arbitrary",), vmem_limit_bytes=room << 20
        ),
        input_output_aliases=aliases or {},
        cost_estimate=pl.CostEstimate(flops=COST, bytes_accessed=COST, transcendentals=0),
        name=name,
    )(scalars, *ins)


def split(refs, *sizes):
    out, at = [], 0
    for size in sizes:
        out.append(refs[at] if size is None else refs[at : at + size])
        at += 1 if size is None else size
    assert at == len(refs)
    return out


def nothing(*_):
    return None


SAVED = (U, A, QKV, O, R, C, M, SLOPE)
MADE = (GZ, GB, GQKV, GRAD)


def image_shapes(slots, rows, width, hidden):
    narrow, wide = (rows, width), (rows, hidden)
    return {
        U: (narrow, bf16),
        A: (narrow, bf16),
        QKV: ((rows, 3 * width), bf16),
        O: (narrow, bf16),
        R: (narrow, f32),
        C: (narrow, bf16),
        M: (wide, bf16),
        SLOPE: (wide, f32),
        GD: (narrow, bf16),
        GZ: (wide, bf16),
        GB: (narrow, bf16),
        GR: (narrow, f32),
        GO: (narrow, bf16),
        GQKV: ((rows, 3 * width), bf16),
        GA: (narrow, f32),
        GU: (narrow, bf16),
        E: (narrow, bf16),
        Y: ((slots, width), bf16),
        GRAD: ((slots, width), bf16),
    }


def first_forward(image, carry, count, index, source, vectors, weights):
    images, slots, width = source.shape
    rows, hidden = padded_rows(slots), weights[2].shape[1]
    shapes = image_shapes(slots, rows, width, hidden)
    work = SAVED + (Y,)
    old = () if carry is None else tuple(carry)
    at = 1 + 2 + len(vectors) + 4

    def kernel(count_ref, index_ref, source_ref, *rest):
        vecs, hbm, _, places, y_ref, local, sem, scratch, padded, out_sem = split(
            rest, len(vectors), 4, len(old), len(work), None, 4, None, len(work), None, None
        )

        @pl.when(first_section())
        def _():
            fetch, near = fetch_weights(sem, hbm, local)
            fetch.start()
            kept = count_ref[image]
            refs = dict(zip(work, scratch))
            store = Copies(out_sem, {name: (refs[name], place.at[image]) for name, place in zip(work, places)})
            pad_rows(padded, source_ref)
            chosen = gather_matrix(index_ref[image : image + 1, :], kept)
            refs[U][:slots, :] = product(chosen, padded[...], TN).astype(bf16)
            refs[U][slots:, :] = jnp.zeros((rows - slots, width), bf16)
            vec = vector_reader(vecs)
            forward_part(refs, fetch.wait, store.start, vec, near, kept)
            fetch.wait(W_DOWN)
            output_part(refs, vec, near, kept)
            store.start(Y)
            y_ref[...] = refs[Y][...]
            store.wait()

    *carry, output = call(
        kernel,
        1,
        count,
        (index, source) + vectors + weights + old,
        [fixed_block(index.shape), image_block((slots, width), image)]
        + [fixed_block(vector.shape) for vector in vectors]
        + [ANY] * (4 + len(old)),
        [jax.ShapeDtypeStruct((images,) + shapes[name][0], shapes[name][1]) for name in work]
        + [jax.ShapeDtypeStruct((1, slots, width), bf16)],
        [ANY] * len(work) + [image_block((slots, width), 0)],
        weight_scratch(weights)
        + [pltpu.VMEM(*shapes[name]) for name in work]
        + [pltpu.VMEM((rows, width), bf16), pltpu.SemaphoreType.DMA((len(work),))],
        f"first_forward_{image}",
        {at + k: k for k in range(len(old))},
    )
    return carry, output


def tick(first, image, late, saved, made, output, sums, scalars, index, received, source, vectors, weights):
    images, slots, width = source.shape
    rows, hidden = padded_rows(slots), weights[2].shape[1]
    shapes = image_shapes(slots, rows, width, hidden)
    carry = SAVED + MADE + (Y,)
    lines = -(-(len(vectors) - 1 + hidden // width) // 8) * 8
    work = (E, GD, GR, GO, GA, GU) + carry
    old = tuple(saved) + (() if made is None else tuple(made)) + (output,) + (() if made is None else (sums,))
    slots_of = [k for k, name in enumerate(carry) if made is not None or name not in MADE]
    slots_of += [] if made is None else [len(carry)]
    at = 1 + 3 + len(vectors) + 4
    other = first if first is not None else late if late is not None else image

    def kernel(scalar_ref, index_ref, received_ref, source_ref, *rest):
        vecs, hbm, previous, places, sums_ref, send_ref, local, sem, scratch, out_sem = split(
            rest, len(vectors), 4, len(old), len(carry), None, None, 4, None, len(work), None
        )
        sums_ref[...] = jnp.zeros(sums_ref.shape, f32) if made is None else previous[-1][...]
        early = first_section()
        later = jnp.logical_not(early)
        here = jnp.where(early, other, image)
        live = scalar_ref[here]
        refs = dict(zip(work, scratch))
        place = {name: ref.at[here] for name, ref in zip(carry, places)}
        store = Copies(out_sem, {name: (refs[name], place[name]) for name in carry})
        vec, add = vector_reader(vecs), vector_adder(sums_ref)

        def gathered():
            pad_rows(refs[E], source_ref)
            chosen = gather_matrix(index_ref[first : first + 1, :], live)
            refs[U][:slots, :] = product(chosen, refs[E][...], TN).astype(bf16)
            refs[U][slots:, :] = jnp.zeros((rows - slots, width), bf16)

        def forward(fetch, near):
            forward_part(refs, fetch.wait, store.start, vec, near, live)
            fetch.wait(W_DOWN)

        def backward(near, wait=nothing):
            feed_forward_back(refs, wait, store.start, vec, near, live, add)
            attention_back(refs, wait, store.start, vec, near, live, add)

        def fetched():
            weights_in = fetch_weights(sem, hbm, local, (W_DOWN, W_UP, W_OUT, W_QKV))[0]
            return weights_in, Copies(out_sem, {name: (place[name], refs[name]) for name in (SLOPE, R, QKV, U)})

        def await_early(*names):
            @pl.when(early)
            def _():
                for copies in fetched():
                    copies.wait(*names)

        def sent():
            refs[GRAD][...] = refs[GU][:slots, :]
            store.start(GRAD)
            send_ref[...] = refs[GU][:slots, :]

        if first is not None:
            fetch, near = fetch_weights(sem, hbm, local)
            fetch.start()

            @pl.when(early)
            def _():
                gathered()

            @pl.when(later)
            def _():
                pad_rows(refs[U], received_ref.at[0])

            forward(fetch, near)

            @pl.when(early)
            def _():
                output_part(refs, vec, near, live)
                store.start(Y)
                send_ref[...] = refs[Y][...]
                Copies(out_sem, {name: (refs[name], place[name]) for name in carry}).wait(*SAVED, Y)

            @pl.when(later)
            def _():
                pad_rows(refs[E], source_ref)
                backward(near)
                sent()
                Copies(out_sem, {name: (refs[name], place[name]) for name in carry}).wait(*SAVED, *MADE)

            return

        @pl.when(later)
        def _():
            fetch, near = fetch_weights(sem, hbm, local)
            fetch.start()
            pad_rows(refs[U], received_ref.at[0])
            pad_rows(refs[E], source_ref)
            forward(fetch, near)
            if late is None:
                backward(near)
                sent()
                store.wait(*SAVED, *MADE)

        if late is None:
            return

        @pl.when(early)
        def _():
            for copies in fetched():
                copies.start()
            pad_rows(refs[E], received_ref.at[0])

        backward(dict(zip(WEIGHTS, local)), await_early)

        @pl.when(early)
        def _():
            chosen = gather_matrix(index_ref[late : late + 1, :], live)
            refs[GRAD][...] = product(chosen, refs[GU][:slots, :], NN)[:slots, :].astype(bf16)
            store.start(GRAD)

        @pl.when(later)
        def _():
            sent()
            Copies(out_sem, {name: (refs[name], place[name]) for name in SAVED}).wait()

        store.wait(*MADE)

    results = call(
        kernel,
        1,
        scalars,
        (index, received, source) + vectors + weights + old,
        [
            fixed_block(index.shape),
            pl.BlockSpec(memory_space=pltpu.VMEM),
            pl.BlockSpec(
                (pl.Squeezed(), slots, width), lambda i, s: (jnp.where(s[images] == 0, other, image), 0, 0)
            ),
        ]
        + [fixed_block(vector.shape) for vector in vectors]
        + [ANY] * (4 + len(old) - (made is not None))
        + ([] if made is None else [fixed_block(sums.shape)]),
        [jax.ShapeDtypeStruct((images,) + shapes[name][0], shapes[name][1]) for name in carry]
        + [jax.ShapeDtypeStruct((lines, width), f32), jax.ShapeDtypeStruct((1, slots, width), bf16)],
        [ANY] * len(carry) + [fixed_block((lines, width)), image_block((slots, width), 0)],
        weight_scratch(weights)
        + [pltpu.VMEM(*shapes[name]) for name in work]
        + [pltpu.SemaphoreType.DMA((len(carry),))],
        f"tick_{image}",
        {at + k: slot for k, slot in enumerate(slots_of)},
    )
    saved, made = results[: len(SAVED)], results[len(SAVED) : len(SAVED) + len(MADE)]
    return saved, made, results[-3], results[-2], results[-1]


def late_feed_forward(image, outputs, saved, made, output, sums, count, received, vectors, weights):
    images, rows, hidden = saved[SAVED.index(M)].shape
    slots, width = received.shape[1:]
    shapes = image_shapes(slots, rows, width, hidden)
    loads = (SLOPE, R, M)
    stores = (GZ, GB, Y)
    work = (SLOPE, R, M, E, GD, GZ, GB, Y)
    near_names = (W_DOWN, W_UP)
    old = [made[MADE.index(GZ)], made[MADE.index(GB)], output, sums]
    at = 1 + 1 + len(vectors) + len(loads) + len(near_names)

    def kernel(count_ref, received_ref, *rest):
        vecs, sources, hbm, previous, places, sums_ref, gr_ref, local, scratch, sem = split(
            rest, len(vectors), len(loads), 2, len(old), len(stores), None, None, 2, len(work), None
        )
        live = count_ref[image]
        refs = dict(zip(work, scratch)) | {GR: gr_ref}
        near = dict(zip(near_names, local))
        far = dict(zip(near_names, hbm))
        source = {name: ref.at[image] for name, ref in zip(loads, sources)}
        place = {name: ref.at[image] for name, ref in zip(stores, places)}
        vec = vector_reader(vecs)
        sums_ref[...] = previous[-1][...]
        early = first_section()

        @pl.when(early)
        def _():
            fetch = Copies(
                sem,
                {
                    W_DOWN: (far[W_DOWN], near[W_DOWN]),
                    SLOPE: (source[SLOPE], refs[SLOPE]),
                    W_UP: (far[W_UP], near[W_UP]),
                    R: (source[R], refs[R]),
                },
            )
            fetch.start()
            store = Copies(sem.at[pl.ds(5, 2)], {name: (refs[name], place[name]) for name in (GZ, GB)})
            pad_rows(refs[E], received_ref.at[0])
            feed_forward_back(refs, fetch.wait, store.start, vec, near, live, vector_adder(sums_ref))
            store.wait()

        @pl.when(jnp.logical_not(early))
        def _():
            fetch = Copies(sem, {W_DOWN: (far[W_DOWN], near[W_DOWN])})
            fetch.start()
            for which in outputs:
                load = Copies(
                    sem.at[pl.ds(1, 2)],
                    {name: (sources[loads.index(name)].at[which], refs[name]) for name in (R, M)},
                )
                load.start()
                fetch.wait()
                load.wait()
                output_part(refs, vec, near, count_ref[which])
                store = Copies(sem.at[pl.ds(4, 1)], {Y: (refs[Y], places[stores.index(Y)].at[which])})
                store.start()
                store.wait()

    gz, gb, output, sums, gr = call(
        kernel,
        1,
        count,
        (received,)
        + vectors
        + tuple(saved[SAVED.index(name)] for name in loads)
        + tuple(weights[WEIGHTS.index(name)] for name in near_names)
        + tuple(old),
        [pl.BlockSpec(memory_space=pltpu.VMEM)]
        + [fixed_block(vector.shape) for vector in vectors]
        + [ANY] * (len(loads) + len(near_names) + len(old) - 1)
        + [fixed_block(sums.shape)],
        [
            jax.ShapeDtypeStruct((images,) + shapes[GZ][0], bf16),
            jax.ShapeDtypeStruct((images,) + shapes[GB][0], bf16),
            jax.ShapeDtypeStruct((images,) + shapes[Y][0], bf16),
            jax.ShapeDtypeStruct(sums.shape, f32),
            jax.ShapeDtypeStruct((1,) + shapes[GR][0], f32),
        ],
        [ANY] * 3 + [fixed_block(sums.shape), image_block(shapes[GR][0], 0)],
        [pltpu.VMEM(weights[WEIGHTS.index(name)].shape, bf16) for name in near_names]
        + [pltpu.VMEM(*shapes[name]) for name in work]
        + [pltpu.SemaphoreType.DMA((7,))],
        f"late_feed_forward_{image}",
        {at + k: k for k in range(len(old))},
    )
    return [gz, gb] + list(made[2:]), output, sums, gr


def late_attention(image, saved, made, sums, gr, count, index, vectors, weights):
    images, slots, width = made[MADE.index(GRAD)].shape
    rows, hidden = saved[SAVED.index(M)].shape[1:]
    shapes = image_shapes(slots, rows, width, hidden)
    work = (GB, QKV, U, GO, GQKV, GA, GU, GRAD)
    near_names = (W_OUT, W_QKV)
    old = [made[MADE.index(GQKV)], made[MADE.index(GRAD)], sums]
    sources = (made[MADE.index(GB)], saved[SAVED.index(QKV)], saved[SAVED.index(U)])
    at = 1 + 2 + len(vectors) + len(sources) + len(near_names)

    def kernel(count_ref, index_ref, gr_ref, *rest):
        vecs, loads, hbm, previous, gqkv_ref, grad_ref, sums_ref, local, scratch, sem = split(
            rest, len(vectors), len(sources), 2, len(old), None, None, None, 2, len(work), None
        )
        live = count_ref[image]
        sums_ref[...] = previous[-1][...]
        refs = dict(zip(work, scratch)) | {GR: gr_ref}
        near = dict(zip(near_names, local))

        @pl.when(first_section())
        def _():
            fetch = Copies(
                sem,
                {
                    GB: (loads[0].at[image], refs[GB]),
                    W_OUT: (hbm[0], near[W_OUT]),
                    QKV: (loads[1].at[image], refs[QKV]),
                    W_QKV: (hbm[1], near[W_QKV]),
                    U: (loads[2].at[image], refs[U]),
                },
            )
            fetch.start()
            store = Copies(
                sem.at[pl.ds(5, 2)],
                {GQKV: (refs[GQKV], gqkv_ref.at[image]), GRAD: (refs[GRAD], grad_ref.at[image])},
            )
            attention_back(refs, fetch.wait, store.start, vector_reader(vecs), near, live, vector_adder(sums_ref))
            chosen = gather_matrix(index_ref[image : image + 1, :], live)
            refs[GRAD][...] = product(chosen, refs[GU][:slots, :], NN)[:slots, :].astype(bf16)
            store.start(GRAD)
            store.wait()

    gqkv, grad, sums = call(
        kernel,
        1,
        count,
        (index, gr)
        + vectors
        + sources
        + tuple(weights[WEIGHTS.index(name)] for name in near_names)
        + tuple(old),
        [fixed_block(index.shape), image_block((rows, width), 0)]
        + [fixed_block(vector.shape) for vector in vectors]
        + [ANY] * (len(sources) + len(near_names) + len(old) - 1)
        + [fixed_block(sums.shape)],
        [
            jax.ShapeDtypeStruct((images,) + shapes[GQKV][0], bf16),
            jax.ShapeDtypeStruct((images,) + shapes[GRAD][0], bf16),
            jax.ShapeDtypeStruct(sums.shape, f32),
        ],
        [ANY] * 2 + [fixed_block(sums.shape)],
        [pltpu.VMEM(weights[WEIGHTS.index(name)].shape, bf16) for name in near_names]
        + [pltpu.VMEM(*shapes[name]) for name in work]
        + [pltpu.SemaphoreType.DMA((7,))],
        f"late_attention_{image}",
        {at + k: k for k in range(len(old))},
    )
    return list(made[:2]) + [gqkv, grad], sums


def pick(table, at):
    value = table[0]
    for k in range(1, len(table)):
        value = jnp.where(at == k, table[k], value)
    return value


def weight_gradient(side, arrays, blocks, name):
    depth = arrays[0].shape[0]
    width = min(array.shape[1] for array in arrays)
    half = len(blocks) // 2

    def chosen(i, scalar_ref):
        bit = scalar_ref[0]
        return jnp.where(i < half, (1 - bit) * half + i, bit * half + i - half)

    def kernel(scalar_ref, *refs):
        send_ref, keep_ref = refs[-2:]
        step = pl.program_id(0)
        block = chosen(step, scalar_ref)
        for left, right in dict.fromkeys((left, right) for left, right, _ in blocks):
            here = functools.reduce(
                jnp.logical_or, [block == k for k, entry in enumerate(blocks) if entry[:2] == (left, right)]
            )

            @pl.when(here & (step < half))
            def _():
                send_ref[...] = product(refs[left][...], refs[right][...], TN).astype(bf16)

            @pl.when(here & (step >= half))
            def _():
                keep_ref[...] = product(refs[left][...], refs[right][...], TN).astype(bf16)

    def columns(at):
        table = [column if right == at else 0 for _, right, column in blocks]
        return pl.BlockSpec((depth, width), lambda i, s: (0, pick(table, chosen(i, s))))

    return call(
        kernel,
        2 * half,
        side,
        arrays,
        [columns(at) for at in range(len(arrays))],
        [jax.ShapeDtypeStruct((half * width, width), bf16)] * 2,
        [
            pl.BlockSpec((width, width), lambda i, s: (jnp.minimum(i, half - 1), 0)),
            pl.BlockSpec((width, width), lambda i, s: (jnp.maximum(i - half, 0), 0)),
        ],
        [],
        name,
        room=60,
    )


def down_gradient(side, count, m, cotangent, received):
    images, slots, width = cotangent.shape
    rows, hidden = m.shape[1:]
    blocks = hidden // width
    half = blocks // 2
    scalars = jnp.concatenate([side, count])

    def chosen(i, scalar_ref):
        bit = scalar_ref[0]
        return jnp.where(i < half, (1 - bit) * half + i, bit * half + i - half)

    def kernel(scalar_ref, m_ref, e_ref, *rest):
        arrived, (send_ref, keep_ref, gd_ref) = rest[:images], rest[images:]
        step = pl.program_id(0)
        early = first_section()

        @pl.when(step == 0)
        def _():
            for image in range(images):
                live = row_mask((slots, width), scalar_ref[1 + image])
                top = slice(image * rows, image * rows + slots)
                gd_ref[top, :] = jnp.where(live, jnp.where(early, arrived[image][...], e_ref[image]), jnp.zeros((), bf16))
                gd_ref[top.stop : (image + 1) * rows, :] = jnp.zeros((rows - slots, width), bf16)

        left = m_ref[...].reshape(images * rows, width)

        @pl.when(step < half)
        def _():
            send_ref[...] = product(left, gd_ref[...], TN).astype(bf16)

        @pl.when(step >= half)
        def _():
            keep_ref[...] = product(left, gd_ref[...], TN).astype(bf16)

    return call(
        kernel,
        blocks,
        scalars,
        (m, cotangent) + tuple(received),
        [
            pl.BlockSpec((images, rows, width), lambda i, s: (0, 0, chosen(i, s))),
            fixed_block(cotangent.shape),
        ]
        + [image_block((slots, width), 0)] * images,
        [jax.ShapeDtypeStruct((half * width, width), bf16)] * 2,
        [
            pl.BlockSpec((width, width), lambda i, s: (jnp.minimum(i, half - 1), 0)),
            pl.BlockSpec((width, width), lambda i, s: (jnp.maximum(i - half, 0), 0)),
        ],
        [pltpu.VMEM((images * rows, width), bf16)],
        "grad_down",
        room=60,
    )


def plain_call(kernel, ins, outs, name):
    return pl.pallas_call(
        kernel,
        out_shape=outs,
        in_specs=[pl.BlockSpec(memory_space=pltpu.VMEM)] * len(ins),
        out_specs=[pl.BlockSpec(memory_space=pltpu.VMEM)] * len(outs),
        compiler_params=pltpu.CompilerParams(vmem_limit_bytes=16 << 20),
        cost_estimate=pl.CostEstimate(flops=COST, bytes_accessed=COST, transcendentals=0),
        name=name,
    )(*(in_vmem(value) for value in ins))


def assembled(own, stride, pieces, places, shapes, before):
    shape = pieces[0].shape

    def kernel(*refs):
        sources, _, outs, (raw, wide, sem) = split(refs, 2, len(before), len(shapes), 3)
        core = lax.axis_index(REP) if own else 1 - lax.axis_index(REP)
        near = bit_of(DP, stride)
        loads = [pltpu.make_async_copy(source, raw.at[k], sem.at[k]) for k, source in enumerate(sources)]
        for load in loads:
            load.start()

        def stores(k, act):
            block = 2 * core + (near if k == 0 else 1 - near)
            for at, (which, row, column) in enumerate(places):
                rows, columns = pl.ds(row * shape[0], shape[0]), pl.ds(column * shape[1], shape[1])

                @pl.when(block == at)
                def _():
                    act(pltpu.make_async_copy(wide.at[k], outs[which].at[rows, columns], sem.at[2 + k]))

        for k in range(2):
            loads[k].wait()
            wide[k] = raw[k].astype(f32)
            stores(k, lambda copy: copy.start())
        for k in range(2):
            stores(k, lambda copy: copy.wait())

    return pl.pallas_call(
        kernel,
        out_shape=[jax.ShapeDtypeStruct(whole, f32) for whole in shapes],
        in_specs=[ANY] * (2 + len(before)),
        out_specs=[ANY] * len(shapes),
        scratch_shapes=[
            pltpu.VMEM((2,) + shape, bf16),
            pltpu.VMEM((2,) + shape, f32),
            pltpu.SemaphoreType.DMA((4,)),
        ],
        input_output_aliases={2 + k: k for k in range(len(before))},
        compiler_params=pltpu.CompilerParams(vmem_limit_bytes=16 << 20),
        cost_estimate=pl.CostEstimate(flops=LATE_COST, bytes_accessed=LATE_COST, transcendentals=0),
        name="assembled",
    )(*pieces, *before)


def in_vmem(value):
    return pltpu.with_memory_space_constraint(value, pltpu.VMEM)


def swapped(value, axis, stride):
    length = lax.axis_size(axis)
    return lax.ppermute(value, axis, [(i, i ^ stride) for i in range(length)])


def bit_of(axis, stride):
    return (lax.axis_index(axis) // stride) % 2


def halved(keep, coming, stride):
    height, width = keep.shape[0] // 2, keep.shape[1]
    if height % ROW_TILE:
        bit = bit_of(DP, stride)
        pair = (keep.astype(f32) + coming.astype(f32)).astype(bf16)
        send = lax.dynamic_slice_in_dim(pair, (1 - bit) * height, height, axis=0)
        return send, lax.dynamic_slice_in_dim(pair, bit * height, height, axis=0)

    def kernel(keep_ref, coming_ref, send_ref, stay_ref):
        bit = bit_of(DP, stride)
        for half, out_ref in ((1 - bit, send_ref), (bit, stay_ref)):
            rows = pl.ds(pl.multiple_of(half * height, ROW_TILE), height)
            out_ref[...] = (keep_ref[rows, :].astype(f32) + coming_ref[rows, :].astype(f32)).astype(bf16)

    shape = jax.ShapeDtypeStruct((height, width), bf16)
    return plain_call(kernel, (keep, coming), [shape] * 2, f"halved_{stride}")


def summed(keep, coming, total):
    if keep.shape[0] % ROW_TILE:
        return ((keep.astype(f32) + coming.astype(f32)) / total).astype(bf16)

    def kernel(keep_ref, coming_ref, out_ref):
        out_ref[...] = ((keep_ref[...].astype(f32) + coming_ref[...].astype(f32)) / total).astype(bf16)

    return plain_call(kernel, (keep, coming), [jax.ShapeDtypeStruct(keep.shape, bf16)], "summed")[0]


def joined(mine, other, stride):
    height, width = mine.shape
    if height % ROW_TILE:
        first = bit_of(DP, stride) == 0
        return jnp.concatenate([jnp.where(first, mine, other), jnp.where(first, other, mine)], axis=0)

    def kernel(mine_ref, other_ref, out_ref):
        bit = bit_of(DP, stride)
        for half, source in ((bit, mine_ref), (1 - bit, other_ref)):
            out_ref[pl.ds(pl.multiple_of(half * height, ROW_TILE), height), :] = source[...]

    shape = jax.ShapeDtypeStruct((2 * height, width), bf16)
    return plain_call(kernel, (mine, other), [shape], f"joined_{stride}")[0]


def strides_of(size):
    return [1 << at for at in range(size.bit_length() - 1)]


class Line:
    def __init__(self):
        self.last = None

    def gate(self, value):
        if self.last is None:
            return value
        return lax.optimization_barrier((value, self.last))[0]

    def passed(self, value):
        self.last = value


class Exchange:
    def __init__(self, line, send, keep, strides, total):
        self.line, self.keep, self.strides, self.total = line, keep, strides, total
        self.at, self.half = 0, None
        self.coming = swapped(send, REP, 1)

    def advance(self):
        coming = self.line.gate(self.coming)
        count = len(self.strides)
        if self.at < count:
            stride = self.strides[self.at]
            send, self.keep = halved(self.keep, coming, stride)
            self.coming = swapped(send, DP, stride)
            self.line.passed(send)
        elif self.at == count:
            self.value = summed(self.keep, coming, self.total)
            self.coming = swapped(self.value, DP, self.strides[-1])
            self.line.passed(self.value)
        elif self.at < 2 * count:
            self.value = joined(self.value, coming, self.strides[2 * count - self.at])
            self.coming = swapped(self.value, DP, self.strides[2 * count - 1 - self.at])
            self.line.passed(self.value)
        elif self.at == 2 * count:
            self.half = (self.value, coming)
            self.others = swapped(lax.optimization_barrier(self.half)[0], REP, 1)
            self.coming = swapped(coming, REP, 1)
        else:
            self.half = (self.others, coming)
        self.at += 1


def added(value, coming):
    def kernel(value_ref, coming_ref, out_ref):
        out_ref[...] = value_ref[...] + coming_ref[...]

    return pl.pallas_call(
        kernel,
        out_shape=jax.ShapeDtypeStruct(value.shape, value.dtype),
        cost_estimate=pl.CostEstimate(flops=LATE_COST, bytes_accessed=LATE_COST, transcendentals=0),
        name="added",
    )(value, coming)


class Total:
    def __init__(self, line, value, strides):
        self.line, self.value = line, value
        self.partners = [(REP, 1)] + [(DP, stride) for stride in strides]
        self.at = 0
        self.coming = swapped(value, *self.partners[0])

    def advance(self):
        self.value = added(self.value, self.line.gate(self.coming))
        self.at += 1
        if self.at < len(self.partners):
            self.coming = swapped(self.value, *self.partners[self.at])
        self.line.passed(self.value)


def shards(
    boundary,
    keep_index,
    keep_count,
    gain_one,
    shift_one,
    w_qkv,
    bias_query,
    bias_value,
    w_out,
    bias_out,
    gain_two,
    shift_two,
    w_up,
    bias_up,
    w_down,
    bias_down,
):
    images = keep_index.shape[0]
    width = boundary.shape[-1]
    weights = (w_qkv[0], w_out[0], w_up[0], w_down[0])
    hidden = weights[2].shape[1]
    vectors = (gain_one, shift_one, bias_query, bias_value, bias_out, gain_two, shift_two, bias_down, bias_up)
    rows_in = boundary[0]

    line = Line()
    assert images == 3
    section = lax.axis_index(SECTION).astype(jnp.int32)
    scalars = jnp.concatenate([keep_count, section[None]])
    carry, received = None, []
    for image in range(2):
        carry, first_output = first_forward(image, carry, keep_count, keep_index, rows_in, vectors, weights)
        received.append(lax.ppermute(first_output, SECTION, [(0, 1)]))
    saved, output = carry[:-1], carry[-1]
    made, sums, returned = None, None, []
    for image, first, late in ((0, 2, None), (1, None, None), (2, None, 0)):
        saved, made, output, sums, sent = tick(
            first, image, late, saved, made, output, sums, scalars, keep_index, in_vmem(line.gate(received[image])),
            rows_in, vectors, weights,
        )
        line.passed(sent)
        both = [(1, 0)] + ([(0, 1)] if first is not None else [])
        returned.append(lax.ppermute(sent, SECTION, both))
        if first is not None:
            received.append(returned[-1])

    def flat(name):
        array = saved[SAVED.index(name)] if name in SAVED else made[MADE.index(name)]
        return array.reshape(-1, array.shape[-1])

    total = images * lax.axis_size((DP, REP))
    side = lax.axis_index(REP).astype(jnp.int32)[None]
    near_first = strides_of(lax.axis_size(DP))
    far_first = near_first[1::-1] + near_first[2:]
    square, many = (width, width), hidden // width
    forwards, attentions = [1, 2], [1, 2]
    residual = [None] * images
    exchanges, outs = {}, {}

    def begin(name, pair, strides):
        line.passed(pair[0])
        exchanges[name] = Exchange(line, *pair, strides, total)

    def feed_forward():
        nonlocal made, output, sums
        image = forwards.pop(0)
        made, output, sums, residual[image] = late_feed_forward(
            image, (0, 1) if image == 1 else (2,), saved, made, output, sums, keep_count, in_vmem(line.gate(returned[image])),
            vectors, weights,
        )
        line.passed(residual[image])

    def attention():
        nonlocal made, sums
        image = attentions.pop(0)
        made, sums = late_attention(
            image, saved, made, sums, line.gate(residual[image]), keep_count, keep_index, vectors, weights
        )
        line.passed(sums)

    def grad_down():
        pair = down_gradient(side, keep_count, line.gate(saved[SAVED.index(M)]), rows_in, returned)
        begin(DOWN, pair, near_first)

    def grad_up():
        blocks = [(0, 1, column) for column in range(many)]
        begin(UP, weight_gradient(side, (line.gate(flat(C)), flat(GZ)), blocks, "grad_up"), far_first)

    def grad_query_value():
        exchanges[SUMS] = Total(line, sums, near_first)
        pair = weight_gradient(side, (line.gate(flat(A)), flat(GQKV)), [(0, 1, 0), (0, 1, 2)], "grad_query_value")
        begin(QUERY_VALUE, pair, near_first)

    def grad_key_out():
        arrays = (line.gate(flat(A)), flat(GQKV), flat(O), flat(GB))
        pair = weight_gradient(side, arrays, [(0, 1, 1), (2, 3, 0)], "grad_key_out")
        begin(KEY_OUT, pair, near_first)

    def widen(name):
        places, kinds = {
            DOWN: ([(0, k, 0) for k in range(many)], {DOWN: (hidden, width)}),
            UP: ([(0, 0, k) for k in range(many)], {UP: (width, hidden)}),
            QUERY_VALUE: ([(0, 0, 0), (0, 1, 0), (0, 0, 2), (0, 1, 2)], {QKV: (width, 3 * width)}),
            KEY_OUT: ([(0, 0, 1), (0, 1, 1), (1, 0, 0), (1, 1, 0)], {QKV: (width, 3 * width), OUT: (width, width)}),
        }[name]
        exchange = exchanges[name]
        before = [outs[kind] for kind in kinds if kind in outs]
        first, second = exchange.half
        wholes = assembled(
            exchange.at == stages - 1,
            exchange.strides[0],
            (first, line.gate(second)),
            places,
            list(kinds.values()),
            before,
        )
        line.passed(wholes[0])
        outs.update(zip(kinds, wholes))

    steps = dict(zip("FAGUQK", (feed_forward, attention, grad_down, grad_up, grad_query_value, grad_key_out)))
    transfers = dict(zip("duqks", (DOWN, UP, QUERY_VALUE, KEY_OUT, SUMS)))
    stages = 2 * len(near_first) + 2
    plain = "FAFAGUQK" + "duqk" * stages + "s" * (stages // 2)
    for step in ORDER if (images, stages) == (3, 8) else plain:
        if step in steps:
            steps[step]()
            continue
        name = transfers[step]
        exchanges[name].advance()
        if name != SUMS and exchanges[name].half is not None:
            widen(name)
    assert all(exchange.at == (stages // 2 if name == SUMS else stages) for name, exchange in exchanges.items())
    sums = exchanges[SUMS].value / total
    small = [sums[at : at + 1] for at in VECTORS[:-1]]
    return (
        output[None],
        made[MADE.index(GRAD)][None],
        small[GAIN_ONE],
        small[SHIFT_ONE],
        outs[QKV][None],
        small[BIAS_QUERY],
        small[BIAS_VALUE],
        outs[OUT][None],
        small[BIAS_OUT],
        small[GAIN_TWO],
        small[SHIFT_TWO],
        outs[UP][None],
        sums[BIAS_UP : BIAS_UP + many].reshape(1, -1),
        outs[DOWN][None],
        small[BIAS_DOWN],
    )


def solution(mesh):
    per_image = (DP, REP)
    matrix, line = P(SECTION, None, None), P(SECTION, None)
    rows = P(SECTION, per_image, None, None)
    kinds = (line, line, matrix, line, line, matrix, line, line, line, matrix, line, matrix, line)
    return jax.shard_map(
        shards,
        mesh=mesh,
        in_specs=(rows, P(per_image, None), P(per_image)) + kinds,
        out_specs=(rows, rows) + kinds,
        check_vma=False,
    )
```
